32 devices in a mesh: rep: 4 (over y, x), shard: 8 (over z, core).
Axes of the slice: x: 2, y: 2, z: 4, core: 2. Of those that a mesh axis runs over, the one named last changes fastest.
Arguments:
- tokens: bfloat16 [4096, 2048], P(('rep', 'shard')), may hold values from -6 to 6
- seq_lengths: int32 [4, 32], P('rep'), may hold values from 1 to 64, as said below
- deal_order: int32 [4, 32], P('rep'), may hold values from 0 to 31, as said below
- attn_gain: bfloat16 [2048], P('shard'), may hold values from 0.099609375 to 1.8984375
- mlp_gain: bfloat16 [2048], P('shard'), may hold values from 0.099609375 to 1.8984375
- q_weight: bfloat16 [2048, 2048], P('shard'), may hold values from -0.125 to 0.125
- k_weight: bfloat16 [2048, 256], P('shard'), may hold values from -0.125 to 0.125
- v_weight: bfloat16 [2048, 256], P('shard'), may hold values from -0.125 to 0.125
- o_weight: bfloat16 [2048, 2048], P('shard'), may hold values from -0.5 to 0.5
- gate_weight: bfloat16 [2048, 5632], P('shard'), may hold values from -0.125 to 0.125
- up_weight: bfloat16 [2048, 5632], P('shard'), may hold values from -0.125 to 0.125
- down_weight: bfloat16 [5632, 2048], P('shard'), may hold values from -0.078125 to 0.078125
- cotangent: bfloat16 [4096, 2048], P(('rep', 'shard')), may hold values from -6 to 6
Outputs:
- layer_out: bfloat16 [4096, 2048], P(('rep', 'shard'))
- input_grad: bfloat16 [4096, 2048], P(('rep', 'shard'))
- attn_gain_grad: float32 [2048], P('shard')
- mlp_gain_grad: float32 [2048], P('shard')
- q_weight_grad: float32 [2048, 2048], P('shard')
- k_weight_grad: float32 [2048, 256], P('shard')
- v_weight_grad: float32 [2048, 256], P('shard')
- o_weight_grad: float32 [2048, 2048], P('shard')
- gate_weight_grad: float32 [2048, 5632], P('shard')
- up_weight_grad: float32 [2048, 5632], P('shard')
- down_weight_grad: float32 [5632, 2048], P('shard')
The draws below stay inside these ranges and needn't reach their ends.
Inputs may be any that keep to these rules, and one draw needn't show every extreme that they name: seq_lengths[g] are the lengths of group g's sequences in initial order and add up to 1024; in every group one sequence has exactly 64 tokens. deal_order[g] is a permutation of the group's 32 sequences; dealt places s * 4 to s * 4 + 3 hold sequences whose lengths add up to exactly 128, so that index s of shard receives whole sequences.
All inputs are finite; a program needn't handle non-finite values.
Results may differ from the reference program's by a relative error of at most 0.014.
Values may be sent and summed in bfloat16 or wider, within the bound.
No kernel may reach another device: no remote copies, remote signals or barrier semaphores. Data moves between devices by JAX's collectives and lax.ppermute only.
A program may use at most 256 MiB of HBM per device.

```python
import jax
import jax.numpy as jnp
from jax import lax

D = 2048
H = 32
KVH = 4
HD = 64
FF = 5632
TOK_DEV = 128
SEQ_DEV = 4
LEN_MAX = 64
SEQS = 32
GROUP_TOK = 1024
TOKENS = 4096
N_REP = 4
N_SHARD = 8


def dealing(key):
    base_key = jax.random.fold_in(key, 7)
    cut_key, force_key, perm_key = jax.random.split(base_key, 3)
    shard_count = SEQS // SEQ_DEV
    group_count = TOKENS // GROUP_TOK
    device_count = group_count * shard_count
    forced_shard = jax.random.randint(force_key, (group_count,), 0, shard_count)
    device_ids = jnp.arange(device_count, dtype=jnp.int32)
    forced = device_ids % shard_count == jnp.repeat(forced_shard, shard_count)
    remain = jnp.full((device_count,), TOK_DEV, jnp.int32)
    columns = []
    for slot_index in range(SEQ_DEV):
        parts_after = SEQ_DEV - 1 - slot_index
        low_end = jnp.maximum(1, remain - parts_after * LEN_MAX)
        high_end = jnp.minimum(LEN_MAX, remain - parts_after)
        if slot_index == 0:
            low_end = jnp.where(forced, LEN_MAX, low_end)
            high_end = jnp.where(forced, LEN_MAX, high_end)
        drawn_len = jax.random.randint(jax.random.fold_in(cut_key, slot_index), (device_count,), low_end, high_end + 1)
        columns.append(drawn_len.astype(jnp.int32))
        remain = remain - drawn_len.astype(jnp.int32)
    dealt_len = jnp.stack(columns, axis=1).reshape(group_count, SEQS).astype(jnp.int32)
    group_keys = jax.random.split(perm_key, group_count)
    order_rows = jax.vmap(lambda one_key: jax.random.permutation(one_key, SEQS))(group_keys).astype(jnp.int32)
    inverse = jnp.argsort(order_rows, axis=1, stable=True)
    lengths = jnp.take_along_axis(dealt_len, inverse, axis=1)
    return (lengths.astype(jnp.int32), order_rows)


def draw_seq_lengths(key, part):
    return dealing(key)[0]


def draw_deal_order(key, part):
    return dealing(key)[1]


def block_levels(rng, dims, shards, low, largest):
    loudness, own = 1.0, jax.random.fold_in(rng, 6)
    for axis_at, shards_of in shards:
        steps = jnp.exp(jax.random.uniform(jax.random.fold_in(own, axis_at), (shards_of,), jnp.float32, low / len(shards), largest / len(shards)))
        loudness = loudness * jnp.repeat(steps, dims[axis_at] // shards_of).reshape([-1 if axis == axis_at else 1 for axis in range(len(dims))])
    return loudness


def bell_draw(key, extent, spread, most, cuts=(), kind=jnp.bfloat16):
    loudness = block_levels(key, extent, cuts, -0.22, 0.18) if cuts else 1.0
    drawn = jax.random.normal(key, extent, jnp.float32) * spread * loudness
    return jnp.minimum(jnp.maximum(drawn, -most), most).astype(kind)


def setup_inputs(seed: int = 0) -> dict:
    splits = jax.random.split(jax.random.key(seed), 14)
    return {
        "tokens": bell_draw(splits[0], (TOKENS, D), 1.0, 6.0, ((0, 32),)),
        "seq_lengths": draw_seq_lengths(jax.random.fold_in(splits[13], 71), 0),
        "deal_order": draw_deal_order(jax.random.fold_in(splits[13], 71), 0),
        "attn_gain": jnp.clip(1.0 + 0.18 * jax.random.normal(splits[3], (D,), jnp.float32), 0.099609375, 1.8984375).astype(jnp.bfloat16),
        "mlp_gain": jnp.clip(1.0 + 0.18 * jax.random.normal(splits[4], (D,), jnp.float32), 0.099609375, 1.8984375).astype(jnp.bfloat16),
        "q_weight": bell_draw(splits[5], (D, D), D ** -0.5, 0.125, ((0, 8),)),
        "k_weight": bell_draw(splits[6], (D, KVH * HD), D ** -0.5, 0.125, ((0, 8),)),
        "v_weight": bell_draw(splits[7], (D, KVH * HD), D ** -0.5, 0.125, ((0, 8),)),
        "o_weight": bell_draw(splits[8], (D, D), (D // 16) ** -0.5, 0.5, ((0, 8),)),
        "gate_weight": bell_draw(splits[9], (D, FF), D ** -0.5, 0.125, ((0, 8),)),
        "up_weight": bell_draw(splits[10], (D, FF), D ** -0.5, 0.125, ((0, 8),)),
        "down_weight": bell_draw(splits[11], (FF, D), FF ** -0.5, 0.078125, ((0, 8),)),
        "cotangent": bell_draw(splits[12], (TOKENS, D), 1.0, 6.0, ((0, 32),)),
    }


EPSILON = 1e-05
ROPE_BASE = 10000.0
NEG_FILL = -1e+30

@jax.custom_vjp
def low(v):
    return lax.optimization_barrier(v.astype(jnp.bfloat16)).astype(jnp.float32)

@jax.custom_vjp
def low_back(v):
    return v

def low_keep(v):
    return (low(v), None)

def low_pass(kept, grad):
    return (grad,)

def back_keep(v):
    return (v, None)

def back_low(kept, grad):
    return (low(grad),)
low.defvjp(low_keep, low_pass)
low_back.defvjp(back_keep, back_low)

def matmul(left, right):
    return jnp.dot(left, right, precision=lax.Precision.HIGHEST, preferred_element_type=jnp.float32)

def rope_tables(positions, head_dim):
    half_dim = head_dim // 2
    steps_index = jnp.arange(half_dim, dtype=jnp.float32)
    inverse = ROPE_BASE ** (-2.0 * steps_index / head_dim)
    angles = positions.astype(jnp.float32)[:, None] * inverse[None, :]
    angles = jnp.concatenate([angles, angles], axis=1)
    return (jnp.cos(angles), jnp.sin(angles))

def rotate(values, cosine, sine_table):
    head_dim = cosine.shape[1]
    half_dim = head_dim // 2
    shaped = values.reshape(values.shape[0], -1, head_dim)
    turned = jnp.concatenate([-shaped[..., half_dim:], shaped[..., :half_dim]], axis=-1)
    return (shaped * cosine[:, None, :] + turned * sine_table[:, None, :]).reshape(values.shape)

def row_maps(seq_len, order_row, shard_id, row_count):
    seq_count = order_row.shape[0]
    seq_ids = jnp.arange(seq_count, dtype=jnp.int32)
    pick_table = (order_row[:, None] == seq_ids[None, :]).astype(jnp.int32)
    dealt_len = lax.optimization_barrier(jnp.sum(pick_table * seq_len[None, :], axis=1))
    orig_start = jnp.cumsum(seq_len) - seq_len
    dealt_start = jnp.cumsum(dealt_len) - dealt_len
    dealt_orig_start = lax.optimization_barrier(jnp.sum(pick_table * orig_start[None, :], axis=1))
    dealt_start_orig = lax.optimization_barrier(jnp.sum(pick_table * dealt_start[:, None], axis=0))
    places = shard_id * row_count + jnp.arange(row_count, dtype=jnp.int32)
    segment = lax.optimization_barrier(jnp.sum((dealt_start[None, :] <= places[:, None]).astype(jnp.int32), axis=1)) - 1
    seq_hit = (segment[:, None] == seq_ids[None, :]).astype(jnp.int32)
    offset = places - lax.optimization_barrier(jnp.sum(seq_hit * dealt_start[None, :], axis=1))
    source = lax.optimization_barrier(jnp.sum(seq_hit * dealt_orig_start[None, :], axis=1)) + offset
    orig_seg = lax.optimization_barrier(jnp.sum((orig_start[None, :] <= places[:, None]).astype(jnp.int32), axis=1)) - 1
    orig_hit = (orig_seg[:, None] == seq_ids[None, :]).astype(jnp.int32)
    back_place = places - lax.optimization_barrier(jnp.sum(orig_hit * orig_start[None, :], axis=1)) + lax.optimization_barrier(jnp.sum(orig_hit * dealt_start_orig[None, :], axis=1))
    return (segment, offset, source, back_place)

def layer_forward(params, x_in, segment, offset):
    gain_one, gain_two, w_query, w_key, w_value, w_out, w_gate, w_up, w_down = params
    row_count = x_in.shape[0]
    cosine, sine_table = rope_tables(offset, HD)
    row_ids = jnp.arange(row_count)
    allowed = (segment[:, None] == segment[None, :]) & (row_ids[None, :] <= row_ids[:, None])
    scale_one = lax.rsqrt(lax.optimization_barrier(jnp.mean(x_in * x_in, axis=1, keepdims=True)) + EPSILON)
    normed_one = low(x_in * scale_one * gain_one[None, :])
    query_rot = low(rotate(low_back(matmul(normed_one, w_query)), cosine, sine_table))
    key_rot = low(rotate(low_back(matmul(normed_one, w_key)), cosine, sine_table))
    value_low = low(low_back(matmul(normed_one, w_value)))
    q_heads = query_rot.reshape(row_count, KVH, H // KVH, HD)
    k_heads = key_rot.reshape(row_count, KVH, HD)
    v_heads = value_low.reshape(row_count, KVH, HD)
    scores = low_back(jnp.einsum('tkgd,skd->kgts', q_heads, k_heads, precision=lax.Precision.HIGHEST) * HD ** (-0.5))
    masked = jnp.where(allowed[None, None], scores, NEG_FILL)
    row_peak = lax.optimization_barrier(jnp.max(masked, axis=-1, keepdims=True))
    exp_scores = jnp.exp(masked - row_peak)
    soft_probs = low(exp_scores / lax.optimization_barrier(jnp.sum(exp_scores, axis=-1, keepdims=True)))
    attended = jnp.einsum('kgts,skd->tkgd', soft_probs, v_heads, precision=lax.Precision.HIGHEST).reshape(row_count, H * HD)
    attn_low = low(low_back(attended))
    x_mid = x_in + low_back(matmul(attn_low, w_out))
    scale_two = lax.rsqrt(lax.optimization_barrier(jnp.mean(x_mid * x_mid, axis=1, keepdims=True)) + EPSILON)
    normed_two = low(x_mid * scale_two * gain_two[None, :])
    gate_pre = low_back(matmul(normed_two, w_gate))
    up_pre = low_back(matmul(normed_two, w_up))
    mixed_low = low(jax.nn.silu(gate_pre) * up_pre)
    return x_mid + low_back(matmul(mixed_low, w_down))

def reference(tokens, seq_lengths, deal_order, attn_gain, mlp_gain, q_weight, k_weight, v_weight, o_weight, gate_weight, up_weight, down_weight, cotangent):
    group_rows = TOK_DEV * N_SHARD
    blocks = N_REP * N_SHARD
    mapper = jax.vmap(lambda seq_len, order_row: row_maps(seq_len, order_row, 0, group_rows))
    segment, offset, source, back_place = mapper(seq_lengths, deal_order)
    group_base = (jnp.arange(N_REP, dtype=jnp.int32) * group_rows)[:, None]
    source_all = (source + group_base).reshape(-1).astype(jnp.int32)
    back_all = (back_place + group_base).reshape(-1).astype(jnp.int32)
    x_dealt = jnp.take(tokens, source_all, axis=0).astype(jnp.float32).reshape(blocks, TOK_DEV, D)
    cot_dealt = jnp.take(cotangent, source_all, axis=0).astype(jnp.float32).reshape(blocks, TOK_DEV, D)
    seg_blocks = segment.reshape(blocks, TOK_DEV)
    off_blocks = offset.reshape(blocks, TOK_DEV)
    params = tuple((weight.astype(jnp.float32) for weight in (attn_gain, mlp_gain, q_weight, k_weight, v_weight, o_weight, gate_weight, up_weight, down_weight)))

    def one_block(totals, operands):
        x_block, cot_block, seg_block, off_block = operands
        result, pullback = jax.vjp(lambda weights, x_value: layer_forward(weights, x_value, seg_block, off_block), params, x_block)
        weight_grads, grad_rows = pullback(cot_block)
        totals = tuple((left + right for left, right in zip(totals, weight_grads)))
        return (totals, (result.astype(jnp.bfloat16), grad_rows.astype(jnp.bfloat16)))
    zero_grads = tuple((jnp.zeros_like(weight) for weight in params))
    totals, (outputs, grad_blocks) = lax.scan(one_block, zero_grads, (x_dealt, cot_dealt, seg_blocks, off_blocks))
    layer_out = jnp.take(outputs.reshape(-1, D), back_all, axis=0)
    input_grad = jnp.take(grad_blocks.reshape(-1, D), back_all, axis=0)
    return (layer_out, input_grad, totals[0], totals[1], totals[2], totals[3], totals[4], totals[5], totals[6], totals[7], totals[8])
```

```python
from functools import partial

import jax
import jax.numpy as jnp
from jax import lax
from jax.sharding import PartitionSpec as P

H = 32
KVH = 4
HD = 64
HALO = 64

EPSILON = 1e-05
ROPE_BASE = 10000.0
NEG_FILL = -1e30

BF = jnp.bfloat16
F32 = jnp.float32


def dot(left, right, contract):
    return lax.dot_general(left, right, (contract, ((), ())), preferred_element_type=F32)


def rows_cols(left, right):
    return dot(left, right, ((1,), (0,)))


def rows_rows(left, right):
    return dot(left, right, ((0,), (0,)))


def cols_cols(left, right):
    return dot(left, right, ((1,), (1,)))


def spread(value, axis, count):
    wide = jnp.broadcast_to(value[None], (count,) + value.shape)
    return lax.all_to_all(wide, axis, split_axis=0, concat_axis=0, tiled=True)


def swap(value, axis):
    return lax.all_to_all(value, axis, split_axis=0, concat_axis=0, tiled=True)


def rope_tables(positions):
    half = HD // 2
    inverse = ROPE_BASE ** (-2.0 * jnp.arange(half, dtype=F32) / HD)
    angles = positions.astype(F32)[:, None] * inverse[None, :]
    angles = jnp.concatenate([angles, angles], axis=1)
    return jnp.cos(angles), jnp.sin(angles)


def rotate(values, cosine, sine):
    half = HD // 2
    shaped = values.reshape(values.shape[0], -1, HD)
    turned = jnp.concatenate([-shaped[..., half:], shaped[..., :half]], axis=-1)
    return (shaped * cosine[:, None, :] + turned * sine[:, None, :]).reshape(values.shape)


def body(
    n_rep,
    n_shard,
    tokens,
    seq_lengths,
    deal_order,
    attn_gain,
    mlp_gain,
    q_weight,
    k_weight,
    v_weight,
    o_weight,
    gate_weight,
    up_weight,
    down_weight,
    cotangent,
):
    rows, width = tokens.shape
    r = lax.axis_index("rep")
    s = lax.axis_index("shard")
    own = width // n_shard
    fine = own // n_rep
    hidden = down_weight.shape[0]
    q_cols = width // n_rep
    heads = H // n_rep
    pair = n_shard // n_rep
    share = max(n_rep // KVH, 1)
    kv_at = (r * KVH) // n_rep
    all_rows = n_rep * rows

    w_qkv_own = jnp.concatenate(
        [
            lax.dynamic_slice_in_dim(q_weight, r * q_cols, q_cols, 1),
            lax.dynamic_slice_in_dim(k_weight, kv_at * HD, HD, 1),
            lax.dynamic_slice_in_dim(v_weight, kv_at * HD, HD, 1),
        ],
        axis=1,
    )
    w_qkv = lax.all_gather(w_qkv_own, "shard", axis=0, tiled=True)
    w_o = lax.all_gather(
        lax.dynamic_slice_in_dim(o_weight, r * fine, fine, 0), "shard", axis=0, tiled=True
    )
    x_all = spread(tokens, "rep", n_rep).reshape(all_rows, width)
    lengths = spread(seq_lengths[0], "rep", n_rep)
    gains = lax.all_gather(jnp.stack([attn_gain, mlp_gain]), "shard", axis=1, tiled=True)
    gain_one = gains[0].astype(F32)
    gain_two = gains[1].astype(F32)

    def quarter(weight):
        part = lax.dynamic_slice_in_dim(weight, r * fine, fine, 0)
        return part.reshape(fine, n_shard, hidden).transpose(1, 0, 2)

    w_pair = jnp.concatenate([quarter(gate_weight), quarter(up_weight)], axis=2)
    w_pair = spread(swap(w_pair, "shard"), "rep", n_rep).reshape(width, 2 * hidden)
    w_gate = w_pair[:, :hidden]
    w_up = w_pair[:, hidden:]
    cot_all = lax.all_gather(cotangent, "shard", axis=0, tiled=True)
    mixed_grad = cols_cols(cot_all, down_weight)

    places = s * rows - HALO + jnp.arange(HALO + rows, dtype=jnp.int32)
    starts = jnp.cumsum(lengths, axis=1) - lengths
    begun = starts[:, None, :] <= places[None, :, None]
    segment = jnp.sum(begun.astype(jnp.int32), axis=2) - 1
    first = jnp.max(jnp.where(begun, starts[:, None, :], 0), axis=2)
    offset = (places[None, :] - first)[:, HALO:].reshape(all_rows)
    cosine, sine = rope_tables(offset)
    place_q = places[HALO:]
    allowed = (segment[:, HALO:, None] == segment[:, None, :]) & (
        places[None, None, :] <= place_q[None, :, None]
    )

    x_wide = x_all.astype(F32)
    inv_one = lax.rsqrt(jnp.mean(x_wide * x_wide, axis=1, keepdims=True) + EPSILON)
    normed_one = (x_wide * inv_one * gain_one[None, :]).astype(BF)
    qkv = rows_cols(normed_one, w_qkv)
    q_low = rotate(qkv[:, :q_cols], cosine, sine).astype(BF)
    k_low = rotate(qkv[:, q_cols : q_cols + HD], cosine, sine).astype(BF)
    v_low = qkv[:, q_cols + HD :].astype(BF)
    kv_own = jnp.concatenate([k_low, v_low], axis=1).reshape(n_rep, rows, 2 * HD)
    kv_halo = lax.ppermute(
        kv_own[:, rows - HALO :], "shard", [(i, i + 1) for i in range(n_shard - 1)]
    )
    kv = jnp.concatenate([kv_halo, kv_own], axis=1)
    keys, values = kv[..., :HD], kv[..., HD:]
    queries = q_low.reshape(n_rep, rows, heads, HD)
    scale = HD ** (-0.5)
    scores = (
        jnp.einsum("btgd,bsd->bgts", queries, keys, preferred_element_type=F32) * scale
    )
    masked = jnp.where(allowed[:, None], scores, NEG_FILL)
    peak = jnp.max(masked, axis=-1, keepdims=True)
    grown = jnp.exp(masked - peak)
    probs = grown / jnp.sum(grown, axis=-1, keepdims=True)
    probs_low = probs.astype(BF)
    attended = jnp.einsum(
        "bgts,bsd->btgd", probs_low, values, preferred_element_type=F32
    ).astype(BF)
    out_in = attended.reshape(all_rows, pair, n_rep, fine).transpose(2, 0, 1, 3)
    out_in = swap(out_in.reshape(n_rep, all_rows, pair * fine), "rep")
    out_in = out_in.transpose(1, 0, 2).reshape(all_rows, q_cols)
    mid_part = rows_cols(out_in, w_o).astype(BF).reshape(n_rep, rows, width)
    x_own = tokens.astype(F32)
    x_mid = x_own + jnp.sum(swap(mid_part, "rep").astype(F32), axis=0)

    def shuffle(value):
        return value.reshape(-1, n_shard, n_rep, fine).transpose(0, 2, 1, 3).reshape(-1, width)

    def unshuffle(value):
        return value.reshape(-1, n_rep, n_shard, fine).transpose(0, 2, 1, 3).reshape(-1, width)

    inv_two = lax.rsqrt(jnp.mean(x_mid * x_mid, axis=1, keepdims=True) + EPSILON)
    normed_two = (x_mid * inv_two * gain_two[None, :]).astype(BF)
    two_all = lax.all_gather(shuffle(normed_two), "shard", axis=0, tiled=True)
    gate_pre = rows_cols(two_all, w_gate)
    up_pre = rows_cols(two_all, w_up)
    sigma = jax.nn.sigmoid(gate_pre)
    silu = gate_pre * sigma
    mixed = (silu * up_pre).astype(BF)
    gate_grad = (mixed_grad * up_pre * sigma * (1.0 + gate_pre * (1.0 - sigma))).astype(BF)
    up_grad = (mixed_grad * silu).astype(BF)
    two_grad_part = (cols_cols(gate_grad, w_gate) + cols_cols(up_grad, w_up)).astype(BF)
    two_grad = unshuffle(
        lax.psum_scatter(two_grad_part, "shard", scatter_dimension=0, tiled=True)
    ).astype(F32)
    down_part = rows_cols(mixed, down_weight).astype(BF)
    down_rows = lax.psum_scatter(down_part, "shard", scatter_dimension=0, tiled=True)
    layer_out = (x_mid + down_rows.astype(F32)).astype(BF)

    gain_two_part = jnp.sum(two_grad * x_mid * inv_two, axis=0)
    scaled_two = two_grad * gain_two[None, :]
    mid_grad = (
        cotangent.astype(F32)
        + inv_two * scaled_two
        - x_mid * inv_two**3 * jnp.mean(scaled_two * x_mid, axis=1, keepdims=True)
    )

    def over_rep(pieces):
        return jnp.sum(swap(pieces, "rep").astype(F32), axis=0).astype(BF)

    w_down_grad = rows_rows(mixed, cot_all).astype(BF)
    w_down_grad = over_rep(w_down_grad.reshape(n_rep, hidden // n_rep, width))
    down_out = spread(w_down_grad, "rep", n_rep).reshape(hidden, width).astype(F32)
    w_pair_grad = rows_rows(two_all, jnp.concatenate([gate_grad, up_grad], axis=1)).astype(BF)
    w_pair_grad = over_rep(w_pair_grad.reshape(n_rep, n_shard * fine, 2 * hidden))
    w_pair_grad = swap(w_pair_grad.reshape(n_shard, fine, 2 * hidden), "shard")
    w_pair_grad = spread(w_pair_grad, "rep", n_rep)

    def assemble(part):
        return part.transpose(0, 2, 1, 3).reshape(own, n_shard * hidden).astype(F32)

    gate_out = assemble(w_pair_grad[..., :hidden])
    up_out = assemble(w_pair_grad[..., hidden:])

    branch_all = spread(mid_grad.astype(BF), "rep", n_rep).reshape(all_rows, width)
    w_o_grad = rows_rows(out_in, branch_all).astype(BF)
    w_o_grad = lax.psum_scatter(w_o_grad, "shard", scatter_dimension=0, tiled=True)
    o_out = spread(w_o_grad, "rep", n_rep).reshape(own, width).astype(F32)
    in_grad = cols_cols(branch_all, w_o).astype(BF)
    in_grad = in_grad.reshape(all_rows, n_rep, pair * fine).transpose(1, 0, 2)
    in_grad = swap(in_grad, "rep").reshape(n_rep, all_rows, pair, fine)
    head_grad = in_grad.transpose(1, 2, 0, 3).reshape(n_rep, rows, heads, HD)
    probs_grad = jnp.einsum("btgd,bsd->bgts", head_grad, values, preferred_element_type=F32)
    value_grad = jnp.einsum("bgts,btgd->bsd", probs_low, head_grad, preferred_element_type=F32)
    inner = jnp.sum(probs * probs_grad, axis=-1, keepdims=True)
    score_grad = (probs * (probs_grad - inner)).astype(BF)
    query_grad = jnp.einsum("bgts,bsd->btgd", score_grad, keys, preferred_element_type=F32)
    key_grad = jnp.einsum("bgts,btgd->bsd", score_grad, queries, preferred_element_type=F32)
    kv_grad = jnp.concatenate([key_grad * scale, value_grad], axis=2)
    kv_back = lax.ppermute(
        kv_grad[:, :HALO], "shard", [(i + 1, i) for i in range(n_shard - 1)]
    )
    kv_grad = kv_grad[:, HALO:]
    kv_grad = jnp.concatenate([kv_grad[:, : rows - HALO], kv_grad[:, rows - HALO :] + kv_back], 1)
    kv_grad = kv_grad.reshape(all_rows, 2 * HD)
    qkv_grad = jnp.concatenate(
        [
            rotate((query_grad * scale).reshape(all_rows, q_cols), cosine, -sine),
            rotate(kv_grad[:, :HD], cosine, -sine),
            kv_grad[:, HD:],
        ],
        axis=1,
    ).astype(BF)
    w_qkv_grad = rows_rows(normed_one, qkv_grad).astype(BF)
    one_grad_part = cols_cols(qkv_grad, w_qkv).astype(BF).reshape(n_rep, rows, width)
    one_grad = jnp.sum(swap(one_grad_part, "rep").astype(F32), axis=0)
    inv_own = lax.rsqrt(jnp.mean(x_own * x_own, axis=1, keepdims=True) + EPSILON)
    gain_one_part = jnp.sum(one_grad * x_own * inv_own, axis=0)
    scaled_one = one_grad * gain_one[None, :]
    input_grad = (
        mid_grad
        + inv_own * scaled_one
        - x_own * inv_own**3 * jnp.mean(scaled_one * x_own, axis=1, keepdims=True)
    ).astype(BF)
    w_qkv_grad = lax.psum_scatter(w_qkv_grad, "shard", scatter_dimension=0, tiled=True)
    w_qkv_grad = spread(w_qkv_grad, "rep", n_rep).astype(F32)

    def columns(part):
        return part.transpose(1, 0, 2).reshape(own, -1)

    def kv_columns(part):
        return columns(jnp.sum(part.reshape(-1, share, own, HD), axis=1))

    q_out = columns(w_qkv_grad[..., :q_cols])
    k_out = kv_columns(w_qkv_grad[..., q_cols : q_cols + HD])
    v_out = kv_columns(w_qkv_grad[..., q_cols + HD :])

    gain_sums = lax.psum(jnp.stack([gain_one_part, gain_two_part]), ("rep", "shard"))
    gain_sums = lax.dynamic_slice_in_dim(gain_sums, s * own, own, 1)
    return (
        layer_out,
        input_grad,
        gain_sums[0],
        gain_sums[1],
        q_out,
        k_out,
        v_out,
        o_out,
        gate_out,
        up_out,
        down_out,
    )


def solution(mesh):
    split = P("shard", None)
    by_token = P(("rep", "shard"), None)
    return jax.shard_map(
        partial(body, mesh.shape["rep"], mesh.shape["shard"]),
        mesh=mesh,
        in_specs=(by_token, P("rep", None), P("rep", None), P("shard"), P("shard"))
        + (split,) * 7
        + (by_token,),
        out_specs=(by_token, by_token, P("shard"), P("shard")) + (split,) * 7,
        check_vma=False,
    )
```

```python
from functools import partial

import jax
import jax.numpy as jnp
from jax import lax
from jax.experimental import pallas as pl
from jax.experimental.pallas import tpu as pltpu
from jax.sharding import PartitionSpec as P

H = 32
KVH = 4
HD = 64
HALO = 64
LANES = 128

EPSILON = 1e-05
ROPE_BASE = 10000.0
NEG_FILL = -1e30

BF = jnp.bfloat16
F32 = jnp.float32


def dot(left, right, contract):
    return lax.dot_general(left, right, (contract, ((), ())), preferred_element_type=F32)


def rows_cols(left, right):
    return dot(left, right, ((1,), (0,)))


def rows_rows(left, right):
    return dot(left, right, ((0,), (0,)))


def cols_cols(left, right):
    return dot(left, right, ((1,), (1,)))


def spread(value, axis, count):
    wide = jnp.broadcast_to(value[None], (count,) + value.shape)
    return lax.all_to_all(wide, axis, split_axis=0, concat_axis=0, tiled=True)


def swap(value, axis):
    return lax.all_to_all(value, axis, split_axis=0, concat_axis=0, tiled=True)


def pairs(count, step):
    return [(i, i ^ step) for i in range(count)]


def spread_far(value, axis, count):
    return [value] + [lax.ppermute(value, axis, pairs(count, k)) for k in range(1, count)]


def place(pieces, me, kind):
    size = pieces[0].shape[0]
    total = jnp.zeros((size * len(pieces),) + pieces[0].shape[1:], kind)
    for k, piece in enumerate(pieces):
        total = lax.dynamic_update_slice_in_dim(total, piece.astype(kind), (me ^ k) * size, 0)
    return total


def swap_far(value, axis, count, me):
    chunk = [lax.dynamic_index_in_dim(value, me ^ k, 0, False) for k in range(count)]
    return [chunk[0]] + [lax.ppermute(chunk[k], axis, pairs(count, k)) for k in range(1, count)]


def norm_scale(value):
    return lax.rsqrt(jnp.mean(value * value, axis=1, keepdims=True) + EPSILON)


def turn(tile, cosine, sine):
    lane = lax.broadcasted_iota(jnp.int32, tile.shape, 1)
    swapped = jnp.where(
        lane % HD < HD // 2,
        -pltpu.roll(tile, LANES - HD // 2, 1),
        pltpu.roll(tile, HD // 2, 1),
    )
    return tile * cosine + swapped * sine


def turn_first(tile, cosine, sine):
    lane = lax.broadcasted_iota(jnp.int32, tile.shape, 1)
    return jnp.where(lane < HD, turn(tile, cosine, sine), tile)


def in_kernel(x_ref, gain_ref, w_ref, cos_ref, sin_ref, normed_ref, q_ref, kv_ref):
    x = x_ref[0].astype(F32)
    normed = (x * norm_scale(x) * gain_ref[...]).astype(BF)
    normed_ref[0] = normed
    qkv = rows_cols(normed, w_ref[...])
    cosine, sine = cos_ref[0], sin_ref[0]
    q_cols = q_ref.shape[2]
    for at in range(0, q_cols, LANES):
        q_ref[0, :, at : at + LANES] = turn(qkv[:, at : at + LANES], cosine, sine).astype(BF)
    kv_ref[0] = turn_first(qkv[:, q_cols:], cosine, sine).astype(BF)


def stack_heads(value):
    return jnp.concatenate(
        [value[:, at : at + HD] for at in range(0, value.shape[1], HD)], axis=0
    )


def unstack_heads(value, rows):
    return jnp.concatenate(
        [value[at : at + rows] for at in range(0, value.shape[0], rows)], axis=1
    )


def attend_kernel(fine, q_ref, own_ref, halo_ref, pos_ref, probs_ref, out_ref):
    rows, q_cols = q_ref.shape[1:]
    heads = q_cols // HD
    count = out_ref.shape[0]
    kv = jnp.concatenate([halo_ref[0], own_ref[0]], axis=0)
    keys, values = kv[:, :HD], kv[:, HD:]
    span = kv.shape[0]
    scores = cols_cols(stack_heads(q_ref[0]), keys) * (HD**-0.5)
    query = lax.broadcasted_iota(jnp.int32, (rows, span), 0) + HALO
    key = lax.broadcasted_iota(jnp.int32, (rows, span), 1)
    first = query - pos_ref[0][:, :1].astype(jnp.int32)
    allowed = (key >= first) & (key <= query)
    scores = jnp.where(allowed[None], scores.reshape(heads, rows, span), NEG_FILL)
    grown = jnp.exp(scores - jnp.max(scores, axis=-1, keepdims=True))
    probs = grown / jnp.sum(grown, axis=-1, keepdims=True)
    probs_ref[0] = probs
    mixed = rows_cols(probs.reshape(heads * rows, span).astype(BF), values)
    mixed = unstack_heads(mixed, rows).astype(BF)
    for to in range(count):
        out_ref[to, 0] = jnp.concatenate(
            [
                mixed[:, at + to * fine : at + (to + 1) * fine]
                for at in range(0, q_cols, count * fine)
            ],
            axis=1,
        )


def attend_back_kernel(
    fine, grad_ref, probs_ref, q_ref, own_ref, halo_ref, cos_ref, sin_ref, q_out, kv_out
):
    rows, q_cols = q_ref.shape[1:]
    heads = q_cols // HD
    count = grad_ref.shape[0]
    kv = jnp.concatenate([halo_ref[0], own_ref[0]], axis=0)
    keys, values = kv[:, :HD], kv[:, HD:]
    span = kv.shape[0]
    grad = jnp.concatenate(
        [
            grad_ref[source, 0][:, at * fine : (at + 1) * fine]
            for at in range(q_cols // (count * fine))
            for source in range(count)
        ],
        axis=1,
    )
    grad = stack_heads(grad)
    probs = probs_ref[0].reshape(heads * rows, span)
    probs_grad = cols_cols(grad, values)
    inner = jnp.sum(probs * probs_grad, axis=-1, keepdims=True)
    score_grad = (probs * (probs_grad - inner)).astype(BF)
    scale = HD**-0.5
    key_grad = rows_rows(score_grad, stack_heads(q_ref[0])) * scale
    value_grad = rows_rows(probs.astype(BF), grad)
    kv_out[0] = jnp.concatenate([key_grad, value_grad], axis=1)
    query_grad = unstack_heads(rows_cols(score_grad, keys) * scale, rows)
    cosine, sine = cos_ref[0], -sin_ref[0]
    for at in range(0, q_cols, LANES):
        q_out[0, :, at : at + LANES] = turn(
            query_grad[:, at : at + LANES], cosine, sine
        ).astype(BF)


def in_back_kernel(
    dq_ref, dkv_ref, back_ref, cos_ref, sin_ref, normed_ref, x_ref, two_ref, w_ref,
    part_ref, grad_ref, total_ref,
):
    at = pl.program_id(0)
    rows = dq_ref.shape[1]
    own = dkv_ref[0, HALO:]
    tail = own[rows - HALO :] + back_ref[0]
    own = jnp.concatenate([own[: rows - HALO], tail], axis=0)
    own = turn_first(own, cos_ref[0], -sin_ref[0]).astype(BF)
    qkv_grad = jnp.concatenate([dq_ref[0], own], axis=1)
    normed_grad = cols_cols(qkv_grad, w_ref[...])
    part_ref[0] = normed_grad.astype(BF)
    x = x_ref[0].astype(F32)
    one = (normed_grad * x * norm_scale(x)).astype(BF)
    cols = qkv_grad.shape[1]
    lane = lax.broadcasted_iota(jnp.int32, (rows, LANES), 1)

    @pl.when(at == 0)
    def _():
        total_ref[:, :cols] = rows_rows(normed_ref[0], qkv_grad)
        total_ref[:, cols:] = rows_rows(one, (lane < HD).astype(BF)) + rows_rows(
            two_ref[...], (lane >= HD).astype(BF)
        )

    @pl.when(at > 0)
    def _():
        total_ref[:, :cols] += rows_rows(normed_ref[0], qkv_grad)
        total_ref[:, cols:] += rows_rows(one, (lane < HD).astype(BF))

    @pl.when(at == pl.num_programs(0) - 1)
    def _():
        grad_ref[...] = total_ref[...].astype(BF)


def middle_kernel(part_ref, x_ref, gain_ref, mid_ref, normed_ref):
    mid = x_ref[...].astype(F32)
    for at in range(part_ref.shape[0]):
        mid += part_ref[at].astype(F32)
    mid_ref[...] = mid
    normed_ref[...] = (mid * norm_scale(mid) * gain_ref[...]).astype(BF)


def middle_back_kernel(grad_ref, mid_ref, gain_ref, cot_ref, out_ref, low_ref, gain_out_ref):
    mid = mid_ref[...]
    scale = norm_scale(mid)
    grad = grad_ref[...].astype(F32)
    gain_out_ref[...] = (grad * mid * scale).astype(BF)
    scaled = grad * gain_ref[...]
    out = (
        cot_ref[...].astype(F32)
        + scale * scaled
        - mid * scale**3 * jnp.mean(scaled * mid, axis=1, keepdims=True)
    )
    out_ref[...] = out
    low_ref[...] = out.astype(BF)


def last_kernel(part_ref, x_ref, gain_ref, mid_ref, out_ref):
    x = x_ref[...].astype(F32)
    scale = norm_scale(x)
    grad = part_ref[0].astype(F32)
    for at in range(1, part_ref.shape[0]):
        grad += part_ref[at].astype(F32)
    scaled = grad * gain_ref[...]
    out = (
        mid_ref[...]
        + scale * scaled
        - x * scale**3 * jnp.mean(scaled * x, axis=1, keepdims=True)
    )
    out_ref[...] = out.astype(BF)


def forward_back_kernel(
    x_ref, cot_ref, pair_ref, down_ref, mixed_ref, gate_out, up_out, part_ref
):
    x = x_ref[...]
    gate = rows_cols(x, pair_ref[0])
    up = rows_cols(x, pair_ref[1])
    mixed_grad = cols_cols(cot_ref[...], down_ref[...])
    sigma = jax.nn.sigmoid(gate)
    silu = gate * sigma
    mixed_ref[...] = (silu * up).astype(BF)
    gate_grad = (mixed_grad * up * sigma * (1.0 + gate * (1.0 - sigma))).astype(BF)
    up_grad = (mixed_grad * silu).astype(BF)
    gate_out[...] = gate_grad
    up_out[...] = up_grad
    part_ref[...] = (
        cols_cols(gate_grad, pair_ref[0]) + cols_cols(up_grad, pair_ref[1])
    ).astype(BF)


def shape(dims, kind):
    return jax.ShapeDtypeStruct(dims, kind)


def call(kernel, name, out_shape, grid=None, in_specs=None, out_specs=None, scratch=()):
    options = {}
    if grid is not None:
        options = {"grid": grid, "in_specs": in_specs, "out_specs": out_specs}
    return pl.pallas_call(
        kernel,
        out_shape=out_shape,
        scratch_shapes=list(scratch),
        name=name,
        compiler_params=pltpu.CompilerParams(vmem_limit_bytes=56 * 1024 * 1024),
        **options,
    )


def by_block(dims):
    return pl.BlockSpec((1,) + dims, lambda g: (g,) + (0,) * len(dims))


def whole(dims):
    return pl.BlockSpec(dims, lambda g: (0,) * len(dims), pipeline_mode=pl.Buffered(1))


def body(
    n_rep,
    n_shard,
    tokens,
    seq_lengths,
    deal_order,
    attn_gain,
    mlp_gain,
    q_weight,
    k_weight,
    v_weight,
    o_weight,
    gate_weight,
    up_weight,
    down_weight,
    cotangent,
):
    rows, width = tokens.shape
    r = lax.axis_index("rep")
    s = lax.axis_index("shard")
    own = width // n_shard
    fine = own // n_rep
    hidden = down_weight.shape[0]
    q_cols = width // n_rep
    heads = H // n_rep
    pair = n_shard // n_rep
    share = max(n_rep // KVH, 1)
    kv_at = (r * KVH) // n_rep
    all_rows = n_rep * rows
    span = HALO + rows
    qkv_cols = q_cols + 2 * HD

    starts = jnp.cumsum(seq_lengths[0]) - seq_lengths[0]
    places = s * rows + jnp.arange(rows, dtype=jnp.int32)
    first = jnp.max(
        jnp.where(starts[None, :] <= places[:, None], starts[None, :], 0), axis=1, keepdims=True
    )
    offset = jnp.broadcast_to((places[:, None] - first).astype(BF), (rows, LANES))

    w_qkv_own = jnp.concatenate(
        [
            lax.dynamic_slice_in_dim(q_weight, r * q_cols, q_cols, 1),
            lax.dynamic_slice_in_dim(k_weight, kv_at * HD, HD, 1),
            lax.dynamic_slice_in_dim(v_weight, kv_at * HD, HD, 1),
        ],
        axis=1,
    )
    w_qkv = lax.all_gather(w_qkv_own, "shard", axis=0, tiled=True)
    w_o = lax.all_gather(
        lax.dynamic_slice_in_dim(o_weight, r * fine, fine, 0), "shard", axis=0, tiled=True
    )
    x_all = spread(jnp.concatenate([tokens, offset], axis=1), "rep", n_rep)
    gains = lax.all_gather(jnp.stack([attn_gain, mlp_gain]), "shard", axis=1, tiled=True)
    gain_one = gains[0:1].astype(F32)
    gain_two = gains[1:2].astype(F32)

    def quarter(weight):
        part = lax.dynamic_slice_in_dim(weight, r * fine, fine, 0)
        return part.reshape(fine, n_shard, hidden).transpose(1, 0, 2)

    w_pair = jnp.stack([quarter(gate_weight), quarter(up_weight)], axis=1)
    w_pair = swap(w_pair, "shard")
    w_pair = spread_far(w_pair, "rep", n_rep)
    grown = jnp.zeros((2, n_shard, n_rep, fine, hidden), BF)
    for k, piece in enumerate(w_pair):
        piece = piece.transpose(1, 0, 2, 3)[:, :, None]
        grown = lax.dynamic_update_slice_in_dim(grown, piece, r ^ k, 2)
    w_pair = grown.reshape(2, width, hidden)
    cot_all = lax.all_gather(cotangent, "shard", axis=0, tiled=True)

    half = HD // 2
    inverse = ROPE_BASE ** (-2.0 * (jnp.arange(LANES) % half).astype(F32) / HD)
    angles = x_all[:, :, width:].astype(F32) * inverse[None, None, :]
    cosine, sine = jnp.cos(angles), jnp.sin(angles)
    x_block = by_block((rows, width))
    table = by_block((rows, LANES))
    normed_one, queries, kv_own = call(
        in_kernel,
        "attn_in",
        (
            shape((n_rep, rows, width), BF),
            shape((n_rep, rows, q_cols), BF),
            shape((n_rep, rows, LANES), BF),
        ),
        (n_rep,),
        [x_block, whole((1, width)), whole((width, qkv_cols)), table, table],
        (x_block, by_block((rows, q_cols)), table),
    )(x_all, gain_one, w_qkv, cosine, sine)
    kv_halo = lax.ppermute(
        kv_own[:, rows - HALO :], "shard", [(i, i + 1) for i in range(n_shard - 1)]
    )
    head_block = pl.BlockSpec((n_rep, 1, rows, pair * fine), lambda g: (0, g, 0, 0))
    probs_block = by_block((heads, rows, span))
    probs, out_in = call(
        partial(attend_kernel, fine),
        "attend",
        (
            shape((n_rep, heads, rows, span), F32),
            shape((n_rep, n_rep, rows, pair * fine), BF),
        ),
        (n_rep,),
        [
            by_block((rows, q_cols)),
            table,
            by_block((HALO, LANES)),
            pl.BlockSpec((1, rows, LANES), lambda g: (g, 0, width // LANES)),
        ],
        (probs_block, head_block),
    )(queries, kv_own, kv_halo, x_all)
    out_in = swap(out_in, "rep").reshape(n_rep, all_rows, pair * fine)
    out_in = out_in.transpose(1, 0, 2).reshape(all_rows, q_cols)
    mid_part = rows_cols(out_in, w_o).astype(BF).reshape(n_rep, rows, width)
    x_mid, normed_two = call(
        middle_kernel, "middle", (shape((rows, width), F32), shape((rows, width), BF))
    )(swap(mid_part, "rep"), tokens, gain_two)

    two_all = lax.all_gather(normed_two, "shard", axis=0, tiled=True)
    step = 256
    group = two_all.shape[0]
    token_block = pl.BlockSpec((step, width), lambda g: (g, 0))
    hidden_block = pl.BlockSpec((step, hidden), lambda g: (g, 0))
    mixed, gate_grad, up_grad, two_grad_part = call(
        forward_back_kernel,
        "forward_back",
        (shape((group, hidden), BF),) * 3 + (shape((group, width), BF),),
        (group // step,),
        [token_block, token_block, whole((2, width, hidden)), whole((hidden, width))],
        (hidden_block,) * 3 + (token_block,),
    )(two_all, cot_all, w_pair, down_weight)
    two_grad = lax.psum_scatter(two_grad_part, "shard", scatter_dimension=0, tiled=True)
    mixed, two_grad_part = lax.optimization_barrier((mixed, two_grad_part))
    down_part = rows_cols(mixed, down_weight).astype(BF)
    down_rows = lax.psum_scatter(down_part, "shard", scatter_dimension=0, tiled=True)
    layer_out = (x_mid + down_rows.astype(F32)).astype(BF)

    mid_grad, branch, gain_two_rows = call(
        middle_back_kernel,
        "middle_back",
        (shape((rows, width), F32), shape((rows, width), BF), shape((rows, width), BF)),
    )(two_grad, x_mid, gain_two, cotangent)

    def total(pieces):
        return sum(piece.astype(F32) for piece in pieces).astype(BF)

    w_down_grad = rows_rows(mixed, cot_all).astype(BF)
    w_down_grad = total(
        swap_far(w_down_grad.reshape(n_rep, hidden // n_rep, width), "rep", n_rep, r)
    )
    down_out = place(spread_far(w_down_grad, "rep", n_rep), r, F32)
    w_pair_grad = jnp.stack([rows_rows(two_all, gate_grad), rows_rows(two_all, up_grad)])
    w_pair_grad = w_pair_grad.astype(BF).reshape(2, n_shard, n_rep, fine, hidden)
    w_pair_grad = total(swap_far(w_pair_grad.transpose(2, 1, 0, 3, 4), "rep", n_rep, r))
    w_pair_grad = swap(w_pair_grad, "shard")
    w_pair_grad = w_pair_grad.transpose(1, 2, 0, 3).reshape(2, fine, n_shard * hidden)
    gate_out = place(spread_far(w_pair_grad[0], "rep", n_rep), r, F32)
    up_out = place(spread_far(w_pair_grad[1], "rep", n_rep), r, F32)

    branch_all = spread(branch, "rep", n_rep).reshape(all_rows, width)
    in_grad = cols_cols(branch_all, w_o).astype(BF)
    in_grad = in_grad.reshape(all_rows, n_rep, pair * fine).transpose(1, 0, 2)
    in_grad = swap(in_grad, "rep").reshape(n_rep, n_rep, rows, pair * fine)
    w_o_grad = rows_rows(out_in, branch_all).astype(BF)
    w_o_grad = lax.psum_scatter(w_o_grad, "shard", scatter_dimension=0, tiled=True)
    o_out = place(spread_far(w_o_grad, "rep", n_rep), r, F32)
    query_grad, kv_grad = call(
        partial(attend_back_kernel, fine),
        "attend_back",
        (shape((n_rep, rows, q_cols), BF), shape((n_rep, span, LANES), F32)),
        (n_rep,),
        [
            head_block,
            probs_block,
            by_block((rows, q_cols)),
            table,
            by_block((HALO, LANES)),
            table,
            table,
        ],
        (by_block((rows, q_cols)), by_block((span, LANES))),
    )(in_grad, probs, queries, kv_own, kv_halo, cosine, sine)
    kv_back = lax.ppermute(
        kv_grad[:, :HALO], "shard", [(i + 1, i) for i in range(n_shard - 1)]
    )
    grad_cols = qkv_cols + LANES
    one_grad_part, w_qkv_grad = call(
        in_back_kernel,
        "attn_in_back",
        (shape((n_rep, rows, width), BF), shape((width, grad_cols), BF)),
        (n_rep,),
        [
            by_block((rows, q_cols)),
            by_block((span, LANES)),
            by_block((HALO, LANES)),
            table,
            table,
            x_block,
            x_block,
            whole((rows, width)),
            whole((width, qkv_cols)),
        ],
        (x_block, pl.BlockSpec((width, grad_cols), lambda g: (0, 0))),
        [pltpu.VMEM((width, grad_cols), F32)],
    )(
        query_grad, kv_grad, kv_back, cosine, sine, normed_one, x_all, gain_two_rows, w_qkv
    )
    w_qkv_grad = lax.psum_scatter(w_qkv_grad, "shard", scatter_dimension=0, tiled=True)
    input_grad = call(last_kernel, "last", shape((rows, width), BF))(
        swap(one_grad_part, "rep"), tokens, gain_one, mid_grad
    )
    w_qkv_grad = spread(w_qkv_grad, "rep", n_rep).astype(F32)

    def columns(part):
        return part.transpose(1, 0, 2).reshape(own, -1)

    def kv_columns(part):
        return columns(jnp.sum(part.reshape(-1, share, own, HD), axis=1))

    q_out = columns(w_qkv_grad[..., :q_cols])
    k_out = kv_columns(w_qkv_grad[..., q_cols : q_cols + HD])
    v_out = kv_columns(w_qkv_grad[..., q_cols + HD : qkv_cols])
    gain_sums = jnp.sum(w_qkv_grad[..., qkv_cols:], axis=0)
    return (
        layer_out,
        input_grad,
        gain_sums[:, 0],
        gain_sums[:, HD],
        q_out,
        k_out,
        v_out,
        o_out,
        gate_out,
        up_out,
        down_out,
    )


def solution(mesh):
    split = P("shard", None)
    by_token = P(("rep", "shard"), None)
    return jax.shard_map(
        partial(body, mesh.shape["rep"], mesh.shape["shard"]),
        mesh=mesh,
        in_specs=(by_token, P("rep", None), P("rep", None), P("shard"), P("shard"))
        + (split,) * 7
        + (by_token,),
        out_specs=(by_token, by_token, P("shard"), P("shard")) + (split,) * 7,
        check_vma=False,
    )
```

```python
from functools import partial

import jax
import jax.numpy as jnp
from jax import lax
from jax.experimental import pallas as pl
from jax.experimental.pallas import tpu as pltpu
from jax.sharding import PartitionSpec as P


H = 32
KVH = 4
HD = 64
HALO = 64
LANES = 128

EPSILON = 1e-05
ROPE_BASE = 10000.0
NEG_FILL = -1e30

BF = jnp.bfloat16
F32 = jnp.float32


def dot(left, right, contract):
    return lax.dot_general(left, right, (contract, ((), ())), preferred_element_type=F32)


def rows_cols(left, right):
    return dot(left, right, ((1,), (0,)))


def rows_rows(left, right):
    return dot(left, right, ((0,), (0,)))


def cols_cols(left, right):
    return dot(left, right, ((1,), (1,)))


def spread(value, axis, count):
    wide = jnp.broadcast_to(value[None], (count,) + value.shape)
    return lax.all_to_all(wide, axis, split_axis=0, concat_axis=0, tiled=True)


def swap(value, axis):
    return lax.all_to_all(value, axis, split_axis=0, concat_axis=0, tiled=True)


def pairs(count, step):
    return [(i, i ^ step) for i in range(count)]


def send(value, axis, count, step):
    return lax.ppermute(value, axis, pairs(count, step))


def sum_rep(chunks, count):
    wide = lambda value: value.astype(F32)
    go = lambda value, step: send(value, "rep", count, step)
    if count != 4:
        return tuple(
            sum([wide(go(chunks[k][h], k)) for k in range(1, count)], wide(chunks[0][h]))
            for h in range(2)
        )
    first_one = go(chunks[1][0], 1)
    first_two = go(chunks[3][0], 1)
    second_one = go(chunks[2][1], 2)
    second_two = go(chunks[3][1], 2)
    joint_one = (wide(chunks[2][0]) + wide(first_two)).astype(BF)
    joint_two = (wide(chunks[1][1]) + wide(second_two)).astype(BF)
    last_one = go(joint_one, 2)
    last_two = go(joint_two, 1)
    return (
        wide(chunks[0][0]) + wide(first_one) + wide(last_one),
        wide(chunks[0][1]) + wide(second_one) + wide(last_two),
    )


def gather_rep(halves, count):
    go = lambda value, step: send(value, "rep", count, step)
    if count != 4:
        return [halves] + [tuple(go(v, k) for v in halves) for k in range(1, count)]
    one = tuple(go(v, 1) for v in halves)
    two = tuple(go(v, 2) for v in halves)
    return [halves, one, two, (go(one[0], 2), go(two[1], 1))]


def place_kernel(count, me_ref, *refs):
    parts, out_ref = refs[:-1], refs[-1]
    at = pl.program_id(0)
    size = len(parts) // count
    for k in range(count):

        @pl.when(at == jnp.bitwise_xor(me_ref[0], k))
        def _(k=k):
            row = 0
            for part in parts[k * size : (k + 1) * size]:
                out_ref[0, row : row + part.shape[0]] = part[...].astype(F32)
                row += part.shape[0]


def place(pieces, me):
    count = len(pieces)
    flat = [part for piece in pieces for part in piece]
    rows = sum(part.shape[0] for part in pieces[0])
    width = flat[0].shape[1]
    grid = pltpu.PrefetchScalarGridSpec(
        num_scalar_prefetch=1,
        grid=(count,),
        in_specs=[
            pl.BlockSpec(part.shape, lambda g, me: (0, 0), pipeline_mode=pl.Buffered(1))
            for part in flat
        ],
        out_specs=pl.BlockSpec((1, rows, width), lambda g, me: (g, 0, 0)),
    )
    return pl.pallas_call(
        partial(place_kernel, count),
        out_shape=shape((count, rows, width), F32),
        grid_spec=grid,
        compiler_params=pltpu.CompilerParams(vmem_limit_bytes=56 * 1024 * 1024),
    )(me.astype(jnp.int32).reshape(1), *flat).reshape(count * rows, width)


def norm_scale(value):
    return lax.rsqrt(jnp.mean(value * value, axis=1, keepdims=True) + EPSILON)


def turn(tile, cosine, sine):
    lane = lax.broadcasted_iota(jnp.int32, tile.shape, 1)
    swapped = jnp.where(
        lane % HD < HD // 2,
        -pltpu.roll(tile, LANES - HD // 2, 1),
        pltpu.roll(tile, HD // 2, 1),
    )
    return tile * cosine + swapped * sine


def turn_first(tile, cosine, sine):
    lane = lax.broadcasted_iota(jnp.int32, tile.shape, 1)
    return jnp.where(lane < HD, turn(tile, cosine, sine), tile)


def in_kernel(x_ref, gain_ref, w_ref, cos_ref, sin_ref, normed_ref, q_ref, kv_ref):
    x = x_ref[0].astype(F32)
    normed = (x * norm_scale(x) * gain_ref[...]).astype(BF)
    normed_ref[0] = normed
    qkv = rows_cols(normed, w_ref[...])
    cosine, sine = cos_ref[0], sin_ref[0]
    q_cols = q_ref.shape[2]
    for at in range(0, q_cols, LANES):
        q_ref[0, :, at : at + LANES] = turn(qkv[:, at : at + LANES], cosine, sine).astype(BF)
    kv_ref[0] = turn_first(qkv[:, q_cols:], cosine, sine).astype(BF)


def stack_heads(value):
    return jnp.concatenate(
        [value[:, at : at + HD] for at in range(0, value.shape[1], HD)], axis=0
    )


def unstack_heads(value, rows):
    return jnp.concatenate(
        [value[at : at + rows] for at in range(0, value.shape[0], rows)], axis=1
    )


def attend_kernel(fine, q_ref, own_ref, halo_ref, pos_ref, probs_ref, out_ref):
    rows, q_cols = q_ref.shape[1:]
    heads = q_cols // HD
    count = out_ref.shape[0]
    kv = jnp.concatenate([halo_ref[0], own_ref[0]], axis=0)
    keys, values = kv[:, :HD], kv[:, HD:]
    span = kv.shape[0]
    scores = cols_cols(stack_heads(q_ref[0]), keys) * (HD**-0.5)
    query = lax.broadcasted_iota(jnp.int32, (rows, span), 0) + HALO
    key = lax.broadcasted_iota(jnp.int32, (rows, span), 1)
    first = query - pos_ref[0][:, :1].astype(jnp.int32)
    allowed = (key >= first) & (key <= query)
    scores = jnp.where(allowed[None], scores.reshape(heads, rows, span), NEG_FILL)
    grown = jnp.exp(scores - jnp.max(scores, axis=-1, keepdims=True))
    probs = grown / jnp.sum(grown, axis=-1, keepdims=True)
    probs_ref[0] = probs
    mixed = rows_cols(probs.reshape(heads * rows, span).astype(BF), values)
    mixed = unstack_heads(mixed, rows).astype(BF)
    for to in range(count):
        out_ref[to, 0] = jnp.concatenate(
            [
                mixed[:, at + to * fine : at + (to + 1) * fine]
                for at in range(0, q_cols, count * fine)
            ],
            axis=1,
        )


def attend_back_kernel(
    fine, grad_ref, probs_ref, q_ref, own_ref, halo_ref, cos_ref, sin_ref, q_out, kv_out
):
    rows, q_cols = q_ref.shape[1:]
    heads = q_cols // HD
    count = grad_ref.shape[0]
    kv = jnp.concatenate([halo_ref[0], own_ref[0]], axis=0)
    keys, values = kv[:, :HD], kv[:, HD:]
    span = kv.shape[0]
    grad = jnp.concatenate(
        [
            grad_ref[source, 0][:, at * fine : (at + 1) * fine]
            for at in range(q_cols // (count * fine))
            for source in range(count)
        ],
        axis=1,
    )
    grad = stack_heads(grad)
    probs = probs_ref[0].reshape(heads * rows, span)
    probs_grad = cols_cols(grad, values)
    inner = jnp.sum(probs * probs_grad, axis=-1, keepdims=True)
    score_grad = (probs * (probs_grad - inner)).astype(BF)
    scale = HD**-0.5
    key_grad = rows_rows(score_grad, stack_heads(q_ref[0])) * scale
    value_grad = rows_rows(probs.astype(BF), grad)
    kv_out[0] = jnp.concatenate([key_grad, value_grad], axis=1)
    query_grad = unstack_heads(rows_cols(score_grad, keys) * scale, rows)
    cosine, sine = cos_ref[0], -sin_ref[0]
    for at in range(0, q_cols, LANES):
        q_out[0, :, at : at + LANES] = turn(
            query_grad[:, at : at + LANES], cosine, sine
        ).astype(BF)


def in_back_kernel(
    dq_ref, dkv_ref, back_ref, cos_ref, sin_ref, normed_ref, x_ref, two_ref, w_ref,
    part_ref, grad_ref, total_ref,
):
    at = pl.program_id(0)
    rows = dq_ref.shape[1]
    own = dkv_ref[0, HALO:]
    tail = own[rows - HALO :] + back_ref[0]
    own = jnp.concatenate([own[: rows - HALO], tail], axis=0)
    own = turn_first(own, cos_ref[0], -sin_ref[0]).astype(BF)
    qkv_grad = jnp.concatenate([dq_ref[0], own], axis=1)
    normed_grad = cols_cols(qkv_grad, w_ref[...])
    part_ref[0] = normed_grad.astype(BF)
    x = x_ref[0].astype(F32)
    one = (normed_grad * x * norm_scale(x)).astype(BF)
    cols = qkv_grad.shape[1]
    lane = lax.broadcasted_iota(jnp.int32, (rows, LANES), 1)

    @pl.when(at == 0)
    def _():
        total_ref[:, :cols] = rows_rows(normed_ref[0], qkv_grad)
        total_ref[:, cols:] = rows_rows(one, (lane < HD).astype(BF)) + rows_rows(
            two_ref[...], (lane >= HD).astype(BF)
        )

    @pl.when(at > 0)
    def _():
        total_ref[:, :cols] += rows_rows(normed_ref[0], qkv_grad)
        total_ref[:, cols:] += rows_rows(one, (lane < HD).astype(BF))

    @pl.when(at == pl.num_programs(0) - 1)
    def _():
        grad_ref[...] = total_ref[...].astype(BF)


def middle_kernel(part_ref, x_ref, gain_ref, mid_ref, normed_ref):
    mid = x_ref[...].astype(F32)
    for at in range(part_ref.shape[0]):
        mid += part_ref[at].astype(F32)
    mid_ref[...] = mid
    normed_ref[...] = (mid * norm_scale(mid) * gain_ref[...]).astype(BF)


def middle_back_kernel(grad_ref, mid_ref, gain_ref, cot_ref, out_ref, low_ref, gain_out_ref):
    mid = mid_ref[...]
    scale = norm_scale(mid)
    grad = grad_ref[...].astype(F32)
    gain_out_ref[...] = (grad * mid * scale).astype(BF)
    scaled = grad * gain_ref[...]
    out = (
        cot_ref[...].astype(F32)
        + scale * scaled
        - mid * scale**3 * jnp.mean(scaled * mid, axis=1, keepdims=True)
    )
    out_ref[...] = out
    low_ref[...] = out.astype(BF)


def last_kernel(part_ref, x_ref, gain_ref, mid_ref, out_ref):
    x = x_ref[...].astype(F32)
    scale = norm_scale(x)
    grad = part_ref[0].astype(F32)
    for at in range(1, part_ref.shape[0]):
        grad += part_ref[at].astype(F32)
    scaled = grad * gain_ref[...]
    out = (
        mid_ref[...]
        + scale * scaled
        - x * scale**3 * jnp.mean(scaled * x, axis=1, keepdims=True)
    )
    out_ref[...] = out.astype(BF)


def forward_back_kernel(
    x_ref, cot_ref, pair_ref, down_ref, mixed_ref, gate_out, up_out, part_ref
):
    x = x_ref[...]
    gate = rows_cols(x, pair_ref[0])
    up = rows_cols(x, pair_ref[1])
    mixed_grad = cols_cols(cot_ref[...], down_ref[...])
    sigma = jax.nn.sigmoid(gate)
    silu = gate * sigma
    mixed_ref[...] = (silu * up).astype(BF)
    gate_grad = (mixed_grad * up * sigma * (1.0 + gate * (1.0 - sigma))).astype(BF)
    up_grad = (mixed_grad * silu).astype(BF)
    gate_out[...] = gate_grad
    up_out[...] = up_grad
    part_ref[...] = (
        cols_cols(gate_grad, pair_ref[0]) + cols_cols(up_grad, pair_ref[1])
    ).astype(BF)


def shape(dims, kind):
    return jax.ShapeDtypeStruct(dims, kind)


def call(kernel, out_shape, grid=None, in_specs=None, out_specs=None, scratch=()):
    options = {}
    if grid is not None:
        options = {"grid": grid, "in_specs": in_specs, "out_specs": out_specs}
    return pl.pallas_call(
        kernel,
        out_shape=out_shape,
        scratch_shapes=list(scratch),
        compiler_params=pltpu.CompilerParams(vmem_limit_bytes=56 * 1024 * 1024),
        **options,
    )


def by_block(dims):
    return pl.BlockSpec((1,) + dims, lambda g: (g,) + (0,) * len(dims))


def whole(dims):
    return pl.BlockSpec(dims, lambda g: (0,) * len(dims), pipeline_mode=pl.Buffered(1))


def body(
    n_rep,
    n_shard,
    tokens,
    seq_lengths,
    deal_order,
    attn_gain,
    mlp_gain,
    q_weight,
    k_weight,
    v_weight,
    o_weight,
    gate_weight,
    up_weight,
    down_weight,
    cotangent,
):
    rows, width = tokens.shape
    r = lax.axis_index("rep")
    s = lax.axis_index("shard")
    own = width // n_shard
    fine = own // n_rep
    hidden = down_weight.shape[0]
    q_cols = width // n_rep
    heads = H // n_rep
    pair = n_shard // n_rep
    share = max(n_rep // KVH, 1)
    kv_at = (r * KVH) // n_rep
    all_rows = n_rep * rows
    span = HALO + rows
    qkv_cols = q_cols + 2 * HD

    starts = jnp.cumsum(seq_lengths[0]) - seq_lengths[0]
    places = s * rows + jnp.arange(rows, dtype=jnp.int32)
    first = jnp.max(
        jnp.where(starts[None, :] <= places[:, None], starts[None, :], 0), axis=1, keepdims=True
    )
    offset = jnp.broadcast_to((places[:, None] - first).astype(BF), (rows, LANES))

    w_qkv_own = jnp.concatenate(
        [
            lax.dynamic_slice_in_dim(q_weight, r * q_cols, q_cols, 1),
            lax.dynamic_slice_in_dim(k_weight, kv_at * HD, HD, 1),
            lax.dynamic_slice_in_dim(v_weight, kv_at * HD, HD, 1),
        ],
        axis=1,
    )
    w_qkv = lax.all_gather(w_qkv_own, "shard", axis=0, tiled=True)
    w_o = lax.all_gather(
        lax.dynamic_slice_in_dim(o_weight, r * fine, fine, 0), "shard", axis=0, tiled=True
    )
    x_all = spread(jnp.concatenate([tokens, offset], axis=1), "rep", n_rep)
    gains = lax.all_gather(jnp.stack([attn_gain, mlp_gain]), "shard", axis=1, tiled=True)
    gain_one = gains[0:1].astype(F32)
    gain_two = gains[1:2].astype(F32)

    def exchange_shard(value):
        total = jnp.zeros_like(value)
        for k in range(n_shard):
            piece = lax.dynamic_slice_in_dim(value, s ^ k, 1, 0)
            if k:
                piece = send(piece, "shard", n_shard, k)
            total = lax.dynamic_update_slice_in_dim(total, piece, s ^ k, 0)
        return total

    def quarter(weight):
        part = lax.dynamic_slice_in_dim(weight, r * fine, fine, 0)
        return part.reshape(fine, n_shard, hidden).transpose(1, 0, 2)

    w_pair = jnp.stack([quarter(gate_weight), quarter(up_weight)], axis=1)
    w_pair = exchange_shard(w_pair).transpose(1, 0, 2, 3)
    w_pair = gather_rep((w_pair[0], w_pair[1]), n_rep)
    grown = jnp.zeros((2, n_shard, n_rep, fine, hidden), BF)
    for k, piece in enumerate(w_pair):
        for h in range(2):
            grown = lax.dynamic_update_slice(
                grown, piece[h][None, :, None], (h, 0, r ^ k, 0, 0)
            )
    w_pair = grown.reshape(2, width, hidden)
    cot_all = lax.all_gather(cotangent, "shard", axis=0, tiled=True)

    half = HD // 2
    inverse = ROPE_BASE ** (-2.0 * (jnp.arange(LANES) % half).astype(F32) / HD)
    angles = x_all[:, :, width:].astype(F32) * inverse[None, None, :]
    cosine, sine = jnp.cos(angles), jnp.sin(angles)
    x_block = by_block((rows, width))
    table = by_block((rows, LANES))
    normed_one, queries, kv_own = call(
        in_kernel,
        (
            shape((n_rep, rows, width), BF),
            shape((n_rep, rows, q_cols), BF),
            shape((n_rep, rows, LANES), BF),
        ),
        (n_rep,),
        [x_block, whole((1, width)), whole((width, qkv_cols)), table, table],
        (x_block, by_block((rows, q_cols)), table),
    )(x_all, gain_one, w_qkv, cosine, sine)
    kv_halo = lax.ppermute(
        kv_own[:, rows - HALO :], "shard", [(i, i + 1) for i in range(n_shard - 1)]
    )
    head_block = pl.BlockSpec((n_rep, 1, rows, pair * fine), lambda g: (0, g, 0, 0))
    probs_block = by_block((heads, rows, span))
    probs, out_in = call(
        partial(attend_kernel, fine),
        (
            shape((n_rep, heads, rows, span), F32),
            shape((n_rep, n_rep, rows, pair * fine), BF),
        ),
        (n_rep,),
        [
            by_block((rows, q_cols)),
            table,
            by_block((HALO, LANES)),
            pl.BlockSpec((1, rows, LANES), lambda g: (g, 0, width // LANES)),
        ],
        (probs_block, head_block),
    )(queries, kv_own, kv_halo, x_all)
    out_in = swap(out_in, "rep").reshape(n_rep, all_rows, pair * fine)
    out_in = out_in.transpose(1, 0, 2).reshape(all_rows, q_cols)
    mid_part = rows_cols(out_in, w_o).astype(BF).reshape(n_rep, rows, width)
    x_mid, normed_two = call(
        middle_kernel, (shape((rows, width), F32), shape((rows, width), BF))
    )(swap(mid_part, "rep"), tokens, gain_two)

    two_all = lax.all_gather(normed_two, "shard", axis=0, tiled=True)
    step = 256
    group = two_all.shape[0]
    token_block = pl.BlockSpec((step, width), lambda g: (g, 0))
    hidden_block = pl.BlockSpec((step, hidden), lambda g: (g, 0))
    mixed, gate_grad, up_grad, two_grad_part = call(
        forward_back_kernel,
        (shape((group, hidden), BF),) * 3 + (shape((group, width), BF),),
        (group // step,),
        [token_block, token_block, whole((2, width, hidden)), whole((hidden, width))],
        (hidden_block,) * 3 + (token_block,),
    )(two_all, cot_all, w_pair, down_weight)
    two_grad = lax.psum_scatter(two_grad_part, "shard", scatter_dimension=0, tiled=True)
    mixed, two_grad_part = lax.optimization_barrier((mixed, two_grad_part))
    down_part = rows_cols(mixed, down_weight).astype(BF)
    down_rows = lax.psum_scatter(down_part, "shard", scatter_dimension=0, tiled=True)
    layer_out = (x_mid + down_rows.astype(F32)).astype(BF)

    mid_grad, branch, gain_two_rows = call(
        middle_back_kernel,
        (shape((rows, width), F32), shape((rows, width), BF), shape((rows, width), BF)),
    )(two_grad, x_mid, gain_two, cotangent)

    part_rows = hidden // n_rep
    cut = (part_rows // 2 + 15) // 16 * 16
    w_down_grad = rows_rows(mixed, cot_all).astype(BF)
    chunks = []
    for k in range(n_rep):
        at = (r ^ k) * part_rows
        chunks.append(
            (
                lax.dynamic_slice_in_dim(w_down_grad, at, cut, 0),
                lax.dynamic_slice_in_dim(w_down_grad, at + cut, part_rows - cut, 0),
            )
        )
    low = lambda values: tuple(value.astype(BF) for value in values)
    w_down_grad = low(sum_rep(chunks, n_rep))
    down_out = place(gather_rep(w_down_grad, n_rep), r)
    halves = [
        rows_rows(two_all, part).astype(BF).reshape(n_shard, n_rep, fine, hidden)
        for part in (gate_grad, up_grad)
    ]
    chunks = [
        tuple(lax.dynamic_index_in_dim(half, r ^ k, 1, False) for half in halves)
        for k in range(n_rep)
    ]
    w_pair_grad = low(sum_rep(chunks, n_rep))
    w_pair_grad = exchange_shard(jnp.stack(w_pair_grad, axis=1))
    w_pair_grad = w_pair_grad.transpose(1, 2, 0, 3).reshape(2, fine, n_shard * hidden)
    w_pair_grad = gather_rep((w_pair_grad[0], w_pair_grad[1]), n_rep)
    gate_out = place([piece[:1] for piece in w_pair_grad], r)
    up_out = place([piece[1:] for piece in w_pair_grad], r)

    branch_all = spread(branch, "rep", n_rep).reshape(all_rows, width)
    in_grad = cols_cols(branch_all, w_o).astype(BF)
    in_grad = in_grad.reshape(all_rows, n_rep, pair * fine).transpose(1, 0, 2)
    in_grad = swap(in_grad, "rep").reshape(n_rep, n_rep, rows, pair * fine)
    w_o_grad = rows_rows(out_in, branch_all).astype(BF)
    w_o_grad = lax.psum_scatter(w_o_grad, "shard", scatter_dimension=0, tiled=True)
    w_o_grad = (w_o_grad[: fine // 2], w_o_grad[fine // 2 :])
    o_out = place(gather_rep(w_o_grad, n_rep), r)
    query_grad, kv_grad = call(
        partial(attend_back_kernel, fine),
        (shape((n_rep, rows, q_cols), BF), shape((n_rep, span, LANES), F32)),
        (n_rep,),
        [
            head_block,
            probs_block,
            by_block((rows, q_cols)),
            table,
            by_block((HALO, LANES)),
            table,
            table,
        ],
        (by_block((rows, q_cols)), by_block((span, LANES))),
    )(in_grad, probs, queries, kv_own, kv_halo, cosine, sine)
    kv_back = lax.ppermute(
        kv_grad[:, :HALO], "shard", [(i + 1, i) for i in range(n_shard - 1)]
    )
    grad_cols = qkv_cols + LANES
    one_grad_part, w_qkv_grad = call(
        in_back_kernel,
        (shape((n_rep, rows, width), BF), shape((width, grad_cols), BF)),
        (n_rep,),
        [
            by_block((rows, q_cols)),
            by_block((span, LANES)),
            by_block((HALO, LANES)),
            table,
            table,
            x_block,
            x_block,
            whole((rows, width)),
            whole((width, qkv_cols)),
        ],
        (x_block, pl.BlockSpec((width, grad_cols), lambda g: (0, 0))),
        [pltpu.VMEM((width, grad_cols), F32)],
    )(
        query_grad, kv_grad, kv_back, cosine, sine, normed_one, x_all, gain_two_rows, w_qkv
    )
    w_qkv_grad = lax.psum_scatter(w_qkv_grad, "shard", scatter_dimension=0, tiled=True)
    input_grad = call(last_kernel, shape((rows, width), BF))(
        swap(one_grad_part, "rep"), tokens, gain_one, mid_grad
    )
    w_qkv_grad = spread(w_qkv_grad, "rep", n_rep).astype(F32)

    def columns(part):
        return part.transpose(1, 0, 2).reshape(own, -1)

    def kv_columns(part):
        return columns(jnp.sum(part.reshape(-1, share, own, HD), axis=1))

    q_out = columns(w_qkv_grad[..., :q_cols])
    k_out = kv_columns(w_qkv_grad[..., q_cols : q_cols + HD])
    v_out = kv_columns(w_qkv_grad[..., q_cols + HD : qkv_cols])
    gain_sums = jnp.sum(w_qkv_grad[..., qkv_cols:], axis=0)
    return (
        layer_out,
        input_grad,
        gain_sums[:, 0],
        gain_sums[:, HD],
        q_out,
        k_out,
        v_out,
        o_out,
        gate_out,
        up_out,
        down_out,
    )


def solution(mesh):
    split = P("shard", None)
    by_token = P(("rep", "shard"), None)
    return jax.shard_map(
        partial(body, mesh.shape["rep"], mesh.shape["shard"]),
        mesh=mesh,
        in_specs=(by_token, P("rep", None), P("rep", None), P("shard"), P("shard"))
        + (split,) * 7
        + (by_token,),
        out_specs=(by_token, by_token, P("shard"), P("shard")) + (split,) * 7,
        check_vma=False,
    )
```

```python
from functools import partial

import jax
import jax.numpy as jnp
from jax import lax
from jax.experimental import pallas as pl
from jax.experimental.pallas import tpu as pltpu
from jax.sharding import PartitionSpec as P


H = 32
KVH = 4
HD = 64
HALO = 64
LANES = 128

EPSILON = 1e-05
ROPE_BASE = 10000.0
NEG_FILL = -1e30

BF = jnp.bfloat16
F32 = jnp.float32


def dot(left, right, contract):
    return lax.dot_general(left, right, (contract, ((), ())), preferred_element_type=F32)


def rows_cols(left, right):
    return dot(left, right, ((1,), (0,)))


def rows_rows(left, right):
    return dot(left, right, ((0,), (0,)))


def cols_cols(left, right):
    return dot(left, right, ((1,), (1,)))


def spread(value, axis, count):
    wide = jnp.broadcast_to(value[None], (count,) + value.shape)
    return lax.all_to_all(wide, axis, split_axis=0, concat_axis=0, tiled=True)


def swap(value, axis):
    return lax.all_to_all(value, axis, split_axis=0, concat_axis=0, tiled=True)


def pairs(count, step):
    return [(i, i ^ step) for i in range(count)]


def send(value, axis, count, step):
    return lax.ppermute(value, axis, pairs(count, step))


def parts_rep(chunks, count):
    go = lambda value, step: send(value, "rep", count, step)
    if count != 4:
        return [
            [chunks[0][h]] + [go(chunks[k][h], k) for k in range(1, count)]
            for h in range(2)
        ]
    add = lambda left, right: (left.astype(F32) + right.astype(F32)).astype(BF)
    first_one = go(chunks[1][0], 1)
    first_two = go(chunks[3][0], 1)
    second_one = go(chunks[2][1], 2)
    second_two = go(chunks[3][1], 2)
    last_one = go(add(chunks[2][0], first_two), 2)
    last_two = go(add(chunks[1][1], second_two), 1)
    return [[chunks[0][0], first_one, last_one], [chunks[0][1], second_one, last_two]]


def gather_rep(halves, count):
    go = lambda value, step: send(value, "rep", count, step)
    if count != 4:
        return [halves] + [tuple(go(v, k) for v in halves) for k in range(1, count)]
    one = tuple(go(v, 1) for v in halves)
    two = tuple(go(v, 2) for v in halves)
    return [halves, one, two, (go(one[0], 2), go(two[1], 1))]


def place_kernel(count, me_ref, *refs):
    parts, out_ref = refs[:-1], refs[-1]
    at = pl.program_id(0)
    size = len(parts) // count
    for k in range(count):

        @pl.when(at == jnp.bitwise_xor(me_ref[0], k))
        def _(k=k):
            row = 0
            for part in parts[k * size : (k + 1) * size]:
                out_ref[0, row : row + part.shape[0]] = part[...].astype(F32)
                row += part.shape[0]


def place(pieces, me):
    count = len(pieces)
    flat = [part for piece in pieces for part in piece]
    rows = sum(part.shape[0] for part in pieces[0])
    width = flat[0].shape[1]
    grid = pltpu.PrefetchScalarGridSpec(
        num_scalar_prefetch=1,
        grid=(count,),
        in_specs=[
            pl.BlockSpec(part.shape, lambda g, me: (0, 0), pipeline_mode=pl.Buffered(1))
            for part in flat
        ],
        out_specs=pl.BlockSpec((1, rows, width), lambda g, me: (g, 0, 0)),
    )
    return pl.pallas_call(
        partial(place_kernel, count),
        out_shape=shape((count, rows, width), F32),
        grid_spec=grid,
        compiler_params=pltpu.CompilerParams(vmem_limit_bytes=56 * 1024 * 1024),
    )(me.astype(jnp.int32).reshape(1), *flat).reshape(count * rows, width)


def split_kernel(id_ref, gate_ref, up_ref, *refs):
    outs, both = refs[:-1], refs[-1]
    hidden = both.shape[3]
    for h, ref in enumerate((gate_ref, up_ref)):
        value = ref[...]
        for at in range(len(outs)):
            both[at, h] = value[:, at * hidden : (at + 1) * hidden]
    for k, out in enumerate(outs):
        out[...] = both[jnp.bitwise_xor(id_ref[1], k)]


def split_pair(ids, gate, up, fine, count):
    hidden = gate.shape[1] // count
    rows = pl.BlockSpec((fine, gate.shape[1]), lambda g, ids: (ids[0], 0))
    piece = (2, fine, hidden)
    return pl.pallas_call(
        split_kernel,
        out_shape=(shape(piece, BF),) * count,
        grid_spec=pltpu.PrefetchScalarGridSpec(
            num_scalar_prefetch=1,
            grid=(1,),
            in_specs=[rows, rows],
            out_specs=(pl.BlockSpec(piece, lambda g, ids: (0, 0, 0)),) * count,
            scratch_shapes=[pltpu.VMEM((count,) + piece, BF)],
        ),
        name="split_pair",
    )(ids, gate, up)


def flat_call(kernel, ids, out_shape, values, scratch=()):
    specs = [pl.BlockSpec(memory_space=pltpu.SMEM)]
    specs += [pl.BlockSpec(memory_space=pltpu.VMEM)] * len(values)
    return pl.pallas_call(
        kernel,
        out_shape=out_shape,
        in_specs=specs,
        scratch_shapes=list(scratch),
        compiler_params=pltpu.CompilerParams(vmem_limit_bytes=56 * 1024 * 1024),
    )(ids, *values)


def order_kernel(id_ref, *refs):
    pieces, (gate_ref, up_ref) = refs[:-2], refs[-2:]
    for k, piece in enumerate(pieces):
        at = jnp.bitwise_xor(id_ref[1], k)
        gate_ref[at] = piece[0]
        up_ref[at] = piece[1]


def join_kernel(id_ref, *refs):
    out_ref = refs[-1]
    for k in range(len(refs) // 2):
        at = jnp.bitwise_xor(id_ref[0], k)
        for h in range(2):
            value = refs[2 * k + h]
            for row in range(value.shape[0]):
                out_ref[h, row, at] = value[row]


def sum_kernel(id_ref, *refs):
    count = refs[0].shape[0]
    outs = refs[len(refs) - count :]
    parts = refs[: len(refs) - count]
    half = len(parts) // 2
    for k, out in enumerate(outs):
        at = jnp.bitwise_xor(id_ref[1], k)
        for h in range(2):
            total = parts[h * half][at].astype(F32)
            for part in parts[h * half + 1 : (h + 1) * half]:
                total += part[at].astype(F32)
            out[h] = total.astype(BF)


def widen_kernel(id_ref, *refs):
    pieces, (gate_ref, up_ref, both) = refs[:-3], refs[-3:]
    hidden = both.shape[3]
    for k, piece in enumerate(pieces):
        both[jnp.bitwise_xor(id_ref[1], k)] = piece[...]
    for h, ref in enumerate((gate_ref, up_ref)):
        for at in range(len(pieces)):
            ref[:, at * hidden : (at + 1) * hidden] = both[at, h]


def norm_scale(value):
    return lax.rsqrt(jnp.mean(value * value, axis=1, keepdims=True) + EPSILON)


def turn(tile, cosine, sine):
    lane = lax.broadcasted_iota(jnp.int32, tile.shape, 1)
    swapped = jnp.where(
        lane % HD < HD // 2,
        -pltpu.roll(tile, LANES - HD // 2, 1),
        pltpu.roll(tile, HD // 2, 1),
    )
    return tile * cosine + swapped * sine


def turn_first(tile, cosine, sine):
    lane = lax.broadcasted_iota(jnp.int32, tile.shape, 1)
    return jnp.where(lane < HD, turn(tile, cosine, sine), tile)


def in_kernel(x_ref, gain_ref, w_ref, cos_ref, sin_ref, normed_ref, q_ref, kv_ref):
    x = x_ref[0].astype(F32)
    normed = (x * norm_scale(x) * gain_ref[...]).astype(BF)
    normed_ref[0] = normed
    qkv = rows_cols(normed, w_ref[...])
    cosine, sine = cos_ref[0], sin_ref[0]
    q_cols = q_ref.shape[2]
    for at in range(0, q_cols, LANES):
        q_ref[0, :, at : at + LANES] = turn(qkv[:, at : at + LANES], cosine, sine).astype(BF)
    kv_ref[0] = turn_first(qkv[:, q_cols:], cosine, sine).astype(BF)


def stack_heads(value):
    return jnp.concatenate(
        [value[:, at : at + HD] for at in range(0, value.shape[1], HD)], axis=0
    )


def unstack_heads(value, rows):
    return jnp.concatenate(
        [value[at : at + rows] for at in range(0, value.shape[0], rows)], axis=1
    )


def attend_kernel(fine, q_ref, own_ref, halo_ref, pos_ref, probs_ref, out_ref):
    rows, q_cols = q_ref.shape[1:]
    heads = q_cols // HD
    count = out_ref.shape[0]
    kv = jnp.concatenate([halo_ref[0], own_ref[0]], axis=0)
    keys, values = kv[:, :HD], kv[:, HD:]
    span = kv.shape[0]
    scores = cols_cols(stack_heads(q_ref[0]), keys) * (HD**-0.5)
    query = lax.broadcasted_iota(jnp.int32, (rows, span), 0) + HALO
    key = lax.broadcasted_iota(jnp.int32, (rows, span), 1)
    first = query - pos_ref[0][:, :1].astype(jnp.int32)
    allowed = (key >= first) & (key <= query)
    scores = jnp.where(allowed[None], scores.reshape(heads, rows, span), NEG_FILL)
    grown = jnp.exp(scores - jnp.max(scores, axis=-1, keepdims=True))
    probs = grown / jnp.sum(grown, axis=-1, keepdims=True)
    probs_ref[0] = probs
    mixed = rows_cols(probs.reshape(heads * rows, span).astype(BF), values)
    mixed = unstack_heads(mixed, rows).astype(BF)
    for to in range(count):
        out_ref[to, 0] = jnp.concatenate(
            [
                mixed[:, at + to * fine : at + (to + 1) * fine]
                for at in range(0, q_cols, count * fine)
            ],
            axis=1,
        )


def attend_back_kernel(
    fine, grad_ref, probs_ref, q_ref, own_ref, halo_ref, cos_ref, sin_ref, q_out, kv_out
):
    rows, q_cols = q_ref.shape[1:]
    heads = q_cols // HD
    count = grad_ref.shape[0]
    kv = jnp.concatenate([halo_ref[0], own_ref[0]], axis=0)
    keys, values = kv[:, :HD], kv[:, HD:]
    span = kv.shape[0]
    grad = jnp.concatenate(
        [
            grad_ref[source, 0][:, at * fine : (at + 1) * fine]
            for at in range(q_cols // (count * fine))
            for source in range(count)
        ],
        axis=1,
    )
    grad = stack_heads(grad)
    probs = probs_ref[0].reshape(heads * rows, span)
    probs_grad = cols_cols(grad, values)
    inner = jnp.sum(probs * probs_grad, axis=-1, keepdims=True)
    score_grad = (probs * (probs_grad - inner)).astype(BF)
    scale = HD**-0.5
    key_grad = rows_rows(score_grad, stack_heads(q_ref[0])) * scale
    value_grad = rows_rows(probs.astype(BF), grad)
    kv_out[0] = jnp.concatenate([key_grad, value_grad], axis=1)
    query_grad = unstack_heads(rows_cols(score_grad, keys) * scale, rows)
    cosine, sine = cos_ref[0], -sin_ref[0]
    for at in range(0, q_cols, LANES):
        q_out[0, :, at : at + LANES] = turn(
            query_grad[:, at : at + LANES], cosine, sine
        ).astype(BF)


def in_back_kernel(
    dq_ref, dkv_ref, back_ref, cos_ref, sin_ref, normed_ref, x_ref, two_ref, w_ref,
    part_ref, grad_ref, total_ref,
):
    at = pl.program_id(0)
    rows = dq_ref.shape[1]
    own = dkv_ref[0, HALO:]
    tail = own[rows - HALO :] + back_ref[0]
    own = jnp.concatenate([own[: rows - HALO], tail], axis=0)
    own = turn_first(own, cos_ref[0], -sin_ref[0]).astype(BF)
    qkv_grad = jnp.concatenate([dq_ref[0], own], axis=1)
    normed_grad = cols_cols(qkv_grad, w_ref[...])
    part_ref[0] = normed_grad.astype(BF)
    x = x_ref[0].astype(F32)
    one = (normed_grad * x * norm_scale(x)).astype(BF)
    cols = qkv_grad.shape[1]
    lane = lax.broadcasted_iota(jnp.int32, (rows, LANES), 1)

    @pl.when(at == 0)
    def _():
        total_ref[:, :cols] = rows_rows(normed_ref[0], qkv_grad)
        total_ref[:, cols:] = rows_rows(one, (lane < HD).astype(BF)) + rows_rows(
            two_ref[...], (lane >= HD).astype(BF)
        )

    @pl.when(at > 0)
    def _():
        total_ref[:, :cols] += rows_rows(normed_ref[0], qkv_grad)
        total_ref[:, cols:] += rows_rows(one, (lane < HD).astype(BF))

    @pl.when(at == pl.num_programs(0) - 1)
    def _():
        grad_ref[...] = total_ref[...].astype(BF)


def middle_kernel(part_ref, x_ref, gain_ref, mid_ref, normed_ref):
    mid = x_ref[...].astype(F32)
    for at in range(part_ref.shape[0]):
        mid += part_ref[at].astype(F32)
    mid_ref[...] = mid
    normed_ref[...] = (mid * norm_scale(mid) * gain_ref[...]).astype(BF)


def middle_back_kernel(grad_ref, mid_ref, gain_ref, cot_ref, out_ref, low_ref, gain_out_ref):
    mid = mid_ref[...]
    scale = norm_scale(mid)
    grad = grad_ref[...].astype(F32)
    gain_out_ref[...] = (grad * mid * scale).astype(BF)
    scaled = grad * gain_ref[...]
    out = (
        cot_ref[...].astype(F32)
        + scale * scaled
        - mid * scale**3 * jnp.mean(scaled * mid, axis=1, keepdims=True)
    )
    out_ref[...] = out
    low_ref[...] = out.astype(BF)


def last_kernel(part_ref, x_ref, gain_ref, mid_ref, out_ref):
    x = x_ref[...].astype(F32)
    scale = norm_scale(x)
    grad = part_ref[0].astype(F32)
    for at in range(1, part_ref.shape[0]):
        grad += part_ref[at].astype(F32)
    scaled = grad * gain_ref[...]
    out = (
        mid_ref[...]
        + scale * scaled
        - x * scale**3 * jnp.mean(scaled * x, axis=1, keepdims=True)
    )
    out_ref[...] = out.astype(BF)


def forward_back_kernel(
    x_ref, cot_ref, pair_ref, down_ref, mixed_ref, gate_out, up_out, part_ref
):
    x = x_ref[...]
    gate = rows_cols(x, pair_ref[0])
    up = rows_cols(x, pair_ref[1])
    mixed_grad = cols_cols(cot_ref[...], down_ref[...])
    sigma = jax.nn.sigmoid(gate)
    silu = gate * sigma
    mixed_ref[...] = (silu * up).astype(BF)
    gate_grad = (mixed_grad * up * sigma * (1.0 + gate * (1.0 - sigma))).astype(BF)
    up_grad = (mixed_grad * silu).astype(BF)
    gate_out[...] = gate_grad
    up_out[...] = up_grad
    part_ref[...] = (
        cols_cols(gate_grad, pair_ref[0]) + cols_cols(up_grad, pair_ref[1])
    ).astype(BF)


def shape(dims, kind):
    return jax.ShapeDtypeStruct(dims, kind)


def call(kernel, out_shape, grid=None, in_specs=None, out_specs=None, scratch=()):
    options = {}
    if grid is not None:
        options = {"grid": grid, "in_specs": in_specs, "out_specs": out_specs}
    return pl.pallas_call(
        kernel,
        out_shape=out_shape,
        scratch_shapes=list(scratch),
        compiler_params=pltpu.CompilerParams(vmem_limit_bytes=56 * 1024 * 1024),
        **options,
    )


def by_block(dims):
    return pl.BlockSpec((1,) + dims, lambda g: (g,) + (0,) * len(dims))


def whole(dims):
    return pl.BlockSpec(dims, lambda g: (0,) * len(dims), pipeline_mode=pl.Buffered(1))


def body(
    n_rep,
    n_shard,
    tokens,
    seq_lengths,
    deal_order,
    attn_gain,
    mlp_gain,
    q_weight,
    k_weight,
    v_weight,
    o_weight,
    gate_weight,
    up_weight,
    down_weight,
    cotangent,
):
    rows, width = tokens.shape
    r = lax.axis_index("rep")
    s = lax.axis_index("shard")
    own = width // n_shard
    fine = own // n_rep
    hidden = down_weight.shape[0]
    q_cols = width // n_rep
    heads = H // n_rep
    pair = n_shard // n_rep
    share = max(n_rep // KVH, 1)
    kv_at = (r * KVH) // n_rep
    all_rows = n_rep * rows
    span = HALO + rows
    qkv_cols = q_cols + 2 * HD

    starts = jnp.cumsum(seq_lengths[0]) - seq_lengths[0]
    places = s * rows + jnp.arange(rows, dtype=jnp.int32)
    first = jnp.max(
        jnp.where(starts[None, :] <= places[:, None], starts[None, :], 0), axis=1, keepdims=True
    )
    offset = jnp.broadcast_to((places[:, None] - first).astype(BF), (rows, LANES))

    w_qkv_own = jnp.concatenate(
        [
            lax.dynamic_slice_in_dim(q_weight, r * q_cols, q_cols, 1),
            lax.dynamic_slice_in_dim(k_weight, kv_at * HD, HD, 1),
            lax.dynamic_slice_in_dim(v_weight, kv_at * HD, HD, 1),
        ],
        axis=1,
    )
    w_qkv = lax.all_gather(w_qkv_own, "shard", axis=0, tiled=True)
    w_o = lax.all_gather(
        lax.dynamic_slice_in_dim(o_weight, r * fine, fine, 0), "shard", axis=0, tiled=True
    )
    x_all = spread(jnp.concatenate([tokens, offset], axis=1), "rep", n_rep)
    gains = lax.all_gather(jnp.stack([attn_gain, mlp_gain]), "shard", axis=1, tiled=True)
    gain_one = gains[0:1].astype(F32)
    gain_two = gains[1:2].astype(F32)

    def exchange_shard(pieces):
        rest = [send(pieces[k], "shard", n_shard, k) for k in range(1, n_shard)]
        return [pieces[0]] + rest

    block = (n_shard, fine, hidden)
    ids = jnp.stack([r, s]).astype(jnp.int32)
    gate_tied, up_tied, _ = lax.optimization_barrier((gate_weight, up_weight, gains))
    w_pair = split_pair(ids, gate_tied, up_tied, fine, n_shard)
    w_pair = exchange_shard(w_pair)
    w_pair = flat_call(order_kernel, ids, (shape(block, BF),) * 2, w_pair)
    w_pair = gather_rep(w_pair, n_rep)
    w_pair = flat_call(
        join_kernel,
        ids,
        shape((2, n_shard, n_rep, fine, hidden), BF),
        [half for piece in w_pair for half in piece],
    ).reshape(2, width, hidden)
    cot_all = lax.all_gather(cotangent, "shard", axis=0, tiled=True)

    half = HD // 2
    inverse = ROPE_BASE ** (-2.0 * (jnp.arange(LANES) % half).astype(F32) / HD)
    angles = x_all[:, :, width:].astype(F32) * inverse[None, None, :]
    cosine, sine = jnp.cos(angles), jnp.sin(angles)
    x_block = by_block((rows, width))
    table = by_block((rows, LANES))
    normed_one, queries, kv_own = call(
        in_kernel,
        (
            shape((n_rep, rows, width), BF),
            shape((n_rep, rows, q_cols), BF),
            shape((n_rep, rows, LANES), BF),
        ),
        (n_rep,),
        [x_block, whole((1, width)), whole((width, qkv_cols)), table, table],
        (x_block, by_block((rows, q_cols)), table),
    )(x_all, gain_one, w_qkv, cosine, sine)
    kv_halo = lax.ppermute(
        kv_own[:, rows - HALO :], "shard", [(i, i + 1) for i in range(n_shard - 1)]
    )
    head_block = pl.BlockSpec((n_rep, 1, rows, pair * fine), lambda g: (0, g, 0, 0))
    probs_block = by_block((heads, rows, span))
    probs, out_in = call(
        partial(attend_kernel, fine),
        (
            shape((n_rep, heads, rows, span), F32),
            shape((n_rep, n_rep, rows, pair * fine), BF),
        ),
        (n_rep,),
        [
            by_block((rows, q_cols)),
            table,
            by_block((HALO, LANES)),
            pl.BlockSpec((1, rows, LANES), lambda g: (g, 0, width // LANES)),
        ],
        (probs_block, head_block),
    )(queries, kv_own, kv_halo, x_all)
    out_in = swap(out_in, "rep").reshape(n_rep, all_rows, pair * fine)
    out_in = out_in.transpose(1, 0, 2).reshape(all_rows, q_cols)
    mid_part = rows_cols(out_in, w_o).astype(BF).reshape(n_rep, rows, width)
    x_mid, normed_two = call(
        middle_kernel, (shape((rows, width), F32), shape((rows, width), BF))
    )(swap(mid_part, "rep"), tokens, gain_two)

    two_all = lax.all_gather(normed_two, "shard", axis=0, tiled=True)
    step = 256
    group = two_all.shape[0]
    token_block = pl.BlockSpec((step, width), lambda g: (g, 0))
    hidden_block = pl.BlockSpec((step, hidden), lambda g: (g, 0))
    mixed, gate_grad, up_grad, two_grad_part = call(
        forward_back_kernel,
        (shape((group, hidden), BF),) * 3 + (shape((group, width), BF),),
        (group // step,),
        [token_block, token_block, whole((2, width, hidden)), whole((hidden, width))],
        (hidden_block,) * 3 + (token_block,),
    )(two_all, cot_all, w_pair, down_weight)
    two_grad = lax.psum_scatter(two_grad_part, "shard", scatter_dimension=0, tiled=True)
    mixed, two_grad_part = lax.optimization_barrier((mixed, two_grad_part))
    down_part = rows_cols(mixed, down_weight).astype(BF)
    down_rows = lax.psum_scatter(down_part, "shard", scatter_dimension=0, tiled=True)
    layer_out = (x_mid + down_rows.astype(F32)).astype(BF)

    mid_grad, branch, gain_two_rows = call(
        middle_back_kernel,
        (shape((rows, width), F32), shape((rows, width), BF), shape((rows, width), BF)),
    )(two_grad, x_mid, gain_two, cotangent)

    part_rows = hidden // n_rep
    cut = (part_rows // 2 + 15) // 16 * 16
    w_down_grad = rows_rows(mixed, cot_all).astype(BF)
    chunks = []
    for k in range(n_rep):
        at = (r ^ k) * part_rows
        chunks.append(
            (
                lax.dynamic_slice_in_dim(w_down_grad, at, cut, 0),
                lax.dynamic_slice_in_dim(w_down_grad, at + cut, part_rows - cut, 0),
            )
        )
    w_down_grad = parts_rep(chunks, n_rep)
    w_down_grad = tuple(
        sum(part.astype(F32) for part in parts).astype(BF) for parts in w_down_grad
    )
    down_out = place(gather_rep(w_down_grad, n_rep), r)
    halves = [
        rows_rows(two_all, part).astype(BF).reshape(n_shard, n_rep, fine, hidden)
        for part in (gate_grad, up_grad)
    ]
    chunks = [
        tuple(lax.dynamic_index_in_dim(half, r ^ k, 1, False) for half in halves)
        for k in range(n_rep)
    ]
    w_pair_grad = parts_rep(chunks, n_rep)
    w_pair_grad = flat_call(
        sum_kernel,
        ids,
        (shape((2, fine, hidden), BF),) * n_shard,
        w_pair_grad[0] + w_pair_grad[1],
    )
    w_pair_grad = exchange_shard(w_pair_grad)
    w_pair_grad = flat_call(
        widen_kernel,
        ids,
        (shape((fine, n_shard * hidden), BF),) * 2,
        w_pair_grad,
        [pltpu.VMEM((n_shard, 2, fine, hidden), BF)],
    )
    w_pair_grad = gather_rep(w_pair_grad, n_rep)
    gate_out = place([piece[:1] for piece in w_pair_grad], r)
    up_out = place([piece[1:] for piece in w_pair_grad], r)

    branch_all = spread(branch, "rep", n_rep).reshape(all_rows, width)
    in_grad = cols_cols(branch_all, w_o).astype(BF)
    branch_all, in_grad = lax.optimization_barrier((branch_all, in_grad))
    in_grad = in_grad.reshape(all_rows, n_rep, pair * fine).transpose(1, 0, 2)
    in_grad = swap(in_grad, "rep").reshape(n_rep, n_rep, rows, pair * fine)
    w_o_grad = rows_rows(out_in, branch_all).astype(BF)
    w_o_grad = lax.psum_scatter(w_o_grad, "shard", scatter_dimension=0, tiled=True)
    w_o_grad = (w_o_grad[: fine // 2], w_o_grad[fine // 2 :])
    o_out = place(gather_rep(w_o_grad, n_rep), r)
    query_grad, kv_grad = call(
        partial(attend_back_kernel, fine),
        (shape((n_rep, rows, q_cols), BF), shape((n_rep, span, LANES), F32)),
        (n_rep,),
        [
            head_block,
            probs_block,
            by_block((rows, q_cols)),
            table,
            by_block((HALO, LANES)),
            table,
            table,
        ],
        (by_block((rows, q_cols)), by_block((span, LANES))),
    )(in_grad, probs, queries, kv_own, kv_halo, cosine, sine)
    kv_back = lax.ppermute(
        kv_grad[:, :HALO], "shard", [(i + 1, i) for i in range(n_shard - 1)]
    )
    grad_cols = qkv_cols + LANES
    one_grad_part, w_qkv_grad = call(
        in_back_kernel,
        (shape((n_rep, rows, width), BF), shape((width, grad_cols), BF)),
        (n_rep,),
        [
            by_block((rows, q_cols)),
            by_block((span, LANES)),
            by_block((HALO, LANES)),
            table,
            table,
            x_block,
            x_block,
            whole((rows, width)),
            whole((width, qkv_cols)),
        ],
        (x_block, pl.BlockSpec((width, grad_cols), lambda g: (0, 0))),
        [pltpu.VMEM((width, grad_cols), F32)],
    )(
        query_grad, kv_grad, kv_back, cosine, sine, normed_one, x_all, gain_two_rows, w_qkv
    )
    w_qkv_grad = lax.psum_scatter(w_qkv_grad, "shard", scatter_dimension=0, tiled=True)
    input_grad = call(last_kernel, shape((rows, width), BF))(
        swap(one_grad_part, "rep"), tokens, gain_one, mid_grad
    )
    w_qkv_grad = spread(w_qkv_grad, "rep", n_rep).astype(F32)

    def columns(part):
        return part.transpose(1, 0, 2).reshape(own, -1)

    def kv_columns(part):
        return columns(jnp.sum(part.reshape(-1, share, own, HD), axis=1))

    q_out = columns(w_qkv_grad[..., :q_cols])
    k_out = kv_columns(w_qkv_grad[..., q_cols : q_cols + HD])
    v_out = kv_columns(w_qkv_grad[..., q_cols + HD : qkv_cols])
    gain_sums = jnp.sum(w_qkv_grad[..., qkv_cols:], axis=0)
    return (
        layer_out,
        input_grad,
        gain_sums[:, 0],
        gain_sums[:, HD],
        q_out,
        k_out,
        v_out,
        o_out,
        gate_out,
        up_out,
        down_out,
    )


def solution(mesh):
    split = P("shard", None)
    by_token = P(("rep", "shard"), None)
    return jax.shard_map(
        partial(body, mesh.shape["rep"], mesh.shape["shard"]),
        mesh=mesh,
        in_specs=(by_token, P("rep", None), P("rep", None), P("shard"), P("shard"))
        + (split,) * 7
        + (by_token,),
        out_specs=(by_token, by_token, P("shard"), P("shard")) + (split,) * 7,
        check_vma=False,
    )
```

```python
from functools import partial

import jax
import jax.numpy as jnp
from jax import lax
from jax.experimental import pallas as pl
from jax.experimental.pallas import tpu as pltpu
from jax.sharding import PartitionSpec as P


H = 32
KVH = 4
HD = 64
HALO = 64
LANES = 128

EPSILON = 1e-05
ROPE_BASE = 10000.0
NEG_FILL = -1e30

BF = jnp.bfloat16
F32 = jnp.float32


def dot(left, right, contract):
    return lax.dot_general(left, right, (contract, ((), ())), preferred_element_type=F32)


def rows_cols(left, right):
    return dot(left, right, ((1,), (0,)))


def rows_rows(left, right):
    return dot(left, right, ((0,), (0,)))


def cols_cols(left, right):
    return dot(left, right, ((1,), (1,)))


def spread(value, axis, count):
    wide = jnp.broadcast_to(value[None], (count,) + value.shape)
    return lax.all_to_all(wide, axis, split_axis=0, concat_axis=0, tiled=True)


def swap(value, axis):
    return lax.all_to_all(value, axis, split_axis=0, concat_axis=0, tiled=True)


def pairs(count, step):
    return [(i, i ^ step) for i in range(count)]


def send(value, axis, count, step):
    return lax.ppermute(value, axis, pairs(count, step))


def parts_rep(chunks, count):
    go = lambda value, step: send(value, "rep", count, step)
    if count != 4:
        return [
            [chunks[0][h]] + [go(chunks[k][h], k) for k in range(1, count)]
            for h in range(2)
        ]
    add = lambda left, right: (left.astype(F32) + right.astype(F32)).astype(BF)
    first_one = go(chunks[1][0], 1)
    first_two = go(chunks[3][0], 1)
    second_one = go(chunks[2][1], 2)
    second_two = go(chunks[3][1], 2)
    last_one = go(add(chunks[2][0], first_two), 2)
    last_two = go(add(chunks[1][1], second_two), 1)
    return [[chunks[0][0], first_one, last_one], [chunks[0][1], second_one, last_two]]


def gather_rep(halves, count):
    go = lambda value, step: send(value, "rep", count, step)
    if count != 4:
        return [halves] + [tuple(go(v, k) for v in halves) for k in range(1, count)]
    one = tuple(go(v, 1) for v in halves)
    two = tuple(go(v, 2) for v in halves)
    return [halves, one, two, (go(one[0], 2), go(two[1], 1))]


def place_kernel(count, me_ref, *refs):
    parts, out_ref = refs[:-1], refs[-1]
    at = pl.program_id(0)
    size = len(parts) // count
    for k in range(count):

        @pl.when(at == jnp.bitwise_xor(me_ref[0], k))
        def _(k=k):
            row = 0
            for part in parts[k * size : (k + 1) * size]:
                out_ref[0, row : row + part.shape[0]] = part[...].astype(F32)
                row += part.shape[0]


def place(pieces, me):
    count = len(pieces)
    flat = [part for piece in pieces for part in piece]
    rows = sum(part.shape[0] for part in pieces[0])
    width = flat[0].shape[1]
    grid = pltpu.PrefetchScalarGridSpec(
        num_scalar_prefetch=1,
        grid=(count,),
        in_specs=[
            pl.BlockSpec(part.shape, lambda g, me: (0, 0), pipeline_mode=pl.Buffered(1))
            for part in flat
        ],
        out_specs=pl.BlockSpec((1, rows, width), lambda g, me: (g, 0, 0)),
    )
    return pl.pallas_call(
        partial(place_kernel, count),
        out_shape=shape((count, rows, width), F32),
        grid_spec=grid,
        compiler_params=pltpu.CompilerParams(vmem_limit_bytes=56 * 1024 * 1024),
    )(me.astype(jnp.int32).reshape(1), *flat).reshape(count * rows, width)


def split_kernel(id_ref, gate_ref, up_ref, *refs):
    outs, both = refs[:-1], refs[-1]
    hidden = both.shape[3]
    for h, ref in enumerate((gate_ref, up_ref)):
        value = ref[...]
        for at in range(len(outs)):
            both[at, h] = value[:, at * hidden : (at + 1) * hidden]
    for k, out in enumerate(outs):
        out[...] = both[jnp.bitwise_xor(id_ref[1], k)]


def split_pair(ids, gate, up, fine, count):
    hidden = gate.shape[1] // count
    rows = pl.BlockSpec((fine, gate.shape[1]), lambda g, ids: (ids[0], 0))
    piece = (2, fine, hidden)
    return pl.pallas_call(
        split_kernel,
        out_shape=(shape(piece, BF),) * count,
        grid_spec=pltpu.PrefetchScalarGridSpec(
            num_scalar_prefetch=1,
            grid=(1,),
            in_specs=[rows, rows],
            out_specs=(pl.BlockSpec(piece, lambda g, ids: (0, 0, 0)),) * count,
            scratch_shapes=[pltpu.VMEM((count,) + piece, BF)],
        ),
        name="split_pair",
    )(ids, gate, up)


def flat_call(kernel, ids, out_shape, values, scratch=()):
    specs = [pl.BlockSpec(memory_space=pltpu.SMEM)]
    specs += [pl.BlockSpec(memory_space=pltpu.VMEM)] * len(values)
    return pl.pallas_call(
        kernel,
        out_shape=out_shape,
        in_specs=specs,
        scratch_shapes=list(scratch),
        compiler_params=pltpu.CompilerParams(vmem_limit_bytes=56 * 1024 * 1024),
    )(ids, *values)


def order_kernel(id_ref, *refs):
    pieces, (gate_ref, up_ref) = refs[:-2], refs[-2:]
    for k, piece in enumerate(pieces):
        at = jnp.bitwise_xor(id_ref[1], k)
        gate_ref[at] = piece[0]
        up_ref[at] = piece[1]


def join_kernel(id_ref, *refs):
    out_ref = refs[-1]
    for k in range(len(refs) // 2):
        at = jnp.bitwise_xor(id_ref[0], k)
        for h in range(2):
            value = refs[2 * k + h]
            for row in range(value.shape[0]):
                out_ref[h, row, at] = value[row]


def sum_kernel(id_ref, *refs):
    count = refs[0].shape[0]
    outs = refs[len(refs) - count :]
    parts = refs[: len(refs) - count]
    half = len(parts) // 2
    for k, out in enumerate(outs):
        at = jnp.bitwise_xor(id_ref[1], k)
        for h in range(2):
            total = parts[h * half][at].astype(F32)
            for part in parts[h * half + 1 : (h + 1) * half]:
                total += part[at].astype(F32)
            out[h] = total.astype(BF)


def widen_kernel(id_ref, *refs):
    pieces, (gate_ref, up_ref, both) = refs[:-3], refs[-3:]
    hidden = both.shape[3]
    for k, piece in enumerate(pieces):
        both[jnp.bitwise_xor(id_ref[1], k)] = piece[...]
    for h, ref in enumerate((gate_ref, up_ref)):
        for at in range(len(pieces)):
            ref[:, at * hidden : (at + 1) * hidden] = both[at, h]


def qkv_kernel(share, id_ref, *refs):
    pieces = refs[:-6]
    q_ref, k_ref, v_ref, gain_ref, k_all, v_all = refs[-6:]
    count = k_all.shape[0]
    q_cols = q_ref.shape[1] // count
    row = 0
    for h in range(2):
        rows = slice(row, row + pieces[h].shape[0])
        total = 0.0
        for k in range(count):
            at = jnp.bitwise_xor(id_ref[0], k)
            value = pieces[2 * k + h][...].astype(F32)
            q_ref[rows, pl.ds(pl.multiple_of(at * q_cols, LANES), q_cols)] = value[:, :q_cols]
            k_all[at, rows] = value[:, q_cols : q_cols + HD]
            v_all[at, rows] = value[:, q_cols + HD : q_cols + 2 * HD]
            total += value[:, q_cols + 2 * HD :]
        gain_ref[rows] = total
        row = rows.stop
    for ref, both in ((k_ref, k_all), (v_ref, v_all)):
        for head in range(count // share):
            total = both[head * share]
            for other in range(head * share + 1, (head + 1) * share):
                total += both[other]
            ref[:, head * HD : (head + 1) * HD] = total


def pair_grad_kernel(fine, id_ref, x_ref, grad_ref, *refs):
    outs, total_ref = refs[:-1], refs[-1]
    total_ref[...] = rows_rows(x_ref[...], grad_ref[...])
    own = fine * len(outs)
    for k, out in enumerate(outs):
        row = jnp.bitwise_xor(id_ref[0], k) * fine
        for block in range(out.shape[0]):
            at = pl.multiple_of(block * own + row, fine)
            out[block] = total_ref[pl.ds(at, fine)].astype(BF)


def pair_grad(ids, x, grad, fine, count, blocks):
    width, hidden = x.shape[1], grad.shape[1]
    tile = 2 * fine * count
    out = (2, fine, hidden)
    return pl.pallas_call(
        partial(pair_grad_kernel, fine),
        out_shape=(shape((blocks, fine, hidden), BF),) * count,
        grid_spec=pltpu.PrefetchScalarGridSpec(
            num_scalar_prefetch=1,
            grid=(width // tile,),
            in_specs=[
                pl.BlockSpec((x.shape[0], tile), lambda g, ids: (0, g)),
                pl.BlockSpec(grad.shape, lambda g, ids: (0, 0), pipeline_mode=pl.Buffered(1)),
            ],
            out_specs=(pl.BlockSpec(out, lambda g, ids: (g, 0, 0)),) * count,
            scratch_shapes=[pltpu.VMEM((tile, hidden), F32)],
        ),
        compiler_params=pltpu.CompilerParams(vmem_limit_bytes=56 * 1024 * 1024),
    )(ids, x, grad)


def norm_scale(value):
    return lax.rsqrt(jnp.mean(value * value, axis=1, keepdims=True) + EPSILON)


def turn(tile, cosine, sine):
    lane = lax.broadcasted_iota(jnp.int32, tile.shape, 1)
    swapped = jnp.where(
        lane % HD < HD // 2,
        -pltpu.roll(tile, LANES - HD // 2, 1),
        pltpu.roll(tile, HD // 2, 1),
    )
    return tile * cosine + swapped * sine


def turn_first(tile, cosine, sine):
    lane = lax.broadcasted_iota(jnp.int32, tile.shape, 1)
    return jnp.where(lane < HD, turn(tile, cosine, sine), tile)


def in_kernel(x_ref, gain_ref, w_ref, cos_ref, sin_ref, normed_ref, q_ref, kv_ref):
    x = x_ref[0].astype(F32)
    normed = (x * norm_scale(x) * gain_ref[...]).astype(BF)
    normed_ref[0] = normed
    qkv = rows_cols(normed, w_ref[...])
    cosine, sine = cos_ref[0], sin_ref[0]
    q_cols = q_ref.shape[2]
    for at in range(0, q_cols, LANES):
        q_ref[0, :, at : at + LANES] = turn(qkv[:, at : at + LANES], cosine, sine).astype(BF)
    kv_ref[0] = turn_first(qkv[:, q_cols:], cosine, sine).astype(BF)


def stack_heads(value):
    return jnp.concatenate(
        [value[:, at : at + HD] for at in range(0, value.shape[1], HD)], axis=0
    )


def unstack_heads(value, rows):
    return jnp.concatenate(
        [value[at : at + rows] for at in range(0, value.shape[0], rows)], axis=1
    )


def attend_kernel(fine, q_ref, own_ref, halo_ref, pos_ref, probs_ref, out_ref):
    rows, q_cols = q_ref.shape[1:]
    heads = q_cols // HD
    count = out_ref.shape[0]
    kv = jnp.concatenate([halo_ref[0], own_ref[0]], axis=0)
    keys, values = kv[:, :HD], kv[:, HD:]
    span = kv.shape[0]
    scores = cols_cols(stack_heads(q_ref[0]), keys) * (HD**-0.5)
    query = lax.broadcasted_iota(jnp.int32, (rows, span), 0) + HALO
    key = lax.broadcasted_iota(jnp.int32, (rows, span), 1)
    first = query - pos_ref[0][:, :1].astype(jnp.int32)
    allowed = (key >= first) & (key <= query)
    scores = jnp.where(allowed[None], scores.reshape(heads, rows, span), NEG_FILL)
    grown = jnp.exp(scores - jnp.max(scores, axis=-1, keepdims=True))
    probs = grown / jnp.sum(grown, axis=-1, keepdims=True)
    probs_ref[0] = probs
    mixed = rows_cols(probs.reshape(heads * rows, span).astype(BF), values)
    mixed = unstack_heads(mixed, rows).astype(BF)
    for to in range(count):
        out_ref[to, 0] = jnp.concatenate(
            [
                mixed[:, at + to * fine : at + (to + 1) * fine]
                for at in range(0, q_cols, count * fine)
            ],
            axis=1,
        )


def attend_back_kernel(
    fine, grad_ref, probs_ref, q_ref, own_ref, halo_ref, cos_ref, sin_ref, q_out, kv_out
):
    rows, q_cols = q_ref.shape[1:]
    heads = q_cols // HD
    count = grad_ref.shape[0]
    kv = jnp.concatenate([halo_ref[0], own_ref[0]], axis=0)
    keys, values = kv[:, :HD], kv[:, HD:]
    span = kv.shape[0]
    grad = jnp.concatenate(
        [
            grad_ref[source, 0][:, at * fine : (at + 1) * fine]
            for at in range(q_cols // (count * fine))
            for source in range(count)
        ],
        axis=1,
    )
    grad = stack_heads(grad)
    probs = probs_ref[0].reshape(heads * rows, span)
    probs_grad = cols_cols(grad, values)
    inner = jnp.sum(probs * probs_grad, axis=-1, keepdims=True)
    score_grad = (probs * (probs_grad - inner)).astype(BF)
    scale = HD**-0.5
    key_grad = rows_rows(score_grad, stack_heads(q_ref[0])) * scale
    value_grad = rows_rows(probs.astype(BF), grad)
    kv_out[0] = jnp.concatenate([key_grad, value_grad], axis=1)
    query_grad = unstack_heads(rows_cols(score_grad, keys) * scale, rows)
    cosine, sine = cos_ref[0], -sin_ref[0]
    for at in range(0, q_cols, LANES):
        q_out[0, :, at : at + LANES] = turn(
            query_grad[:, at : at + LANES], cosine, sine
        ).astype(BF)


def in_back_kernel(
    dq_ref, dkv_ref, back_ref, cos_ref, sin_ref, normed_ref, x_ref, two_ref, w_ref,
    part_ref, grad_ref, total_ref,
):
    at = pl.program_id(0)
    rows = dq_ref.shape[1]
    own = dkv_ref[0, HALO:]
    tail = own[rows - HALO :] + back_ref[0]
    own = jnp.concatenate([own[: rows - HALO], tail], axis=0)
    own = turn_first(own, cos_ref[0], -sin_ref[0]).astype(BF)
    qkv_grad = jnp.concatenate([dq_ref[0], own], axis=1)
    normed_grad = cols_cols(qkv_grad, w_ref[...])
    part_ref[0] = normed_grad.astype(BF)
    x = x_ref[0].astype(F32)
    one = (normed_grad * x * norm_scale(x)).astype(BF)
    cols = qkv_grad.shape[1]
    lane = lax.broadcasted_iota(jnp.int32, (rows, LANES), 1)

    @pl.when(at == 0)
    def _():
        total_ref[:, :cols] = rows_rows(normed_ref[0], qkv_grad)
        total_ref[:, cols:] = rows_rows(one, (lane < HD).astype(BF)) + rows_rows(
            two_ref[...], (lane >= HD).astype(BF)
        )

    @pl.when(at > 0)
    def _():
        total_ref[:, :cols] += rows_rows(normed_ref[0], qkv_grad)
        total_ref[:, cols:] += rows_rows(one, (lane < HD).astype(BF))

    @pl.when(at == pl.num_programs(0) - 1)
    def _():
        grad_ref[...] = total_ref[...].astype(BF)


def middle_kernel(part_ref, x_ref, gain_ref, mid_ref, normed_ref):
    mid = x_ref[...].astype(F32)
    for at in range(part_ref.shape[0]):
        mid += part_ref[at].astype(F32)
    mid_ref[...] = mid
    normed_ref[...] = (mid * norm_scale(mid) * gain_ref[...]).astype(BF)


def middle_back_kernel(grad_ref, mid_ref, gain_ref, cot_ref, out_ref, low_ref, gain_out_ref):
    mid = mid_ref[...]
    scale = norm_scale(mid)
    grad = grad_ref[...].astype(F32)
    gain_out_ref[...] = (grad * mid * scale).astype(BF)
    scaled = grad * gain_ref[...]
    out = (
        cot_ref[...].astype(F32)
        + scale * scaled
        - mid * scale**3 * jnp.mean(scaled * mid, axis=1, keepdims=True)
    )
    out_ref[...] = out
    low_ref[...] = out.astype(BF)


def last_kernel(part_ref, x_ref, gain_ref, mid_ref, out_ref):
    x = x_ref[...].astype(F32)
    scale = norm_scale(x)
    grad = part_ref[0].astype(F32)
    for at in range(1, part_ref.shape[0]):
        grad += part_ref[at].astype(F32)
    scaled = grad * gain_ref[...]
    out = (
        mid_ref[...]
        + scale * scaled
        - x * scale**3 * jnp.mean(scaled * x, axis=1, keepdims=True)
    )
    out_ref[...] = out.astype(BF)


def forward_back_kernel(
    x_ref, cot_ref, pair_ref, down_ref, mixed_ref, gate_out, up_out, part_ref
):
    x = x_ref[...]
    gate = rows_cols(x, pair_ref[0])
    up = rows_cols(x, pair_ref[1])
    mixed_grad = cols_cols(cot_ref[...], down_ref[...])
    sigma = jax.nn.sigmoid(gate)
    silu = gate * sigma
    mixed_ref[...] = (silu * up).astype(BF)
    gate_grad = (mixed_grad * up * sigma * (1.0 + gate * (1.0 - sigma))).astype(BF)
    up_grad = (mixed_grad * silu).astype(BF)
    gate_out[...] = gate_grad
    up_out[...] = up_grad
    part_ref[...] = (
        cols_cols(gate_grad, pair_ref[0]) + cols_cols(up_grad, pair_ref[1])
    ).astype(BF)


def shape(dims, kind):
    return jax.ShapeDtypeStruct(dims, kind)


def call(kernel, out_shape, grid=None, in_specs=None, out_specs=None, scratch=()):
    options = {}
    if grid is not None:
        options = {"grid": grid, "in_specs": in_specs, "out_specs": out_specs}
    return pl.pallas_call(
        kernel,
        out_shape=out_shape,
        scratch_shapes=list(scratch),
        compiler_params=pltpu.CompilerParams(vmem_limit_bytes=56 * 1024 * 1024),
        **options,
    )


def by_block(dims):
    return pl.BlockSpec((1,) + dims, lambda g: (g,) + (0,) * len(dims))


def whole(dims):
    return pl.BlockSpec(dims, lambda g: (0,) * len(dims), pipeline_mode=pl.Buffered(1))


def body(
    n_rep,
    n_shard,
    tokens,
    seq_lengths,
    deal_order,
    attn_gain,
    mlp_gain,
    q_weight,
    k_weight,
    v_weight,
    o_weight,
    gate_weight,
    up_weight,
    down_weight,
    cotangent,
):
    rows, width = tokens.shape
    r = lax.axis_index("rep")
    s = lax.axis_index("shard")
    own = width // n_shard
    fine = own // n_rep
    hidden = down_weight.shape[0]
    q_cols = width // n_rep
    heads = H // n_rep
    pair = n_shard // n_rep
    share = max(n_rep // KVH, 1)
    kv_at = (r * KVH) // n_rep
    all_rows = n_rep * rows
    span = HALO + rows
    qkv_cols = q_cols + 2 * HD

    starts = jnp.cumsum(seq_lengths[0]) - seq_lengths[0]
    places = s * rows + jnp.arange(rows, dtype=jnp.int32)
    first = jnp.max(
        jnp.where(starts[None, :] <= places[:, None], starts[None, :], 0), axis=1, keepdims=True
    )
    offset = jnp.broadcast_to((places[:, None] - first).astype(BF), (rows, LANES))

    w_qkv_own = jnp.concatenate(
        [
            lax.dynamic_slice_in_dim(q_weight, r * q_cols, q_cols, 1),
            lax.dynamic_slice_in_dim(k_weight, kv_at * HD, HD, 1),
            lax.dynamic_slice_in_dim(v_weight, kv_at * HD, HD, 1),
        ],
        axis=1,
    )
    w_qkv = lax.all_gather(w_qkv_own, "shard", axis=0, tiled=True)
    w_o = lax.all_gather(
        lax.dynamic_slice_in_dim(o_weight, r * fine, fine, 0), "shard", axis=0, tiled=True
    )
    x_all = spread(jnp.concatenate([tokens, offset], axis=1), "rep", n_rep)
    gains = lax.all_gather(jnp.stack([attn_gain, mlp_gain]), "shard", axis=1, tiled=True)
    gain_one = gains[0:1].astype(F32)
    gain_two = gains[1:2].astype(F32)

    def exchange_shard(pieces):
        rest = [send(pieces[k], "shard", n_shard, k) for k in range(1, n_shard)]
        return [pieces[0]] + rest

    block = (n_shard, fine, hidden)
    ids = jnp.stack([r, s]).astype(jnp.int32)
    gate_tied, up_tied, _ = lax.optimization_barrier((gate_weight, up_weight, gains))
    w_pair = split_pair(ids, gate_tied, up_tied, fine, n_shard)
    w_pair = exchange_shard(w_pair)
    w_pair = flat_call(order_kernel, ids, (shape(block, BF),) * 2, w_pair)
    w_pair = gather_rep(w_pair, n_rep)
    w_pair = flat_call(
        join_kernel,
        ids,
        shape((2, n_shard, n_rep, fine, hidden), BF),
        [half for piece in w_pair for half in piece],
    ).reshape(2, width, hidden)
    cot_all = lax.all_gather(cotangent, "shard", axis=0, tiled=True)

    half = HD // 2
    inverse = ROPE_BASE ** (-2.0 * (jnp.arange(LANES) % half).astype(F32) / HD)
    angles = x_all[:, :, width:].astype(F32) * inverse[None, None, :]
    cosine, sine = jnp.cos(angles), jnp.sin(angles)
    x_block = by_block((rows, width))
    table = by_block((rows, LANES))
    normed_one, queries, kv_own = call(
        in_kernel,
        (
            shape((n_rep, rows, width), BF),
            shape((n_rep, rows, q_cols), BF),
            shape((n_rep, rows, LANES), BF),
        ),
        (n_rep,),
        [x_block, whole((1, width)), whole((width, qkv_cols)), table, table],
        (x_block, by_block((rows, q_cols)), table),
    )(x_all, gain_one, w_qkv, cosine, sine)
    kv_halo = lax.ppermute(
        kv_own[:, rows - HALO :], "shard", [(i, i + 1) for i in range(n_shard - 1)]
    )
    head_block = pl.BlockSpec((n_rep, 1, rows, pair * fine), lambda g: (0, g, 0, 0))
    probs_block = by_block((heads, rows, span))
    probs, out_in = call(
        partial(attend_kernel, fine),
        (
            shape((n_rep, heads, rows, span), F32),
            shape((n_rep, n_rep, rows, pair * fine), BF),
        ),
        (n_rep,),
        [
            by_block((rows, q_cols)),
            table,
            by_block((HALO, LANES)),
            pl.BlockSpec((1, rows, LANES), lambda g: (g, 0, width // LANES)),
        ],
        (probs_block, head_block),
    )(queries, kv_own, kv_halo, x_all)
    out_in = swap(out_in, "rep").reshape(n_rep, all_rows, pair * fine)
    out_in = out_in.transpose(1, 0, 2).reshape(all_rows, q_cols)
    mid_part = rows_cols(out_in, w_o).astype(BF).reshape(n_rep, rows, width)
    x_mid, normed_two = call(
        middle_kernel, (shape((rows, width), F32), shape((rows, width), BF))
    )(swap(mid_part, "rep"), tokens, gain_two)

    two_all = lax.all_gather(normed_two, "shard", axis=0, tiled=True)
    step = 256
    group = two_all.shape[0]
    token_block = pl.BlockSpec((step, width), lambda g: (g, 0))
    hidden_block = pl.BlockSpec((step, hidden), lambda g: (g, 0))
    mixed, gate_grad, up_grad, two_grad_part = call(
        forward_back_kernel,
        (shape((group, hidden), BF),) * 3 + (shape((group, width), BF),),
        (group // step,),
        [token_block, token_block, whole((2, width, hidden)), whole((hidden, width))],
        (hidden_block,) * 3 + (token_block,),
    )(two_all, cot_all, w_pair, down_weight)
    two_grad = lax.psum_scatter(two_grad_part, "shard", scatter_dimension=0, tiled=True)
    mid_grad, branch, gain_two_rows = call(
        middle_back_kernel,
        (shape((rows, width), F32), shape((rows, width), BF), shape((rows, width), BF)),
    )(two_grad, x_mid, gain_two, cotangent)

    gate_chunks = pair_grad(ids, two_all, gate_grad, fine, n_rep, n_shard)
    up_grad, _ = lax.optimization_barrier((up_grad, gate_chunks[0]))
    up_chunks = pair_grad(ids, two_all, up_grad, fine, n_rep, n_shard)
    pair_chunks = list(zip(gate_chunks, up_chunks))
    mixed, _ = lax.optimization_barrier((mixed, up_chunks[0]))
    part_rows = hidden // n_rep
    cut = (part_rows // 2 + 15) // 16 * 16
    w_down_grad = rows_rows(mixed, cot_all).astype(BF)
    mixed, w_down_grad = lax.optimization_barrier((mixed, w_down_grad))
    down_part = rows_cols(mixed, down_weight).astype(BF)
    down_rows = lax.psum_scatter(down_part, "shard", scatter_dimension=0, tiled=True)
    layer_out = (x_mid + down_rows.astype(F32)).astype(BF)
    chunks = []
    for k in range(n_rep):
        at = (r ^ k) * part_rows
        chunks.append(
            (
                lax.dynamic_slice_in_dim(w_down_grad, at, cut, 0),
                lax.dynamic_slice_in_dim(w_down_grad, at + cut, part_rows - cut, 0),
            )
        )
    w_down_grad = parts_rep(chunks, n_rep)
    w_down_grad = tuple(
        sum(part.astype(F32) for part in parts).astype(BF) for parts in w_down_grad
    )
    down_out = place(gather_rep(w_down_grad, n_rep), r)
    w_pair_grad = parts_rep(pair_chunks, n_rep)
    w_pair_grad = flat_call(
        sum_kernel,
        ids,
        (shape((2, fine, hidden), BF),) * n_shard,
        w_pair_grad[0] + w_pair_grad[1],
    )
    w_pair_grad = exchange_shard(w_pair_grad)
    w_pair_grad = flat_call(
        widen_kernel,
        ids,
        (shape((fine, n_shard * hidden), BF),) * 2,
        w_pair_grad,
        [pltpu.VMEM((n_shard, 2, fine, hidden), BF)],
    )
    w_pair_grad = gather_rep(w_pair_grad, n_rep)
    gate_out = place([piece[:1] for piece in w_pair_grad], r)
    up_out = place([piece[1:] for piece in w_pair_grad], r)

    branch_all = spread(branch, "rep", n_rep).reshape(all_rows, width)
    in_grad = cols_cols(branch_all, w_o).astype(BF)
    branch_all, in_grad = lax.optimization_barrier((branch_all, in_grad))
    in_grad = in_grad.reshape(all_rows, n_rep, pair * fine).transpose(1, 0, 2)
    in_grad = swap(in_grad, "rep").reshape(n_rep, n_rep, rows, pair * fine)
    w_o_grad = rows_rows(out_in, branch_all).astype(BF)
    w_o_grad = lax.psum_scatter(w_o_grad, "shard", scatter_dimension=0, tiled=True)
    w_o_grad = (w_o_grad[: fine // 2], w_o_grad[fine // 2 :])
    o_out = place(gather_rep(w_o_grad, n_rep), r)
    query_grad, kv_grad = call(
        partial(attend_back_kernel, fine),
        (shape((n_rep, rows, q_cols), BF), shape((n_rep, span, LANES), F32)),
        (n_rep,),
        [
            head_block,
            probs_block,
            by_block((rows, q_cols)),
            table,
            by_block((HALO, LANES)),
            table,
            table,
        ],
        (by_block((rows, q_cols)), by_block((span, LANES))),
    )(in_grad, probs, queries, kv_own, kv_halo, cosine, sine)
    kv_back = lax.ppermute(
        kv_grad[:, :HALO], "shard", [(i + 1, i) for i in range(n_shard - 1)]
    )
    grad_cols = qkv_cols + LANES
    one_grad_part, w_qkv_grad = call(
        in_back_kernel,
        (shape((n_rep, rows, width), BF), shape((width, grad_cols), BF)),
        (n_rep,),
        [
            by_block((rows, q_cols)),
            by_block((span, LANES)),
            by_block((HALO, LANES)),
            table,
            table,
            x_block,
            x_block,
            whole((rows, width)),
            whole((width, qkv_cols)),
        ],
        (x_block, pl.BlockSpec((width, grad_cols), lambda g: (0, 0))),
        [pltpu.VMEM((width, grad_cols), F32)],
    )(
        query_grad, kv_grad, kv_back, cosine, sine, normed_one, x_all, gain_two_rows, w_qkv
    )
    w_qkv_grad = lax.psum_scatter(w_qkv_grad, "shard", scatter_dimension=0, tiled=True)
    input_grad = call(last_kernel, shape((rows, width), BF))(
        swap(one_grad_part, "rep"), tokens, gain_one, mid_grad
    )
    w_qkv_grad = (w_qkv_grad[: own // 2], w_qkv_grad[own // 2 :])
    q_out, k_out, v_out, gain_sums = flat_call(
        partial(qkv_kernel, share),
        ids,
        (
            shape((own, width), F32),
            shape((own, KVH * HD), F32),
            shape((own, KVH * HD), F32),
            shape((own, LANES), F32),
        ),
        [half for piece in gather_rep(w_qkv_grad, n_rep) for half in piece],
        [pltpu.VMEM((n_rep, own, HD), F32)] * 2,
    )
    return (
        layer_out,
        input_grad,
        gain_sums[:, 0],
        gain_sums[:, HD],
        q_out,
        k_out,
        v_out,
        o_out,
        gate_out,
        up_out,
        down_out,
    )


def solution(mesh):
    split = P("shard", None)
    by_token = P(("rep", "shard"), None)
    return jax.shard_map(
        partial(body, mesh.shape["rep"], mesh.shape["shard"]),
        mesh=mesh,
        in_specs=(by_token, P("rep", None), P("rep", None), P("shard"), P("shard"))
        + (split,) * 7
        + (by_token,),
        out_specs=(by_token, by_token, P("shard"), P("shard")) + (split,) * 7,
        check_vma=False,
    )
```

```python
from functools import partial

import jax
import jax.numpy as jnp
from jax import lax
from jax.experimental import pallas as pl
from jax.experimental.pallas import tpu as pltpu
from jax.sharding import PartitionSpec as P


H = 32
KVH = 4
HD = 64
HALO = 64
LANES = 128

EPSILON = 1e-05
ROPE_BASE = 10000.0
NEG_FILL = -1e30

BF = jnp.bfloat16
F32 = jnp.float32


def dot(left, right, contract):
    return lax.dot_general(left, right, (contract, ((), ())), preferred_element_type=F32)


def rows_cols(left, right):
    return dot(left, right, ((1,), (0,)))


def rows_rows(left, right):
    return dot(left, right, ((0,), (0,)))


def cols_cols(left, right):
    return dot(left, right, ((1,), (1,)))


def spread(value, axis, count):
    wide = jnp.broadcast_to(value[None], (count,) + value.shape)
    return lax.all_to_all(wide, axis, split_axis=0, concat_axis=0, tiled=True)


def swap(value, axis):
    return lax.all_to_all(value, axis, split_axis=0, concat_axis=0, tiled=True)


def pairs(count, step):
    return [(i, i ^ step) for i in range(count)]


def send(value, axis, count, step):
    return lax.ppermute(value, axis, pairs(count, step))


def parts_rep(chunks, count):
    go = lambda value, step: send(value, "rep", count, step)
    if count != 4:
        return [
            [chunks[0][h]] + [go(chunks[k][h], k) for k in range(1, count)]
            for h in range(2)
        ]
    add = lambda left, right: (left.astype(F32) + right.astype(F32)).astype(BF)
    first_one = go(chunks[1][0], 1)
    first_two = go(chunks[3][0], 1)
    second_one = go(chunks[2][1], 2)
    second_two = go(chunks[3][1], 2)
    last_one = go(add(chunks[2][0], first_two), 2)
    last_two = go(add(chunks[1][1], second_two), 1)
    return [[chunks[0][0], first_one, last_one], [chunks[0][1], second_one, last_two]]


def gather_direct(value, count):
    return [value] + [send(value, "rep", count, k) for k in range(1, count)]


def gather_rep(halves, count):
    go = lambda value, step: send(value, "rep", count, step)
    if count != 4:
        return [halves] + [tuple(go(v, k) for v in halves) for k in range(1, count)]
    one = tuple(go(v, 1) for v in halves)
    two = tuple(go(v, 2) for v in halves)
    return [halves, one, two, (go(one[0], 2), go(two[1], 1))]


def place_kernel(count, me_ref, *refs):
    parts, out_ref = refs[:-1], refs[-1]
    at = pl.program_id(0)
    size = len(parts) // count
    for k in range(count):

        @pl.when(at == jnp.bitwise_xor(me_ref[0], k))
        def _(k=k):
            row = 0
            for part in parts[k * size : (k + 1) * size]:
                out_ref[0, row : row + part.shape[0]] = part[...].astype(F32)
                row += part.shape[0]


def place(pieces, me):
    count = len(pieces)
    flat = [part for piece in pieces for part in piece]
    rows = sum(part.shape[0] for part in pieces[0])
    width = flat[0].shape[1]
    grid = pltpu.PrefetchScalarGridSpec(
        num_scalar_prefetch=1,
        grid=(count,),
        in_specs=[
            pl.BlockSpec(part.shape, lambda g, me: (0, 0), pipeline_mode=pl.Buffered(1))
            for part in flat
        ],
        out_specs=pl.BlockSpec((1, rows, width), lambda g, me: (g, 0, 0)),
    )
    return pl.pallas_call(
        partial(place_kernel, count),
        out_shape=shape((count, rows, width), F32),
        grid_spec=grid,
        compiler_params=pltpu.CompilerParams(vmem_limit_bytes=56 * 1024 * 1024),
    )(me.astype(jnp.int32).reshape(1), *flat).reshape(count * rows, width)


def split_kernel(id_ref, gate_ref, up_ref, *refs):
    outs, both = refs[:-1], refs[-1]
    hidden = both.shape[3]
    for h, ref in enumerate((gate_ref, up_ref)):
        value = ref[...]
        for at in range(len(outs)):
            both[at, h] = value[:, at * hidden : (at + 1) * hidden]
    for k, out in enumerate(outs):
        out[...] = both[jnp.bitwise_xor(id_ref[1], k)]


def split_pair(ids, gate, up, fine, count):
    hidden = gate.shape[1] // count
    rows = pl.BlockSpec((fine, gate.shape[1]), lambda g, ids: (ids[0], 0))
    piece = (2, fine, hidden)
    return pl.pallas_call(
        split_kernel,
        out_shape=(shape(piece, BF),) * count,
        grid_spec=pltpu.PrefetchScalarGridSpec(
            num_scalar_prefetch=1,
            grid=(1,),
            in_specs=[rows, rows],
            out_specs=(pl.BlockSpec(piece, lambda g, ids: (0, 0, 0)),) * count,
            scratch_shapes=[pltpu.VMEM((count,) + piece, BF)],
        ),
        name="split_pair",
    )(ids, gate, up)


def flat_call(kernel, ids, out_shape, values, scratch=()):
    specs = [pl.BlockSpec(memory_space=pltpu.SMEM)]
    specs += [pl.BlockSpec(memory_space=pltpu.VMEM)] * len(values)
    return pl.pallas_call(
        kernel,
        out_shape=out_shape,
        in_specs=specs,
        scratch_shapes=list(scratch),
        compiler_params=pltpu.CompilerParams(vmem_limit_bytes=56 * 1024 * 1024),
    )(ids, *values)


def order_kernel(id_ref, *refs):
    pieces, (gate_ref, up_ref) = refs[:-2], refs[-2:]
    for k, piece in enumerate(pieces):
        at = jnp.bitwise_xor(id_ref[1], k)
        gate_ref[at] = piece[0]
        up_ref[at] = piece[1]


def join_kernel(id_ref, *refs):
    out_ref = refs[-1]
    for k in range(len(refs) // 2):
        at = jnp.bitwise_xor(id_ref[0], k)
        for h in range(2):
            value = refs[2 * k + h]
            for row in range(value.shape[0]):
                out_ref[h, row, at] = value[row]


def sum_kernel(id_ref, *refs):
    count = refs[0].shape[0]
    outs = refs[len(refs) - count :]
    parts = refs[: len(refs) - count]
    half = len(parts) // 2
    for k, out in enumerate(outs):
        at = jnp.bitwise_xor(id_ref[1], k)
        for h in range(2):
            total = parts[h * half][at].astype(F32)
            for part in parts[h * half + 1 : (h + 1) * half]:
                total += part[at].astype(F32)
            out[h] = total.astype(BF)


def widen_kernel(id_ref, *refs):
    pieces, (gate_ref, up_ref, both) = refs[:-3], refs[-3:]
    hidden = both.shape[3]
    for k, piece in enumerate(pieces):
        both[jnp.bitwise_xor(id_ref[1], k)] = piece[...]
    for h, ref in enumerate((gate_ref, up_ref)):
        for at in range(len(pieces)):
            ref[:, at * hidden : (at + 1) * hidden] = both[at, h]


def qkv_kernel(share, id_ref, *refs):
    pieces = refs[:-6]
    q_ref, k_ref, v_ref, gain_ref, k_all, v_all = refs[-6:]
    count = k_all.shape[0]
    q_cols = q_ref.shape[1] // count
    total = 0.0
    for k, piece in enumerate(pieces):
        at = jnp.bitwise_xor(id_ref[0], k)
        value = piece[...].astype(F32)
        q_ref[:, pl.ds(pl.multiple_of(at * q_cols, LANES), q_cols)] = value[:, :q_cols]
        k_all[at] = value[:, q_cols : q_cols + HD]
        v_all[at] = value[:, q_cols + HD : q_cols + 2 * HD]
        total += value[:, q_cols + 2 * HD :]
    gain_ref[...] = total
    for ref, both in ((k_ref, k_all), (v_ref, v_all)):
        for head in range(count // share):
            total = both[head * share]
            for other in range(head * share + 1, (head + 1) * share):
                total += both[other]
            ref[:, head * HD : (head + 1) * HD] = total


def pair_grad_kernel(fine, id_ref, x_ref, grad_ref, *refs):
    outs, total_ref = refs[:-1], refs[-1]
    total_ref[...] = rows_rows(x_ref[...], grad_ref[...])
    own = fine * len(outs)
    for k, out in enumerate(outs):
        row = jnp.bitwise_xor(id_ref[0], k) * fine
        for block in range(out.shape[0]):
            at = pl.multiple_of(block * own + row, fine)
            out[block] = total_ref[pl.ds(at, fine)].astype(BF)


def pair_grad(ids, x, grad, fine, count, blocks):
    width, hidden = x.shape[1], grad.shape[1]
    tile = 2 * fine * count
    out = (2, fine, hidden)
    return pl.pallas_call(
        partial(pair_grad_kernel, fine),
        out_shape=(shape((blocks, fine, hidden), BF),) * count,
        grid_spec=pltpu.PrefetchScalarGridSpec(
            num_scalar_prefetch=1,
            grid=(width // tile,),
            in_specs=[
                pl.BlockSpec((x.shape[0], tile), lambda g, ids: (0, g)),
                pl.BlockSpec(grad.shape, lambda g, ids: (0, 0), pipeline_mode=pl.Buffered(1)),
            ],
            out_specs=(pl.BlockSpec(out, lambda g, ids: (g, 0, 0)),) * count,
            scratch_shapes=[pltpu.VMEM((tile, hidden), F32)],
        ),
        compiler_params=pltpu.CompilerParams(vmem_limit_bytes=56 * 1024 * 1024),
    )(ids, x, grad)


def norm_scale(value):
    return lax.rsqrt(jnp.mean(value * value, axis=1, keepdims=True) + EPSILON)


def turn(tile, cosine, sine):
    lane = lax.broadcasted_iota(jnp.int32, tile.shape, 1)
    swapped = jnp.where(
        lane % HD < HD // 2,
        -pltpu.roll(tile, LANES - HD // 2, 1),
        pltpu.roll(tile, HD // 2, 1),
    )
    return tile * cosine + swapped * sine


def turn_first(tile, cosine, sine):
    lane = lax.broadcasted_iota(jnp.int32, tile.shape, 1)
    return jnp.where(lane < HD, turn(tile, cosine, sine), tile)


def in_kernel(x_ref, gain_ref, w_ref, cos_ref, sin_ref, normed_ref, q_ref, kv_ref):
    x = x_ref[0].astype(F32)
    normed = (x * norm_scale(x) * gain_ref[...]).astype(BF)
    normed_ref[0] = normed
    qkv = rows_cols(normed, w_ref[...])
    cosine, sine = cos_ref[0], sin_ref[0]
    q_cols = q_ref.shape[2]
    for at in range(0, q_cols, LANES):
        q_ref[0, :, at : at + LANES] = turn(qkv[:, at : at + LANES], cosine, sine).astype(BF)
    kv_ref[0] = turn_first(qkv[:, q_cols:], cosine, sine).astype(BF)


def stack_heads(value):
    return jnp.concatenate(
        [value[:, at : at + HD] for at in range(0, value.shape[1], HD)], axis=0
    )


def unstack_heads(value, rows):
    return jnp.concatenate(
        [value[at : at + rows] for at in range(0, value.shape[0], rows)], axis=1
    )


def attend_kernel(fine, q_ref, own_ref, halo_ref, pos_ref, probs_ref, out_ref):
    rows, q_cols = q_ref.shape[1:]
    heads = q_cols // HD
    count = out_ref.shape[0]
    kv = jnp.concatenate([halo_ref[0], own_ref[0]], axis=0)
    keys, values = kv[:, :HD], kv[:, HD:]
    span = kv.shape[0]
    scores = cols_cols(stack_heads(q_ref[0]), keys) * (HD**-0.5)
    query = lax.broadcasted_iota(jnp.int32, (rows, span), 0) + HALO
    key = lax.broadcasted_iota(jnp.int32, (rows, span), 1)
    first = query - pos_ref[0][:, :1].astype(jnp.int32)
    allowed = (key >= first) & (key <= query)
    scores = jnp.where(allowed[None], scores.reshape(heads, rows, span), NEG_FILL)
    grown = jnp.exp(scores - jnp.max(scores, axis=-1, keepdims=True))
    probs = grown / jnp.sum(grown, axis=-1, keepdims=True)
    probs_ref[0] = probs
    mixed = rows_cols(probs.reshape(heads * rows, span).astype(BF), values)
    mixed = unstack_heads(mixed, rows).astype(BF)
    for to in range(count):
        out_ref[to, 0] = jnp.concatenate(
            [
                mixed[:, at + to * fine : at + (to + 1) * fine]
                for at in range(0, q_cols, count * fine)
            ],
            axis=1,
        )


def attend_back_kernel(
    fine, grad_ref, probs_ref, q_ref, own_ref, halo_ref, cos_ref, sin_ref, q_out, kv_out
):
    rows, q_cols = q_ref.shape[1:]
    heads = q_cols // HD
    count = grad_ref.shape[0]
    kv = jnp.concatenate([halo_ref[0], own_ref[0]], axis=0)
    keys, values = kv[:, :HD], kv[:, HD:]
    span = kv.shape[0]
    grad = jnp.concatenate(
        [
            grad_ref[source, 0][:, at * fine : (at + 1) * fine]
            for at in range(q_cols // (count * fine))
            for source in range(count)
        ],
        axis=1,
    )
    grad = stack_heads(grad)
    probs = probs_ref[0].reshape(heads * rows, span)
    probs_grad = cols_cols(grad, values)
    inner = jnp.sum(probs * probs_grad, axis=-1, keepdims=True)
    score_grad = (probs * (probs_grad - inner)).astype(BF)
    scale = HD**-0.5
    key_grad = rows_rows(score_grad, stack_heads(q_ref[0])) * scale
    value_grad = rows_rows(probs.astype(BF), grad)
    kv_out[0] = jnp.concatenate([key_grad, value_grad], axis=1)
    query_grad = unstack_heads(rows_cols(score_grad, keys) * scale, rows)
    cosine, sine = cos_ref[0], -sin_ref[0]
    for at in range(0, q_cols, LANES):
        q_out[0, :, at : at + LANES] = turn(
            query_grad[:, at : at + LANES], cosine, sine
        ).astype(BF)


def in_back_kernel(
    dq_ref, dkv_ref, back_ref, cos_ref, sin_ref, normed_ref, x_ref, two_ref, w_ref,
    part_ref, grad_ref, total_ref,
):
    at = pl.program_id(0)
    rows = dq_ref.shape[1]
    own = dkv_ref[0, HALO:]
    tail = own[rows - HALO :] + back_ref[0]
    own = jnp.concatenate([own[: rows - HALO], tail], axis=0)
    own = turn_first(own, cos_ref[0], -sin_ref[0]).astype(BF)
    qkv_grad = jnp.concatenate([dq_ref[0], own], axis=1)
    normed_grad = cols_cols(qkv_grad, w_ref[...])
    part_ref[0] = normed_grad.astype(BF)
    x = x_ref[0].astype(F32)
    one = (normed_grad * x * norm_scale(x)).astype(BF)
    cols = qkv_grad.shape[1]
    lane = lax.broadcasted_iota(jnp.int32, (rows, LANES), 1)

    @pl.when(at == 0)
    def _():
        total_ref[:, :cols] = rows_rows(normed_ref[0], qkv_grad)
        total_ref[:, cols:] = rows_rows(one, (lane < HD).astype(BF)) + rows_rows(
            two_ref[...], (lane >= HD).astype(BF)
        )

    @pl.when(at > 0)
    def _():
        total_ref[:, :cols] += rows_rows(normed_ref[0], qkv_grad)
        total_ref[:, cols:] += rows_rows(one, (lane < HD).astype(BF))

    @pl.when(at == pl.num_programs(0) - 1)
    def _():
        grad_ref[...] = total_ref[...].astype(BF)


def middle_kernel(part_ref, x_ref, gain_ref, mid_ref, normed_ref):
    mid = x_ref[...].astype(F32)
    for at in range(part_ref.shape[0]):
        mid += part_ref[at].astype(F32)
    mid_ref[...] = mid
    normed_ref[...] = (mid * norm_scale(mid) * gain_ref[...]).astype(BF)


def middle_back_kernel(grad_ref, mid_ref, gain_ref, cot_ref, out_ref, low_ref, gain_out_ref):
    mid = mid_ref[...]
    scale = norm_scale(mid)
    grad = grad_ref[...].astype(F32)
    gain_out_ref[...] = (grad * mid * scale).astype(BF)
    scaled = grad * gain_ref[...]
    out = (
        cot_ref[...].astype(F32)
        + scale * scaled
        - mid * scale**3 * jnp.mean(scaled * mid, axis=1, keepdims=True)
    )
    out_ref[...] = out
    low_ref[...] = out.astype(BF)


def last_kernel(part_ref, x_ref, gain_ref, mid_ref, out_ref):
    x = x_ref[...].astype(F32)
    scale = norm_scale(x)
    grad = part_ref[0].astype(F32)
    for at in range(1, part_ref.shape[0]):
        grad += part_ref[at].astype(F32)
    scaled = grad * gain_ref[...]
    out = (
        mid_ref[...]
        + scale * scaled
        - x * scale**3 * jnp.mean(scaled * x, axis=1, keepdims=True)
    )
    out_ref[...] = out.astype(BF)


def forward_back_kernel(
    x_ref, cot_ref, pair_ref, down_ref, mixed_ref, gate_out, up_out, part_ref
):
    x = x_ref[...]
    gate = rows_cols(x, pair_ref[0])
    up = rows_cols(x, pair_ref[1])
    mixed_grad = cols_cols(cot_ref[...], down_ref[...])
    sigma = jax.nn.sigmoid(gate)
    silu = gate * sigma
    mixed_ref[...] = (silu * up).astype(BF)
    gate_grad = (mixed_grad * up * sigma * (1.0 + gate * (1.0 - sigma))).astype(BF)
    up_grad = (mixed_grad * silu).astype(BF)
    gate_out[...] = gate_grad
    up_out[...] = up_grad
    part_ref[...] = (
        cols_cols(gate_grad, pair_ref[0]) + cols_cols(up_grad, pair_ref[1])
    ).astype(BF)


def shape(dims, kind):
    return jax.ShapeDtypeStruct(dims, kind)


def call(kernel, out_shape, grid=None, in_specs=None, out_specs=None, scratch=()):
    options = {}
    if grid is not None:
        options = {"grid": grid, "in_specs": in_specs, "out_specs": out_specs}
    return pl.pallas_call(
        kernel,
        out_shape=out_shape,
        scratch_shapes=list(scratch),
        compiler_params=pltpu.CompilerParams(vmem_limit_bytes=56 * 1024 * 1024),
        **options,
    )


def by_block(dims):
    return pl.BlockSpec((1,) + dims, lambda g: (g,) + (0,) * len(dims))


def whole(dims):
    return pl.BlockSpec(dims, lambda g: (0,) * len(dims), pipeline_mode=pl.Buffered(1))


def body(
    n_rep,
    n_shard,
    tokens,
    seq_lengths,
    deal_order,
    attn_gain,
    mlp_gain,
    q_weight,
    k_weight,
    v_weight,
    o_weight,
    gate_weight,
    up_weight,
    down_weight,
    cotangent,
):
    rows, width = tokens.shape
    r = lax.axis_index("rep")
    s = lax.axis_index("shard")
    own = width // n_shard
    fine = own // n_rep
    hidden = down_weight.shape[0]
    q_cols = width // n_rep
    heads = H // n_rep
    pair = n_shard // n_rep
    share = max(n_rep // KVH, 1)
    kv_at = (r * KVH) // n_rep
    all_rows = n_rep * rows
    span = HALO + rows
    qkv_cols = q_cols + 2 * HD

    starts = jnp.cumsum(seq_lengths[0]) - seq_lengths[0]
    places = s * rows + jnp.arange(rows, dtype=jnp.int32)
    first = jnp.max(
        jnp.where(starts[None, :] <= places[:, None], starts[None, :], 0), axis=1, keepdims=True
    )
    offset = jnp.broadcast_to((places[:, None] - first).astype(BF), (rows, LANES))

    w_qkv_own = jnp.concatenate(
        [
            lax.dynamic_slice_in_dim(q_weight, r * q_cols, q_cols, 1),
            lax.dynamic_slice_in_dim(k_weight, kv_at * HD, HD, 1),
            lax.dynamic_slice_in_dim(v_weight, kv_at * HD, HD, 1),
        ],
        axis=1,
    )
    w_qkv = lax.all_gather(w_qkv_own, "shard", axis=0, tiled=True)
    w_o = lax.all_gather(
        lax.dynamic_slice_in_dim(o_weight, r * fine, fine, 0), "shard", axis=0, tiled=True
    )
    x_all = spread(jnp.concatenate([tokens, offset], axis=1), "rep", n_rep)
    gains = lax.all_gather(jnp.stack([attn_gain, mlp_gain]), "shard", axis=1, tiled=True)
    gain_one = gains[0:1].astype(F32)
    gain_two = gains[1:2].astype(F32)

    def exchange_shard(pieces):
        rest = [send(pieces[k], "shard", n_shard, k) for k in range(1, n_shard)]
        return [pieces[0]] + rest

    block = (n_shard, fine, hidden)
    ids = jnp.stack([r, s]).astype(jnp.int32)
    gate_tied, up_tied, _ = lax.optimization_barrier((gate_weight, up_weight, gains))
    w_pair = split_pair(ids, gate_tied, up_tied, fine, n_shard)
    w_pair = exchange_shard(w_pair)
    w_pair = flat_call(order_kernel, ids, (shape(block, BF),) * 2, w_pair)
    w_pair = gather_rep(w_pair, n_rep)
    w_pair = flat_call(
        join_kernel,
        ids,
        shape((2, n_shard, n_rep, fine, hidden), BF),
        [half for piece in w_pair for half in piece],
    ).reshape(2, width, hidden)
    cot_all = lax.all_gather(cotangent, "shard", axis=0, tiled=True)

    half = HD // 2
    inverse = ROPE_BASE ** (-2.0 * (jnp.arange(LANES) % half).astype(F32) / HD)
    angles = x_all[:, :, width:].astype(F32) * inverse[None, None, :]
    cosine, sine = jnp.cos(angles), jnp.sin(angles)
    x_block = by_block((rows, width))
    table = by_block((rows, LANES))
    normed_one, queries, kv_own = call(
        in_kernel,
        (
            shape((n_rep, rows, width), BF),
            shape((n_rep, rows, q_cols), BF),
            shape((n_rep, rows, LANES), BF),
        ),
        (n_rep,),
        [x_block, whole((1, width)), whole((width, qkv_cols)), table, table],
        (x_block, by_block((rows, q_cols)), table),
    )(x_all, gain_one, w_qkv, cosine, sine)
    kv_halo = lax.ppermute(
        kv_own[:, rows - HALO :], "shard", [(i, i + 1) for i in range(n_shard - 1)]
    )
    head_block = pl.BlockSpec((n_rep, 1, rows, pair * fine), lambda g: (0, g, 0, 0))
    probs_block = by_block((heads, rows, span))
    probs, out_in = call(
        partial(attend_kernel, fine),
        (
            shape((n_rep, heads, rows, span), F32),
            shape((n_rep, n_rep, rows, pair * fine), BF),
        ),
        (n_rep,),
        [
            by_block((rows, q_cols)),
            table,
            by_block((HALO, LANES)),
            pl.BlockSpec((1, rows, LANES), lambda g: (g, 0, width // LANES)),
        ],
        (probs_block, head_block),
    )(queries, kv_own, kv_halo, x_all)
    out_in = swap(out_in, "rep").reshape(n_rep, all_rows, pair * fine)
    out_in = out_in.transpose(1, 0, 2).reshape(all_rows, q_cols)
    mid_part = rows_cols(out_in, w_o).astype(BF).reshape(n_rep, rows, width)
    x_mid, normed_two = call(
        middle_kernel, (shape((rows, width), F32), shape((rows, width), BF))
    )(swap(mid_part, "rep"), tokens, gain_two)

    two_all = lax.all_gather(normed_two, "shard", axis=0, tiled=True)
    step = 256
    group = two_all.shape[0]
    token_block = pl.BlockSpec((step, width), lambda g: (g, 0))
    hidden_block = pl.BlockSpec((step, hidden), lambda g: (g, 0))
    mixed, gate_grad, up_grad, two_grad_part = call(
        forward_back_kernel,
        (shape((group, hidden), BF),) * 3 + (shape((group, width), BF),),
        (group // step,),
        [token_block, token_block, whole((2, width, hidden)), whole((hidden, width))],
        (hidden_block,) * 3 + (token_block,),
    )(two_all, cot_all, w_pair, down_weight)
    two_grad = lax.psum_scatter(two_grad_part, "shard", scatter_dimension=0, tiled=True)
    mid_grad, branch, gain_two_rows = call(
        middle_back_kernel,
        (shape((rows, width), F32), shape((rows, width), BF), shape((rows, width), BF)),
    )(two_grad, x_mid, gain_two, cotangent)

    gate_chunks = pair_grad(ids, two_all, gate_grad, fine, n_rep, n_shard)
    up_grad, _ = lax.optimization_barrier((up_grad, gate_chunks[0]))
    up_chunks = pair_grad(ids, two_all, up_grad, fine, n_rep, n_shard)
    pair_chunks = list(zip(gate_chunks, up_chunks))
    mixed, _ = lax.optimization_barrier((mixed, up_chunks[0]))
    part_rows = hidden // n_rep
    cut = (part_rows // 2 + 15) // 16 * 16
    w_down_grad = rows_rows(mixed, cot_all).astype(BF)
    mixed, w_down_grad = lax.optimization_barrier((mixed, w_down_grad))
    down_part = rows_cols(mixed, down_weight).astype(BF)
    down_rows = lax.psum_scatter(down_part, "shard", scatter_dimension=0, tiled=True)
    layer_out = (x_mid + down_rows.astype(F32)).astype(BF)
    chunks = []
    for k in range(n_rep):
        at = (r ^ k) * part_rows
        chunks.append(
            (
                lax.dynamic_slice_in_dim(w_down_grad, at, cut, 0),
                lax.dynamic_slice_in_dim(w_down_grad, at + cut, part_rows - cut, 0),
            )
        )
    w_down_grad = parts_rep(chunks, n_rep)
    w_down_grad = tuple(
        sum(part.astype(F32) for part in parts).astype(BF) for parts in w_down_grad
    )
    down_out = place(gather_rep(w_down_grad, n_rep), r)
    w_pair_grad = parts_rep(pair_chunks, n_rep)
    w_pair_grad = flat_call(
        sum_kernel,
        ids,
        (shape((2, fine, hidden), BF),) * n_shard,
        w_pair_grad[0] + w_pair_grad[1],
    )
    w_pair_grad = exchange_shard(w_pair_grad)
    w_pair_grad = flat_call(
        widen_kernel,
        ids,
        (shape((fine, n_shard * hidden), BF),) * 2,
        w_pair_grad,
        [pltpu.VMEM((n_shard, 2, fine, hidden), BF)],
    )
    w_pair_grad = gather_rep(w_pair_grad, n_rep)
    gate_out = place([piece[:1] for piece in w_pair_grad], r)
    up_out = place([piece[1:] for piece in w_pair_grad], r)

    branch_all = spread(branch, "rep", n_rep).reshape(all_rows, width)
    in_grad = cols_cols(branch_all, w_o).astype(BF)
    branch_all, in_grad = lax.optimization_barrier((branch_all, in_grad))
    in_grad = in_grad.reshape(all_rows, n_rep, pair * fine).transpose(1, 0, 2)
    in_grad = swap(in_grad, "rep").reshape(n_rep, n_rep, rows, pair * fine)
    w_o_grad = rows_rows(out_in, branch_all).astype(BF)
    w_o_grad = lax.psum_scatter(w_o_grad, "shard", scatter_dimension=0, tiled=True)
    o_out = place([(v,) for v in gather_direct(w_o_grad, n_rep)], r)
    query_grad, kv_grad = call(
        partial(attend_back_kernel, fine),
        (shape((n_rep, rows, q_cols), BF), shape((n_rep, span, LANES), F32)),
        (n_rep,),
        [
            head_block,
            probs_block,
            by_block((rows, q_cols)),
            table,
            by_block((HALO, LANES)),
            table,
            table,
        ],
        (by_block((rows, q_cols)), by_block((span, LANES))),
    )(in_grad, probs, queries, kv_own, kv_halo, cosine, sine)
    kv_back = lax.ppermute(
        kv_grad[:, :HALO], "shard", [(i + 1, i) for i in range(n_shard - 1)]
    )
    grad_cols = qkv_cols + LANES
    one_grad_part, w_qkv_grad = call(
        in_back_kernel,
        (shape((n_rep, rows, width), BF), shape((width, grad_cols), BF)),
        (n_rep,),
        [
            by_block((rows, q_cols)),
            by_block((span, LANES)),
            by_block((HALO, LANES)),
            table,
            table,
            x_block,
            x_block,
            whole((rows, width)),
            whole((width, qkv_cols)),
        ],
        (x_block, pl.BlockSpec((width, grad_cols), lambda g: (0, 0))),
        [pltpu.VMEM((width, grad_cols), F32)],
    )(
        query_grad, kv_grad, kv_back, cosine, sine, normed_one, x_all, gain_two_rows, w_qkv
    )
    w_qkv_grad = lax.psum_scatter(w_qkv_grad, "shard", scatter_dimension=0, tiled=True)
    input_grad = call(last_kernel, shape((rows, width), BF))(
        swap(one_grad_part, "rep"), tokens, gain_one, mid_grad
    )
    q_out, k_out, v_out, gain_sums = flat_call(
        partial(qkv_kernel, share),
        ids,
        (
            shape((own, width), F32),
            shape((own, KVH * HD), F32),
            shape((own, KVH * HD), F32),
            shape((own, LANES), F32),
        ),
        gather_direct(w_qkv_grad, n_rep),
        [pltpu.VMEM((n_rep, own, HD), F32)] * 2,
    )
    return (
        layer_out,
        input_grad,
        gain_sums[:, 0],
        gain_sums[:, HD],
        q_out,
        k_out,
        v_out,
        o_out,
        gate_out,
        up_out,
        down_out,
    )


def solution(mesh):
    split = P("shard", None)
    by_token = P(("rep", "shard"), None)
    return jax.shard_map(
        partial(body, mesh.shape["rep"], mesh.shape["shard"]),
        mesh=mesh,
        in_specs=(by_token, P("rep", None), P("rep", None), P("shard"), P("shard"))
        + (split,) * 7
        + (by_token,),
        out_specs=(by_token, by_token, P("shard"), P("shard")) + (split,) * 7,
        check_vma=False,
    )
```

```python
from functools import partial

import jax
import jax.numpy as jnp
from jax import lax
from jax.experimental import pallas as pl
from jax.experimental.pallas import tpu as pltpu
from jax.sharding import PartitionSpec as P


H = 32
KVH = 4
HD = 64
HALO = 64
LANES = 128

EPSILON = 1e-05
ROPE_BASE = 10000.0
NEG_FILL = -1e30

BF = jnp.bfloat16
F32 = jnp.float32


def dot(left, right, contract):
    return lax.dot_general(left, right, (contract, ((), ())), preferred_element_type=F32)


def rows_cols(left, right):
    return dot(left, right, ((1,), (0,)))


def rows_rows(left, right):
    return dot(left, right, ((0,), (0,)))


def cols_cols(left, right):
    return dot(left, right, ((1,), (1,)))


def spread(value, axis, count):
    wide = jnp.broadcast_to(value[None], (count,) + value.shape)
    return lax.all_to_all(wide, axis, split_axis=0, concat_axis=0, tiled=True)


def swap(value, axis):
    return lax.all_to_all(value, axis, split_axis=0, concat_axis=0, tiled=True)


def pairs(count, step):
    return [(i, i ^ step) for i in range(count)]


def send(value, axis, count, step):
    return lax.ppermute(value, axis, pairs(count, step))


def parts_rep(chunks, count):
    go = lambda value, step: send(value, "rep", count, step)
    if count != 4:
        return [
            [chunks[0][h]] + [go(chunks[k][h], k) for k in range(1, count)]
            for h in range(2)
        ]
    add = lambda left, right: (left.astype(F32) + right.astype(F32)).astype(BF)
    first_one = go(chunks[1][0], 1)
    first_two = go(chunks[3][0], 1)
    second_one = go(chunks[2][1], 2)
    second_two = go(chunks[3][1], 2)
    last_one = go(add(chunks[2][0], first_two), 2)
    last_two = go(add(chunks[1][1], second_two), 1)
    return [[chunks[0][0], first_one, last_one], [chunks[0][1], second_one, last_two]]


def gather_direct(value, count):
    return [value] + [send(value, "rep", count, k) for k in range(1, count)]


def gather_rep(halves, count):
    go = lambda value, step: send(value, "rep", count, step)
    if count != 4:
        return [halves] + [tuple(go(v, k) for v in halves) for k in range(1, count)]
    one = tuple(go(v, 1) for v in halves)
    two = tuple(go(v, 2) for v in halves)
    return [halves, one, two, (go(one[0], 2), go(two[1], 1))]


def place_kernel(count, me_ref, *refs):
    parts, out_ref = refs[:-1], refs[-1]
    at = pl.program_id(0)
    size = len(parts) // count
    for k in range(count):

        @pl.when(at == jnp.bitwise_xor(me_ref[0], k))
        def _(k=k):
            row = 0
            for part in parts[k * size : (k + 1) * size]:
                out_ref[0, row : row + part.shape[0]] = part[...].astype(F32)
                row += part.shape[0]


def place(pieces, me):
    count = len(pieces)
    flat = [part for piece in pieces for part in piece]
    rows = sum(part.shape[0] for part in pieces[0])
    width = flat[0].shape[1]
    grid = pltpu.PrefetchScalarGridSpec(
        num_scalar_prefetch=1,
        grid=(count,),
        in_specs=[
            pl.BlockSpec(part.shape, lambda g, me: (0, 0), pipeline_mode=pl.Buffered(1))
            for part in flat
        ],
        out_specs=pl.BlockSpec((1, rows, width), lambda g, me: (g, 0, 0)),
    )
    return pl.pallas_call(
        partial(place_kernel, count),
        out_shape=shape((count, rows, width), F32),
        grid_spec=grid,
        compiler_params=pltpu.CompilerParams(vmem_limit_bytes=56 * 1024 * 1024),
    )(me.astype(jnp.int32).reshape(1), *flat).reshape(count * rows, width)


def split_kernel(id_ref, gate_ref, up_ref, *refs):
    outs, both = refs[:-1], refs[-1]
    hidden = both.shape[3]
    for h, ref in enumerate((gate_ref, up_ref)):
        value = ref[...]
        for at in range(len(outs)):
            both[at, h] = value[:, at * hidden : (at + 1) * hidden]
    for k, out in enumerate(outs):
        out[...] = both[jnp.bitwise_xor(id_ref[1], k)]


def split_pair(ids, gate, up, fine, count):
    hidden = gate.shape[1] // count
    rows = pl.BlockSpec((fine, gate.shape[1]), lambda g, ids: (ids[0], 0))
    piece = (2, fine, hidden)
    return pl.pallas_call(
        split_kernel,
        out_shape=(shape(piece, BF),) * count,
        grid_spec=pltpu.PrefetchScalarGridSpec(
            num_scalar_prefetch=1,
            grid=(1,),
            in_specs=[rows, rows],
            out_specs=(pl.BlockSpec(piece, lambda g, ids: (0, 0, 0)),) * count,
            scratch_shapes=[pltpu.VMEM((count,) + piece, BF)],
        ),
        name="split_pair",
    )(ids, gate, up)


def flat_call(kernel, ids, out_shape, values, scratch=()):
    specs = [pl.BlockSpec(memory_space=pltpu.SMEM)]
    specs += [pl.BlockSpec(memory_space=pltpu.VMEM)] * len(values)
    return pl.pallas_call(
        kernel,
        out_shape=out_shape,
        in_specs=specs,
        scratch_shapes=list(scratch),
        compiler_params=pltpu.CompilerParams(vmem_limit_bytes=56 * 1024 * 1024),
    )(ids, *values)


def order_kernel(id_ref, *refs):
    pieces, (gate_ref, up_ref) = refs[:-2], refs[-2:]
    for k, piece in enumerate(pieces):
        at = jnp.bitwise_xor(id_ref[1], k)
        gate_ref[at] = piece[0]
        up_ref[at] = piece[1]


def join_kernel(id_ref, *refs):
    out_ref = refs[-1]
    for k in range(len(refs) // 2):
        at = jnp.bitwise_xor(id_ref[0], k)
        for h in range(2):
            value = refs[2 * k + h]
            for row in range(value.shape[0]):
                out_ref[h, row, at] = value[row]


def sum_kernel(id_ref, *refs):
    count = refs[0].shape[0]
    outs = refs[len(refs) - count :]
    parts = refs[: len(refs) - count]
    half = len(parts) // 2
    for k, out in enumerate(outs):
        at = jnp.bitwise_xor(id_ref[1], k)
        for h in range(2):
            total = parts[h * half][at].astype(F32)
            for part in parts[h * half + 1 : (h + 1) * half]:
                total += part[at].astype(F32)
            out[h] = total.astype(BF)


def widen_kernel(id_ref, *refs):
    pieces, (gate_ref, up_ref, both) = refs[:-3], refs[-3:]
    hidden = both.shape[3]
    for k, piece in enumerate(pieces):
        both[jnp.bitwise_xor(id_ref[1], k)] = piece[...]
    for h, ref in enumerate((gate_ref, up_ref)):
        for at in range(len(pieces)):
            ref[:, at * hidden : (at + 1) * hidden] = both[at, h]


def qkv_kernel(share, id_ref, *refs):
    pieces = refs[:-6]
    q_ref, k_ref, v_ref, gain_ref, k_all, v_all = refs[-6:]
    count = k_all.shape[0]
    q_cols = q_ref.shape[1] // count
    total = 0.0
    for k, piece in enumerate(pieces):
        at = jnp.bitwise_xor(id_ref[0], k)
        value = piece[...].astype(F32)
        q_ref[:, pl.ds(pl.multiple_of(at * q_cols, LANES), q_cols)] = value[:, :q_cols]
        k_all[at] = value[:, q_cols : q_cols + HD]
        v_all[at] = value[:, q_cols + HD : q_cols + 2 * HD]
        total += value[:, q_cols + 2 * HD :]
    gain_ref[...] = total
    for ref, both in ((k_ref, k_all), (v_ref, v_all)):
        for head in range(count // share):
            total = both[head * share]
            for other in range(head * share + 1, (head + 1) * share):
                total += both[other]
            ref[:, head * HD : (head + 1) * HD] = total


def pair_grad_kernel(fine, id_ref, x_ref, grad_ref, *refs):
    outs, total_ref = refs[:-1], refs[-1]
    total_ref[...] = rows_rows(x_ref[...], grad_ref[...])
    own = fine * len(outs)
    for k, out in enumerate(outs):
        row = jnp.bitwise_xor(id_ref[0], k) * fine
        for block in range(out.shape[0]):
            at = pl.multiple_of(block * own + row, fine)
            out[block] = total_ref[pl.ds(at, fine)].astype(BF)


def pair_grad(ids, x, grad, fine, count, blocks):
    width, hidden = x.shape[1], grad.shape[1]
    tile = 2 * fine * count
    out = (2, fine, hidden)
    return pl.pallas_call(
        partial(pair_grad_kernel, fine),
        out_shape=(shape((blocks, fine, hidden), BF),) * count,
        grid_spec=pltpu.PrefetchScalarGridSpec(
            num_scalar_prefetch=1,
            grid=(width // tile,),
            in_specs=[
                pl.BlockSpec((x.shape[0], tile), lambda g, ids: (0, g)),
                pl.BlockSpec(grad.shape, lambda g, ids: (0, 0), pipeline_mode=pl.Buffered(1)),
            ],
            out_specs=(pl.BlockSpec(out, lambda g, ids: (g, 0, 0)),) * count,
            scratch_shapes=[pltpu.VMEM((tile, hidden), F32)],
        ),
        compiler_params=pltpu.CompilerParams(vmem_limit_bytes=56 * 1024 * 1024),
    )(ids, x, grad)


def norm_scale(value):
    return lax.rsqrt(jnp.mean(value * value, axis=1, keepdims=True) + EPSILON)


def turn(tile, cosine, sine):
    lane = lax.broadcasted_iota(jnp.int32, tile.shape, 1)
    swapped = jnp.where(
        lane % HD < HD // 2,
        -pltpu.roll(tile, LANES - HD // 2, 1),
        pltpu.roll(tile, HD // 2, 1),
    )
    return tile * cosine + swapped * sine


def turn_first(tile, cosine, sine):
    lane = lax.broadcasted_iota(jnp.int32, tile.shape, 1)
    return jnp.where(lane < HD, turn(tile, cosine, sine), tile)


def in_kernel(
    x_ref, w_ref, lane_ref, cos_ref, sin_ref, normed_ref, q_ref, kv_ref, gain_ref
):
    @pl.when(pl.program_id(0) == 0)
    def _():
        row = lax.broadcasted_iota(jnp.int32, (gain_ref.shape[0], LANES), 0)
        lane = lax.broadcasted_iota(jnp.int32, (gain_ref.shape[0], LANES), 1)
        gain_ref[...] = cols_cols((lane == row * HD).astype(BF), lane_ref[...])

    x = x_ref[0].astype(F32)
    normed = (x * norm_scale(x) * gain_ref[0:1]).astype(BF)
    normed_ref[0] = normed
    qkv = rows_cols(normed, w_ref[...])
    cosine, sine = cos_ref[0], sin_ref[0]
    q_cols = q_ref.shape[2]
    for at in range(0, q_cols, LANES):
        q_ref[0, :, at : at + LANES] = turn(qkv[:, at : at + LANES], cosine, sine).astype(BF)
    kv_ref[0] = turn_first(qkv[:, q_cols:], cosine, sine).astype(BF)


def out_kernel(heads_ref, w_ref, part_ref, joined_ref):
    cols = part_ref.shape[2]

    @pl.when(pl.program_id(0) == 0)
    def _():
        joined_ref[...] = jnp.concatenate(
            [heads_ref[source] for source in range(heads_ref.shape[0])], axis=1
        )

    w = w_ref[:, 0].reshape(joined_ref.shape[1], w_ref.shape[3])[:, :cols]
    part = rows_cols(joined_ref[...], w).astype(BF)
    part_ref[...] = part.reshape(part_ref.shape)


def out_back_kernel(grad_ref, w_ref, heads_ref, total_ref):
    at = pl.program_id(0)
    cols = grad_ref.shape[1]
    w = w_ref[:, 0].reshape(total_ref.shape[1], w_ref.shape[3])[:, :cols]
    part = cols_cols(grad_ref[...], w)

    @pl.when(at == 0)
    def _():
        total_ref[...] = part

    @pl.when(at > 0)
    def _():
        total_ref[...] += part

    @pl.when(at == pl.num_programs(0) - 1)
    def _():
        size = heads_ref.shape[2]
        for source in range(heads_ref.shape[0]):
            heads_ref[source] = total_ref[:, source * size : (source + 1) * size].astype(BF)


def stack_heads(value):
    return jnp.concatenate(
        [value[:, at : at + HD] for at in range(0, value.shape[1], HD)], axis=0
    )


def unstack_heads(value, rows):
    return jnp.concatenate(
        [value[at : at + rows] for at in range(0, value.shape[0], rows)], axis=1
    )


def attend_kernel(fine, q_ref, own_ref, halo_ref, pos_ref, probs_ref, out_ref):
    rows, q_cols = q_ref.shape[1:]
    heads = q_cols // HD
    count = out_ref.shape[0]
    kv = jnp.concatenate([halo_ref[0], own_ref[0]], axis=0)
    keys, values = kv[:, :HD], kv[:, HD:]
    span = kv.shape[0]
    scores = cols_cols(stack_heads(q_ref[0]), keys) * (HD**-0.5)
    query = lax.broadcasted_iota(jnp.int32, (rows, span), 0) + HALO
    key = lax.broadcasted_iota(jnp.int32, (rows, span), 1)
    first = query - pos_ref[0][:, :1].astype(jnp.int32)
    allowed = (key >= first) & (key <= query)
    scores = jnp.where(allowed[None], scores.reshape(heads, rows, span), NEG_FILL)
    grown = jnp.exp(scores - jnp.max(scores, axis=-1, keepdims=True))
    probs = grown / jnp.sum(grown, axis=-1, keepdims=True)
    probs_ref[0] = probs
    mixed = rows_cols(probs.reshape(heads * rows, span).astype(BF), values)
    mixed = unstack_heads(mixed, rows).astype(BF)
    for to in range(count):
        out_ref[to, 0] = jnp.concatenate(
            [
                mixed[:, at + to * fine : at + (to + 1) * fine]
                for at in range(0, q_cols, count * fine)
            ],
            axis=1,
        )


def attend_back_kernel(
    fine, grad_ref, probs_ref, q_ref, own_ref, halo_ref, cos_ref, sin_ref, q_out, kv_out
):
    rows, q_cols = q_ref.shape[1:]
    heads = q_cols // HD
    count = grad_ref.shape[0]
    kv = jnp.concatenate([halo_ref[0], own_ref[0]], axis=0)
    keys, values = kv[:, :HD], kv[:, HD:]
    span = kv.shape[0]
    grad = jnp.concatenate(
        [
            grad_ref[source, 0][:, at * fine : (at + 1) * fine]
            for at in range(q_cols // (count * fine))
            for source in range(count)
        ],
        axis=1,
    )
    grad = stack_heads(grad)
    probs = probs_ref[0].reshape(heads * rows, span)
    probs_grad = cols_cols(grad, values)
    inner = jnp.sum(probs * probs_grad, axis=-1, keepdims=True)
    score_grad = (probs * (probs_grad - inner)).astype(BF)
    scale = HD**-0.5
    key_grad = rows_rows(score_grad, stack_heads(q_ref[0])) * scale
    value_grad = rows_rows(probs.astype(BF), grad)
    kv_out[0] = jnp.concatenate([key_grad, value_grad], axis=1)
    query_grad = unstack_heads(rows_cols(score_grad, keys) * scale, rows)
    cosine, sine = cos_ref[0], -sin_ref[0]
    for at in range(0, q_cols, LANES):
        q_out[0, :, at : at + LANES] = turn(
            query_grad[:, at : at + LANES], cosine, sine
        ).astype(BF)


def in_back_kernel(
    dq_ref, dkv_ref, back_ref, cos_ref, sin_ref, normed_ref, x_ref, two_ref, w_ref,
    part_ref, grad_ref, total_ref,
):
    at = pl.program_id(0)
    rows = dq_ref.shape[1]
    own = dkv_ref[0, HALO:]
    tail = own[rows - HALO :] + back_ref[0]
    own = jnp.concatenate([own[: rows - HALO], tail], axis=0)
    own = turn_first(own, cos_ref[0], -sin_ref[0]).astype(BF)
    qkv_grad = jnp.concatenate([dq_ref[0], own], axis=1)
    normed_grad = cols_cols(qkv_grad, w_ref[...])
    part_ref[0] = normed_grad.astype(BF)
    x = x_ref[0].astype(F32)
    one = (normed_grad * x * norm_scale(x)).astype(BF)
    cols = qkv_grad.shape[1]
    lane = lax.broadcasted_iota(jnp.int32, (rows, LANES), 1)

    @pl.when(at == 0)
    def _():
        total_ref[:, :cols] = rows_rows(normed_ref[0], qkv_grad)
        total_ref[:, cols:] = rows_rows(one, (lane < HD).astype(BF)) + rows_rows(
            two_ref[...], (lane >= HD).astype(BF)
        )

    @pl.when(at > 0)
    def _():
        total_ref[:, :cols] += rows_rows(normed_ref[0], qkv_grad)
        total_ref[:, cols:] += rows_rows(one, (lane < HD).astype(BF))

    @pl.when(at == pl.num_programs(0) - 1)
    def _():
        grad_ref[...] = total_ref[...].astype(BF)


def middle_kernel(part_ref, x_ref, gain_ref, mid_ref, normed_ref):
    mid = x_ref[...].astype(F32)
    for at in range(part_ref.shape[0]):
        mid += part_ref[at].astype(F32)
    mid_ref[...] = mid
    normed_ref[...] = (mid * norm_scale(mid) * gain_ref[1:2]).astype(BF)


def middle_back_kernel(grad_ref, mid_ref, gain_ref, cot_ref, out_ref, low_ref, gain_out_ref):
    mid = mid_ref[...]
    scale = norm_scale(mid)
    grad = grad_ref[...].astype(F32)
    gain_out_ref[...] = (grad * mid * scale).astype(BF)
    scaled = grad * gain_ref[1:2]
    out = (
        cot_ref[...].astype(F32)
        + scale * scaled
        - mid * scale**3 * jnp.mean(scaled * mid, axis=1, keepdims=True)
    )
    out_ref[...] = out
    low_ref[...] = out.astype(BF)


def last_kernel(part_ref, x_ref, gain_ref, mid_ref, out_ref):
    x = x_ref[...].astype(F32)
    scale = norm_scale(x)
    grad = part_ref[0].astype(F32)
    for at in range(1, part_ref.shape[0]):
        grad += part_ref[at].astype(F32)
    scaled = grad * gain_ref[0:1]
    out = (
        mid_ref[...]
        + scale * scaled
        - x * scale**3 * jnp.mean(scaled * x, axis=1, keepdims=True)
    )
    out_ref[...] = out.astype(BF)


def forward_back_kernel(
    x_ref, cot_ref, pair_ref, down_ref, mixed_ref, gate_out, up_out, part_ref
):
    x = x_ref[...]
    gate = rows_cols(x, pair_ref[0])
    up = rows_cols(x, pair_ref[1])
    mixed_grad = cols_cols(cot_ref[...], down_ref[...])
    sigma = jax.nn.sigmoid(gate)
    silu = gate * sigma
    mixed_ref[...] = (silu * up).astype(BF)
    gate_grad = (mixed_grad * up * sigma * (1.0 + gate * (1.0 - sigma))).astype(BF)
    up_grad = (mixed_grad * silu).astype(BF)
    gate_out[...] = gate_grad
    up_out[...] = up_grad
    part_ref[...] = (
        cols_cols(gate_grad, pair_ref[0]) + cols_cols(up_grad, pair_ref[1])
    ).astype(BF)


def shape(dims, kind):
    return jax.ShapeDtypeStruct(dims, kind)


def call(kernel, out_shape, grid=None, in_specs=None, out_specs=None, scratch=()):
    options = {}
    if grid is not None:
        options = {"grid": grid, "in_specs": in_specs, "out_specs": out_specs}
    return pl.pallas_call(
        kernel,
        out_shape=out_shape,
        scratch_shapes=list(scratch),
        compiler_params=pltpu.CompilerParams(vmem_limit_bytes=56 * 1024 * 1024),
        **options,
    )


def by_block(dims):
    return pl.BlockSpec((1,) + dims, lambda g: (g,) + (0,) * len(dims))


def whole(dims):
    return pl.BlockSpec(dims, lambda g: (0,) * len(dims), pipeline_mode=pl.Buffered(1))


def body(
    n_rep,
    n_shard,
    tokens,
    seq_lengths,
    deal_order,
    attn_gain,
    mlp_gain,
    q_weight,
    k_weight,
    v_weight,
    o_weight,
    gate_weight,
    up_weight,
    down_weight,
    cotangent,
):
    rows, width = tokens.shape
    r = lax.axis_index("rep")
    s = lax.axis_index("shard")
    own = width // n_shard
    fine = own // n_rep
    hidden = down_weight.shape[0]
    q_cols = width // n_rep
    heads = H // n_rep
    pair = n_shard // n_rep
    share = max(n_rep // KVH, 1)
    kv_at = (r * KVH) // n_rep
    all_rows = n_rep * rows
    span = HALO + rows
    qkv_cols = q_cols + 2 * HD

    starts = jnp.cumsum(seq_lengths[0]) - seq_lengths[0]
    places = s * rows + jnp.arange(rows, dtype=jnp.int32)
    first = jnp.max(
        jnp.where(starts[None, :] <= places[:, None], starts[None, :], 0), axis=1, keepdims=True
    )
    offset = jnp.broadcast_to((places[:, None] - first).astype(BF), (rows, LANES))

    w_o_own = lax.dynamic_slice_in_dim(o_weight, r * fine, fine, 0)
    w_own = jnp.concatenate(
        [
            lax.dynamic_slice_in_dim(q_weight, r * q_cols, q_cols, 1),
            lax.dynamic_slice_in_dim(k_weight, kv_at * HD, HD, 1),
            lax.dynamic_slice_in_dim(v_weight, kv_at * HD, HD, 1),
            w_o_own.reshape(fine, n_rep, q_cols).transpose(1, 0, 2).reshape(own, q_cols),
            jnp.broadcast_to(attn_gain[:, None], (own, HD)),
            jnp.broadcast_to(mlp_gain[:, None], (own, LANES - HD)),
        ],
        axis=1,
    )
    w_attn = lax.all_gather(w_own, "shard", axis=0, tiled=True)
    x_all = spread(jnp.concatenate([tokens, offset], axis=1), "rep", n_rep)

    def exchange_shard(pieces):
        rest = [send(pieces[k], "shard", n_shard, k) for k in range(1, n_shard)]
        return [pieces[0]] + rest

    block = (n_shard, fine, hidden)
    ids = jnp.stack([r, s]).astype(jnp.int32)
    w_pair = split_pair(ids, gate_weight, up_weight, fine, n_shard)
    w_pair = exchange_shard(w_pair)
    w_pair = flat_call(order_kernel, ids, (shape(block, BF),) * 2, w_pair)
    w_pair = gather_rep(w_pair, n_rep)
    w_pair = flat_call(
        join_kernel,
        ids,
        shape((2, n_shard, n_rep, fine, hidden), BF),
        [half for piece in w_pair for half in piece],
    ).reshape(2, width, hidden)
    cot_all = lax.all_gather(cotangent, "shard", axis=0, tiled=True)

    half = HD // 2
    inverse = ROPE_BASE ** (-2.0 * (jnp.arange(LANES) % half).astype(F32) / HD)
    angles = x_all[:, :, width:].astype(F32) * inverse[None, None, :]
    cosine, sine = jnp.cos(angles), jnp.sin(angles)
    x_block = by_block((rows, width))
    table = by_block((rows, LANES))
    w_qkv_block = whole((width, qkv_cols))
    normed_one, queries, kv_own, gains = call(
        in_kernel,
        (
            shape((n_rep, rows, width), BF),
            shape((n_rep, rows, q_cols), BF),
            shape((n_rep, rows, LANES), BF),
            shape((8, width), F32),
        ),
        (n_rep,),
        [
            x_block,
            w_qkv_block,
            pl.BlockSpec((width, LANES), lambda g: (0, 2 * qkv_cols // LANES - 1)),
            table,
            table,
        ],
        (x_block, by_block((rows, q_cols)), table, pl.BlockSpec((8, width), lambda g: (0, 0))),
    )(x_all, w_attn, w_attn, cosine, sine)
    kv_halo = lax.ppermute(
        kv_own[:, rows - HALO :], "shard", [(i, i + 1) for i in range(n_shard - 1)]
    )
    head_block = pl.BlockSpec((n_rep, 1, rows, pair * fine), lambda g: (0, g, 0, 0))
    probs_block = by_block((heads, rows, span))
    probs, out_in = call(
        partial(attend_kernel, fine),
        (
            shape((n_rep, heads, rows, span), F32),
            shape((n_rep, n_rep, rows, pair * fine), BF),
        ),
        (n_rep,),
        [
            by_block((rows, q_cols)),
            table,
            by_block((HALO, LANES)),
            pl.BlockSpec((1, rows, LANES), lambda g: (g, 0, width // LANES)),
        ],
        (probs_block, head_block),
    )(queries, kv_own, kv_halo, x_all)
    out_in = swap(out_in, "rep").reshape(n_rep, all_rows, pair * fine)
    w_out = w_attn.reshape(n_shard, n_rep, fine, 2 * qkv_cols)
    w_out_block = pl.BlockSpec((n_shard, 1, fine, qkv_cols), lambda g: (0, g, 0, 1))
    heads_block = whole((n_rep, all_rows, pair * fine))
    mid_part, out_in = call(
        out_kernel,
        (shape((n_rep, rows, width), BF), shape((all_rows, q_cols), BF)),
        (n_rep,),
        [heads_block, w_out_block],
        (
            pl.BlockSpec((n_rep, rows, q_cols), lambda g: (0, 0, g)),
            pl.BlockSpec((all_rows, q_cols), lambda g: (0, 0)),
        ),
    )(out_in, w_out)
    x_mid, normed_two = call(
        middle_kernel, (shape((rows, width), F32), shape((rows, width), BF))
    )(swap(mid_part, "rep"), tokens, gains)

    two_all = lax.all_gather(normed_two, "shard", axis=0, tiled=True)
    step = 256
    group = two_all.shape[0]
    token_block = pl.BlockSpec((step, width), lambda g: (g, 0))
    hidden_block = pl.BlockSpec((step, hidden), lambda g: (g, 0))
    mixed, gate_grad, up_grad, two_grad_part = call(
        forward_back_kernel,
        (shape((group, hidden), BF),) * 3 + (shape((group, width), BF),),
        (group // step,),
        [token_block, token_block, whole((2, width, hidden)), whole((hidden, width))],
        (hidden_block,) * 3 + (token_block,),
    )(two_all, cot_all, w_pair, down_weight)
    two_grad = lax.psum_scatter(two_grad_part, "shard", scatter_dimension=0, tiled=True)
    mid_grad, branch, gain_two_rows = call(
        middle_back_kernel,
        (shape((rows, width), F32), shape((rows, width), BF), shape((rows, width), BF)),
    )(two_grad, x_mid, gains, cotangent)

    gate_chunks = pair_grad(ids, two_all, gate_grad, fine, n_rep, n_shard)
    up_grad, _ = lax.optimization_barrier((up_grad, gate_chunks[0]))
    up_chunks = pair_grad(ids, two_all, up_grad, fine, n_rep, n_shard)
    pair_chunks = list(zip(gate_chunks, up_chunks))
    mixed, _ = lax.optimization_barrier((mixed, up_chunks[0]))
    part_rows = hidden // n_rep
    cut = (part_rows // 2 + 15) // 16 * 16
    w_down_grad = rows_rows(mixed, cot_all).astype(BF)
    mixed, w_down_grad = lax.optimization_barrier((mixed, w_down_grad))
    down_part = rows_cols(mixed, down_weight).astype(BF)
    down_rows = lax.psum_scatter(down_part, "shard", scatter_dimension=0, tiled=True)
    layer_out = (x_mid + down_rows.astype(F32)).astype(BF)
    chunks = []
    for k in range(n_rep):
        at = (r ^ k) * part_rows
        chunks.append(
            (
                lax.dynamic_slice_in_dim(w_down_grad, at, cut, 0),
                lax.dynamic_slice_in_dim(w_down_grad, at + cut, part_rows - cut, 0),
            )
        )
    w_down_grad = parts_rep(chunks, n_rep)
    w_down_grad = tuple(
        sum(part.astype(F32) for part in parts).astype(BF) for parts in w_down_grad
    )
    down_out = place(gather_rep(w_down_grad, n_rep), r)
    w_pair_grad = parts_rep(pair_chunks, n_rep)
    w_pair_grad = flat_call(
        sum_kernel,
        ids,
        (shape((2, fine, hidden), BF),) * n_shard,
        w_pair_grad[0] + w_pair_grad[1],
    )
    w_pair_grad = exchange_shard(w_pair_grad)
    w_pair_grad = flat_call(
        widen_kernel,
        ids,
        (shape((fine, n_shard * hidden), BF),) * 2,
        w_pair_grad,
        [pltpu.VMEM((n_shard, 2, fine, hidden), BF)],
    )
    w_pair_grad = gather_rep(w_pair_grad, n_rep)
    gate_out = place([piece[:1] for piece in w_pair_grad], r)
    up_out = place([piece[1:] for piece in w_pair_grad], r)

    branch_all = spread(branch, "rep", n_rep).reshape(all_rows, width)
    in_grad = call(
        out_back_kernel,
        shape((n_rep, all_rows, pair * fine), BF),
        (n_rep,),
        [pl.BlockSpec((all_rows, q_cols), lambda g: (0, g)), w_out_block],
        pl.BlockSpec((n_rep, all_rows, pair * fine), lambda g: (0, 0, 0)),
        [pltpu.VMEM((all_rows, q_cols), F32)],
    )(branch_all, w_out)
    branch_all, in_grad = lax.optimization_barrier((branch_all, in_grad))
    in_grad = swap(in_grad, "rep").reshape(n_rep, n_rep, rows, pair * fine)
    w_o_grad = rows_rows(out_in, branch_all).astype(BF)
    w_o_grad = lax.psum_scatter(w_o_grad, "shard", scatter_dimension=0, tiled=True)
    o_out = place([(v,) for v in gather_direct(w_o_grad, n_rep)], r)
    query_grad, kv_grad = call(
        partial(attend_back_kernel, fine),
        (shape((n_rep, rows, q_cols), BF), shape((n_rep, span, LANES), F32)),
        (n_rep,),
        [
            head_block,
            probs_block,
            by_block((rows, q_cols)),
            table,
            by_block((HALO, LANES)),
            table,
            table,
        ],
        (by_block((rows, q_cols)), by_block((span, LANES))),
    )(in_grad, probs, queries, kv_own, kv_halo, cosine, sine)
    kv_back = lax.ppermute(
        kv_grad[:, :HALO], "shard", [(i + 1, i) for i in range(n_shard - 1)]
    )
    grad_cols = qkv_cols + LANES
    one_grad_part, w_qkv_grad = call(
        in_back_kernel,
        (shape((n_rep, rows, width), BF), shape((width, grad_cols), BF)),
        (n_rep,),
        [
            by_block((rows, q_cols)),
            by_block((span, LANES)),
            by_block((HALO, LANES)),
            table,
            table,
            x_block,
            x_block,
            whole((rows, width)),
            w_qkv_block,
        ],
        (x_block, pl.BlockSpec((width, grad_cols), lambda g: (0, 0))),
        [pltpu.VMEM((width, grad_cols), F32)],
    )(
        query_grad, kv_grad, kv_back, cosine, sine, normed_one, x_all, gain_two_rows, w_attn
    )
    w_qkv_grad = lax.psum_scatter(w_qkv_grad, "shard", scatter_dimension=0, tiled=True)
    input_grad = call(last_kernel, shape((rows, width), BF))(
        swap(one_grad_part, "rep"), tokens, gains, mid_grad
    )
    q_out, k_out, v_out, gain_sums = flat_call(
        partial(qkv_kernel, share),
        ids,
        (
            shape((own, width), F32),
            shape((own, KVH * HD), F32),
            shape((own, KVH * HD), F32),
            shape((own, LANES), F32),
        ),
        gather_direct(w_qkv_grad, n_rep),
        [pltpu.VMEM((n_rep, own, HD), F32)] * 2,
    )
    return (
        layer_out,
        input_grad,
        gain_sums[:, 0],
        gain_sums[:, HD],
        q_out,
        k_out,
        v_out,
        o_out,
        gate_out,
        up_out,
        down_out,
    )


def solution(mesh):
    split = P("shard", None)
    by_token = P(("rep", "shard"), None)
    return jax.shard_map(
        partial(body, mesh.shape["rep"], mesh.shape["shard"]),
        mesh=mesh,
        in_specs=(by_token, P("rep", None), P("rep", None), P("shard"), P("shard"))
        + (split,) * 7
        + (by_token,),
        out_specs=(by_token, by_token, P("shard"), P("shard")) + (split,) * 7,
        check_vma=False,
    )
```

```python
from functools import partial

import jax
import jax.numpy as jnp
from jax import lax
from jax.experimental import pallas as pl
from jax.experimental.pallas import tpu as pltpu
from jax.sharding import PartitionSpec as P


H = 32
KVH = 4
HD = 64
HALO = 64
LANES = 128

EPSILON = 1e-05
ROPE_BASE = 10000.0
NEG_FILL = -1e30

BF = jnp.bfloat16
F32 = jnp.float32


def dot(left, right, contract):
    return lax.dot_general(left, right, (contract, ((), ())), preferred_element_type=F32)


def rows_cols(left, right):
    return dot(left, right, ((1,), (0,)))


def rows_rows(left, right):
    return dot(left, right, ((0,), (0,)))


def cols_cols(left, right):
    return dot(left, right, ((1,), (1,)))


def spread(value, axis, count):
    wide = jnp.broadcast_to(value[None], (count,) + value.shape)
    return lax.all_to_all(wide, axis, split_axis=0, concat_axis=0, tiled=True)


def swap(value, axis):
    return lax.all_to_all(value, axis, split_axis=0, concat_axis=0, tiled=True)


def pairs(count, step):
    return [(i, i ^ step) for i in range(count)]


def send(value, axis, count, step):
    return lax.ppermute(value, axis, pairs(count, step))


def parts_rep(chunks, count):
    go = lambda value, step: send(value, "rep", count, step)
    if count != 4:
        return [[chunks[0][h]] + [go(chunks[k][h], k) for k in range(1, count)] for h in range(2)]
    add = lambda left, right: (left.astype(F32) + right.astype(F32)).astype(BF)
    first_one = go(chunks[1][0], 1)
    first_two = go(chunks[3][0], 1)
    second_one = go(chunks[2][1], 2)
    second_two = go(chunks[3][1], 2)
    last_one = go(add(chunks[2][0], first_two), 2)
    last_two = go(add(chunks[1][1], second_two), 1)
    return [[chunks[0][0], first_one, last_one], [chunks[0][1], second_one, last_two]]


def gather_direct(value, count):
    return [value] + [send(value, "rep", count, k) for k in range(1, count)]


def gather_rep(halves, count):
    go = lambda value, step: send(value, "rep", count, step)
    if count != 4:
        return [halves] + [tuple(go(v, k) for v in halves) for k in range(1, count)]
    one = tuple(go(v, 1) for v in halves)
    two = tuple(go(v, 2) for v in halves)
    return [halves, one, two, (go(one[0], 2), go(two[1], 1))]


def place_kernel(count, me_ref, *refs):
    parts, out_ref = refs[:-1], refs[-1]
    at = pl.program_id(0)
    size = len(parts) // count
    for k in range(count):

        @pl.when(at == jnp.bitwise_xor(me_ref[0], k))
        def _(k=k):
            row = 0
            for part in parts[k * size : (k + 1) * size]:
                out_ref[0, row : row + part.shape[0]] = part[...].astype(F32)
                row += part.shape[0]


def place(pieces, me):
    count = len(pieces)
    flat = [part for piece in pieces for part in piece]
    rows = sum(part.shape[0] for part in pieces[0])
    width = flat[0].shape[1]
    grid = pltpu.PrefetchScalarGridSpec(
        num_scalar_prefetch=1,
        grid=(count,),
        in_specs=[
            pl.BlockSpec(part.shape, lambda g, me: (0, 0), pipeline_mode=pl.Buffered(1))
            for part in flat
        ],
        out_specs=pl.BlockSpec((1, rows, width), lambda g, me: (g, 0, 0)),
    )
    return pl.pallas_call(
        partial(place_kernel, count),
        out_shape=shape((count, rows, width), F32),
        grid_spec=grid,
        compiler_params=pltpu.CompilerParams(vmem_limit_bytes=56 * 1024 * 1024),
    )(me.astype(jnp.int32).reshape(1), *flat).reshape(count * rows, width)


def split_kernel(id_ref, gate_ref, up_ref, *refs):
    outs, both = refs[:-1], refs[-1]
    hidden = both.shape[3]
    for h, ref in enumerate((gate_ref, up_ref)):
        value = ref[...]
        for at in range(len(outs)):
            both[at, h] = value[:, at * hidden : (at + 1) * hidden]
    for k, out in enumerate(outs):
        out[...] = both[jnp.bitwise_xor(id_ref[1], k)]


def split_pair(ids, gate, up, fine, count):
    hidden = gate.shape[1] // count
    rows = pl.BlockSpec((fine, gate.shape[1]), lambda g, ids: (ids[0], 0))
    piece = (2, fine, hidden)
    return pl.pallas_call(
        split_kernel,
        out_shape=(shape(piece, BF),) * count,
        grid_spec=pltpu.PrefetchScalarGridSpec(
            num_scalar_prefetch=1,
            grid=(1,),
            in_specs=[rows, rows],
            out_specs=(pl.BlockSpec(piece, lambda g, ids: (0, 0, 0)),) * count,
            scratch_shapes=[pltpu.VMEM((count,) + piece, BF)],
        ),
        name="split_pair",
    )(ids, gate, up)


def flat_call(kernel, ids, out_shape, values, scratch=()):
    specs = [pl.BlockSpec(memory_space=pltpu.SMEM)]
    specs += [pl.BlockSpec(memory_space=pltpu.VMEM)] * len(values)
    return pl.pallas_call(
        kernel,
        out_shape=out_shape,
        in_specs=specs,
        scratch_shapes=list(scratch),
        compiler_params=pltpu.CompilerParams(vmem_limit_bytes=56 * 1024 * 1024),
    )(ids, *values)


def order_kernel(id_ref, *refs):
    pieces, (gate_ref, up_ref) = refs[:-2], refs[-2:]
    for k, piece in enumerate(pieces):
        at = jnp.bitwise_xor(id_ref[1], k)
        gate_ref[at] = piece[0]
        up_ref[at] = piece[1]


def join_kernel(id_ref, *refs):
    out_ref = refs[-1]
    for k in range(len(refs) // 2):
        at = jnp.bitwise_xor(id_ref[0], k)
        for h in range(2):
            value = refs[2 * k + h]
            for row in range(value.shape[0]):
                out_ref[h, row, at] = value[row]


def sum_kernel(id_ref, *refs):
    count = refs[0].shape[0]
    outs = refs[len(refs) - count :]
    parts = refs[: len(refs) - count]
    half = len(parts) // 2
    for k, out in enumerate(outs):
        at = jnp.bitwise_xor(id_ref[1], k)
        for h in range(2):
            total = parts[h * half][at].astype(F32)
            for part in parts[h * half + 1 : (h + 1) * half]:
                total += part[at].astype(F32)
            out[h] = total.astype(BF)


def widen_kernel(id_ref, *refs):
    pieces, (gate_ref, up_ref, both) = refs[:-3], refs[-3:]
    hidden = both.shape[3]
    for k, piece in enumerate(pieces):
        both[jnp.bitwise_xor(id_ref[1], k)] = piece[...]
    for h, ref in enumerate((gate_ref, up_ref)):
        for at in range(len(pieces)):
            ref[:, at * hidden : (at + 1) * hidden] = both[at, h]


def qkv_kernel(share, id_ref, *refs):
    pieces = refs[:-6]
    q_ref, k_ref, v_ref, gain_ref, k_all, v_all = refs[-6:]
    count = k_all.shape[0]
    q_cols = q_ref.shape[1] // count
    total = 0.0
    for k, piece in enumerate(pieces):
        at = jnp.bitwise_xor(id_ref[0], k)
        value = piece[...].astype(F32)
        q_ref[:, pl.ds(pl.multiple_of(at * q_cols, LANES), q_cols)] = value[:, :q_cols]
        k_all[at] = value[:, q_cols : q_cols + HD]
        v_all[at] = value[:, q_cols + HD : q_cols + 2 * HD]
        total += value[:, q_cols + 2 * HD :]
    gain_ref[...] = total
    for ref, both in ((k_ref, k_all), (v_ref, v_all)):
        for head in range(count // share):
            total = both[head * share]
            for other in range(head * share + 1, (head + 1) * share):
                total += both[other]
            ref[:, head * HD : (head + 1) * HD] = total


def pair_grad_kernel(fine, id_ref, x_ref, grad_ref, *refs):
    outs, total_ref = refs[:-1], refs[-1]
    total_ref[...] = rows_rows(x_ref[...], grad_ref[...])
    own = fine * len(outs)
    for k, out in enumerate(outs):
        row = jnp.bitwise_xor(id_ref[0], k) * fine
        for block in range(out.shape[0]):
            at = pl.multiple_of(block * own + row, fine)
            out[block] = total_ref[pl.ds(at, fine)].astype(BF)


def pair_grad(ids, x, grad, fine, count, blocks):
    width, hidden = x.shape[1], grad.shape[1]
    tile = 2 * fine * count
    out = (2, fine, hidden)
    return pl.pallas_call(
        partial(pair_grad_kernel, fine),
        out_shape=(shape((blocks, fine, hidden), BF),) * count,
        grid_spec=pltpu.PrefetchScalarGridSpec(
            num_scalar_prefetch=1,
            grid=(width // tile,),
            in_specs=[
                pl.BlockSpec((x.shape[0], tile), lambda g, ids: (0, g)),
                pl.BlockSpec(grad.shape, lambda g, ids: (0, 0), pipeline_mode=pl.Buffered(1)),
            ],
            out_specs=(pl.BlockSpec(out, lambda g, ids: (g, 0, 0)),) * count,
            scratch_shapes=[pltpu.VMEM((tile, hidden), F32)],
        ),
        compiler_params=pltpu.CompilerParams(vmem_limit_bytes=56 * 1024 * 1024),
    )(ids, x, grad)


def down_grad_kernel(id_ref, mixed_ref, cot_ref, *refs):
    outs, total_ref = refs[:-1], refs[-1]
    total_ref[...] = rows_rows(mixed_ref[...], cot_ref[...])
    rows = total_ref.shape[0] // (len(outs) // 2)
    for k in range(len(outs) // 2):
        at = jnp.bitwise_xor(id_ref[0], k) * rows
        for h in range(2):
            out = outs[2 * k + h]
            start = at + h * outs[0].shape[0]
            out[...] = total_ref[pl.ds(pl.multiple_of(start, 16), out.shape[0])].astype(BF)


def down_grad(ids, mixed, cot, cut, count):
    hidden, width = mixed.shape[1], cot.shape[1]
    rest = hidden // count - cut
    tile = width // 2
    heights = (cut, rest) * count
    outs = pl.pallas_call(
        down_grad_kernel,
        out_shape=tuple(shape((rows, width), BF) for rows in heights),
        grid_spec=pltpu.PrefetchScalarGridSpec(
            num_scalar_prefetch=1,
            grid=(width // tile,),
            in_specs=[
                pl.BlockSpec(mixed.shape, lambda g, ids: (0, 0), pipeline_mode=pl.Buffered(1)),
                pl.BlockSpec((cot.shape[0], tile), lambda g, ids: (0, g)),
            ],
            out_specs=tuple(pl.BlockSpec((rows, tile), lambda g, ids: (0, g)) for rows in heights),
            scratch_shapes=[pltpu.VMEM((hidden, tile), F32)],
        ),
        name="down_grad",
        compiler_params=pltpu.CompilerParams(vmem_limit_bytes=56 * 1024 * 1024),
    )(ids, mixed, cot)
    return list(zip(outs[0::2], outs[1::2]))


def norm_scale(value):
    return lax.rsqrt(jnp.mean(value * value, axis=1, keepdims=True) + EPSILON)


def turn(tile, cosine, sine):
    lane = lax.broadcasted_iota(jnp.int32, tile.shape, 1)
    swapped = jnp.where(
        lane % HD < HD // 2,
        -pltpu.roll(tile, LANES - HD // 2, 1),
        pltpu.roll(tile, HD // 2, 1),
    )
    return tile * cosine + swapped * sine


def turn_first(tile, cosine, sine):
    lane = lax.broadcasted_iota(jnp.int32, tile.shape, 1)
    return jnp.where(lane < HD, turn(tile, cosine, sine), tile)


def in_kernel(x_ref, gain_ref, w_ref, cos_ref, sin_ref, normed_ref, q_ref, kv_ref):
    x = x_ref[0].astype(F32)
    normed = (x * norm_scale(x) * gain_ref[...]).astype(BF)
    normed_ref[0] = normed
    qkv = rows_cols(normed, w_ref[...])
    cosine, sine = cos_ref[0], sin_ref[0]
    q_cols = q_ref.shape[2]
    for at in range(0, q_cols, LANES):
        q_ref[0, :, at : at + LANES] = turn(qkv[:, at : at + LANES], cosine, sine).astype(BF)
    kv_ref[0] = turn_first(qkv[:, q_cols:], cosine, sine).astype(BF)


def stack_heads(value):
    return jnp.concatenate(
        [value[:, at : at + HD] for at in range(0, value.shape[1], HD)], axis=0
    )


def unstack_heads(value, rows):
    return jnp.concatenate(
        [value[at : at + rows] for at in range(0, value.shape[0], rows)], axis=1
    )


def attend_kernel(fine, q_ref, own_ref, halo_ref, pos_ref, probs_ref, out_ref):
    rows, q_cols = q_ref.shape[1:]
    heads = q_cols // HD
    count = out_ref.shape[0]
    kv = jnp.concatenate([halo_ref[0], own_ref[0]], axis=0)
    keys, values = kv[:, :HD], kv[:, HD:]
    span = kv.shape[0]
    scores = cols_cols(stack_heads(q_ref[0]), keys) * (HD**-0.5)
    query = lax.broadcasted_iota(jnp.int32, (rows, span), 0) + HALO
    key = lax.broadcasted_iota(jnp.int32, (rows, span), 1)
    first = query - pos_ref[0][:, :1].astype(jnp.int32)
    allowed = (key >= first) & (key <= query)
    scores = jnp.where(allowed[None], scores.reshape(heads, rows, span), NEG_FILL)
    grown = jnp.exp(scores - jnp.max(scores, axis=-1, keepdims=True))
    probs = grown / jnp.sum(grown, axis=-1, keepdims=True)
    probs_ref[0] = probs
    mixed = rows_cols(probs.reshape(heads * rows, span).astype(BF), values)
    mixed = unstack_heads(mixed, rows).astype(BF)
    for to in range(count):
        out_ref[to, 0] = jnp.concatenate(
            [
                mixed[:, at + to * fine : at + (to + 1) * fine]
                for at in range(0, q_cols, count * fine)
            ],
            axis=1,
        )


def attend_back_kernel(
    fine, grad_ref, probs_ref, q_ref, own_ref, halo_ref, cos_ref, sin_ref, q_out, kv_out
):
    rows, q_cols = q_ref.shape[1:]
    heads = q_cols // HD
    count = grad_ref.shape[0]
    kv = jnp.concatenate([halo_ref[0], own_ref[0]], axis=0)
    keys, values = kv[:, :HD], kv[:, HD:]
    span = kv.shape[0]
    grad = jnp.concatenate(
        [
            grad_ref[source, 0][:, at * fine : (at + 1) * fine]
            for at in range(q_cols // (count * fine))
            for source in range(count)
        ],
        axis=1,
    )
    grad = stack_heads(grad)
    probs = probs_ref[0].reshape(heads * rows, span)
    probs_grad = cols_cols(grad, values)
    inner = jnp.sum(probs * probs_grad, axis=-1, keepdims=True)
    score_grad = (probs * (probs_grad - inner)).astype(BF)
    scale = HD**-0.5
    key_grad = rows_rows(score_grad, stack_heads(q_ref[0])) * scale
    value_grad = rows_rows(probs.astype(BF), grad)
    kv_out[0] = jnp.concatenate([key_grad, value_grad], axis=1)
    query_grad = unstack_heads(rows_cols(score_grad, keys) * scale, rows)
    cosine, sine = cos_ref[0], -sin_ref[0]
    for at in range(0, q_cols, LANES):
        q_out[0, :, at : at + LANES] = turn(
            query_grad[:, at : at + LANES], cosine, sine
        ).astype(BF)


def in_back_kernel(
    dq_ref, dkv_ref, back_ref, cos_ref, sin_ref, normed_ref, x_ref, two_ref, w_ref,
    part_ref, grad_ref, total_ref,
):
    at = pl.program_id(0)
    rows = dq_ref.shape[1]
    own = dkv_ref[0, HALO:]
    tail = own[rows - HALO :] + back_ref[0]
    own = jnp.concatenate([own[: rows - HALO], tail], axis=0)
    own = turn_first(own, cos_ref[0], -sin_ref[0]).astype(BF)
    qkv_grad = jnp.concatenate([dq_ref[0], own], axis=1)
    normed_grad = cols_cols(qkv_grad, w_ref[...])
    part_ref[0] = normed_grad.astype(BF)
    x = x_ref[0].astype(F32)
    one = (normed_grad * x * norm_scale(x)).astype(BF)
    cols = qkv_grad.shape[1]
    lane = lax.broadcasted_iota(jnp.int32, (rows, LANES), 1)

    @pl.when(at == 0)
    def _():
        total_ref[:, :cols] = rows_rows(normed_ref[0], qkv_grad)
        total_ref[:, cols:] = rows_rows(one, (lane < HD).astype(BF)) + rows_rows(
            two_ref[...], (lane >= HD).astype(BF)
        )

    @pl.when(at > 0)
    def _():
        total_ref[:, :cols] += rows_rows(normed_ref[0], qkv_grad)
        total_ref[:, cols:] += rows_rows(one, (lane < HD).astype(BF))

    @pl.when(at == pl.num_programs(0) - 1)
    def _():
        grad_ref[...] = total_ref[...].astype(BF)


def middle_kernel(part_ref, x_ref, gain_ref, mid_ref, normed_ref):
    mid = x_ref[...].astype(F32)
    for at in range(part_ref.shape[0]):
        mid += part_ref[at].astype(F32)
    mid_ref[...] = mid
    normed_ref[...] = (mid * norm_scale(mid) * gain_ref[...]).astype(BF)


def middle_back_kernel(grad_ref, mid_ref, gain_ref, cot_ref, out_ref, low_ref, gain_out_ref):
    mid = mid_ref[...]
    scale = norm_scale(mid)
    grad = grad_ref[...].astype(F32)
    gain_out_ref[...] = (grad * mid * scale).astype(BF)
    scaled = grad * gain_ref[...]
    out = (
        cot_ref[...].astype(F32)
        + scale * scaled
        - mid * scale**3 * jnp.mean(scaled * mid, axis=1, keepdims=True)
    )
    out_ref[...] = out
    low_ref[...] = out.astype(BF)


def last_kernel(part_ref, x_ref, gain_ref, mid_ref, out_ref):
    x = x_ref[...].astype(F32)
    scale = norm_scale(x)
    grad = part_ref[0].astype(F32)
    for at in range(1, part_ref.shape[0]):
        grad += part_ref[at].astype(F32)
    scaled = grad * gain_ref[...]
    out = (
        mid_ref[...]
        + scale * scaled
        - x * scale**3 * jnp.mean(scaled * x, axis=1, keepdims=True)
    )
    out_ref[...] = out.astype(BF)


def forward_kernel(x_ref, back_ref, pair_ref, mixed_ref, gate_out, up_out):
    x = x_ref[...]
    gate = rows_cols(x, pair_ref[0])
    up = rows_cols(x, pair_ref[1])
    mixed_grad = back_ref[...]
    sigma = jax.nn.sigmoid(gate)
    silu = gate * sigma
    mixed_ref[...] = (silu * up).astype(BF)
    gate_out[...] = (mixed_grad * up * sigma * (1.0 + gate * (1.0 - sigma))).astype(BF)
    up_out[...] = (mixed_grad * silu).astype(BF)


def back_kernel(gate_ref, up_ref, pair_ref, part_ref):
    part_ref[...] = (
        cols_cols(gate_ref[...], pair_ref[0]) + cols_cols(up_ref[...], pair_ref[1])
    ).astype(BF)


def shape(dims, kind):
    return jax.ShapeDtypeStruct(dims, kind)


def call(kernel, out_shape, grid=None, in_specs=None, out_specs=None, scratch=()):
    options = {}
    if grid is not None:
        options = {"grid": grid, "in_specs": in_specs, "out_specs": out_specs}
    return pl.pallas_call(
        kernel,
        out_shape=out_shape,
        scratch_shapes=list(scratch),
        compiler_params=pltpu.CompilerParams(vmem_limit_bytes=56 * 1024 * 1024),
        **options,
    )


def by_block(dims):
    return pl.BlockSpec((1,) + dims, lambda g: (g,) + (0,) * len(dims))


def whole(dims):
    return pl.BlockSpec(dims, lambda g: (0,) * len(dims), pipeline_mode=pl.Buffered(1))


def body(
    n_rep,
    n_shard,
    tokens,
    seq_lengths,
    deal_order,
    attn_gain,
    mlp_gain,
    q_weight,
    k_weight,
    v_weight,
    o_weight,
    gate_weight,
    up_weight,
    down_weight,
    cotangent,
):
    rows, width = tokens.shape
    r = lax.axis_index("rep")
    s = lax.axis_index("shard")
    own = width // n_shard
    fine = own // n_rep
    hidden = down_weight.shape[0]
    q_cols = width // n_rep
    heads = H // n_rep
    pair = n_shard // n_rep
    share = max(n_rep // KVH, 1)
    kv_at = (r * KVH) // n_rep
    all_rows = n_rep * rows
    span = HALO + rows
    qkv_cols = q_cols + 2 * HD

    starts = jnp.cumsum(seq_lengths[0]) - seq_lengths[0]
    places = s * rows + jnp.arange(rows, dtype=jnp.int32)
    first = jnp.max(
        jnp.where(starts[None, :] <= places[:, None], starts[None, :], 0), axis=1, keepdims=True
    )
    offset = jnp.broadcast_to((places[:, None] - first).astype(BF), (rows, LANES))

    w_qkv_own = jnp.concatenate(
        [
            lax.dynamic_slice_in_dim(q_weight, r * q_cols, q_cols, 1),
            lax.dynamic_slice_in_dim(k_weight, kv_at * HD, HD, 1),
            lax.dynamic_slice_in_dim(v_weight, kv_at * HD, HD, 1),
        ],
        axis=1,
    )
    w_qkv = lax.all_gather(w_qkv_own, "shard", axis=0, tiled=True)
    w_o = lax.all_gather(
        lax.dynamic_slice_in_dim(o_weight, r * fine, fine, 0), "shard", axis=0, tiled=True
    )
    x_all = spread(jnp.concatenate([tokens, offset], axis=1), "rep", n_rep)
    gains = lax.all_gather(jnp.stack([attn_gain, mlp_gain]), "shard", axis=1, tiled=True)
    gain_one = gains[0:1].astype(F32)
    gain_two = gains[1:2].astype(F32)

    def exchange_shard(pieces):
        rest = [send(pieces[k], "shard", n_shard, k) for k in range(1, n_shard)]
        return [pieces[0]] + rest

    block = (n_shard, fine, hidden)
    ids = jnp.stack([r, s]).astype(jnp.int32)
    gate_tied, up_tied, _ = lax.optimization_barrier((gate_weight, up_weight, gains))
    w_pair = split_pair(ids, gate_tied, up_tied, fine, n_shard)
    w_pair = exchange_shard(w_pair)
    w_pair = flat_call(order_kernel, ids, (shape(block, BF),) * 2, w_pair)
    w_pair = gather_rep(w_pair, n_rep)
    w_pair = flat_call(
        join_kernel,
        ids,
        shape((2, n_shard, n_rep, fine, hidden), BF),
        [half for piece in w_pair for half in piece],
    ).reshape(2, width, hidden)
    cot_all = lax.all_gather(cotangent, "shard", axis=0, tiled=True)

    half = HD // 2
    inverse = ROPE_BASE ** (-2.0 * (jnp.arange(LANES) % half).astype(F32) / HD)
    angles = x_all[:, :, width:].astype(F32) * inverse[None, None, :]
    cosine, sine = jnp.cos(angles), jnp.sin(angles)
    x_block = by_block((rows, width))
    table = by_block((rows, LANES))
    normed_one, queries, kv_own = call(
        in_kernel,
        (
            shape((n_rep, rows, width), BF),
            shape((n_rep, rows, q_cols), BF),
            shape((n_rep, rows, LANES), BF),
        ),
        (n_rep,),
        [x_block, whole((1, width)), whole((width, qkv_cols)), table, table],
        (x_block, by_block((rows, q_cols)), table),
    )(x_all, gain_one, w_qkv, cosine, sine)
    kv_halo = lax.ppermute(
        kv_own[:, rows - HALO :], "shard", [(i, i + 1) for i in range(n_shard - 1)]
    )
    head_block = pl.BlockSpec((n_rep, 1, rows, pair * fine), lambda g: (0, g, 0, 0))
    probs_block = by_block((heads, rows, span))
    probs, out_in = call(
        partial(attend_kernel, fine),
        (
            shape((n_rep, heads, rows, span), F32),
            shape((n_rep, n_rep, rows, pair * fine), BF),
        ),
        (n_rep,),
        [
            by_block((rows, q_cols)),
            table,
            by_block((HALO, LANES)),
            pl.BlockSpec((1, rows, LANES), lambda g: (g, 0, width // LANES)),
        ],
        (probs_block, head_block),
    )(queries, kv_own, kv_halo, x_all)
    out_in = swap(out_in, "rep").reshape(n_rep, all_rows, pair * fine)
    out_in = out_in.transpose(1, 0, 2).reshape(all_rows, q_cols)
    mid_part = rows_cols(out_in, w_o).astype(BF).reshape(n_rep, rows, width)
    x_mid, normed_two = call(
        middle_kernel, (shape((rows, width), F32), shape((rows, width), BF))
    )(swap(mid_part, "rep"), tokens, gain_two)

    two_all = lax.all_gather(normed_two, "shard", axis=0, tiled=True)
    mixed_grad = cols_cols(cot_all, down_weight)
    step = 256
    group = two_all.shape[0]
    token_block = pl.BlockSpec((step, width), lambda g: (g, 0))
    hidden_block = pl.BlockSpec((step, hidden), lambda g: (g, 0))
    mixed, gate_grad, up_grad = call(
        forward_kernel,
        (shape((group, hidden), BF),) * 3,
        (group // step,),
        [token_block, hidden_block, whole((2, width, hidden))],
        (hidden_block,) * 3,
    )(two_all, mixed_grad, w_pair)
    part_rows = hidden // n_rep
    cut = (part_rows // 2 + 15) // 16 * 16
    if part_rows % 16:
        whole_grad = rows_rows(mixed, cot_all).astype(BF)
        down_chunks = []
        for k in range(n_rep):
            part = lax.dynamic_slice_in_dim(whole_grad, (r ^ k) * part_rows, part_rows, 0)
            down_chunks.append((part[:cut], part[cut:]))
    else:
        down_chunks = down_grad(ids, mixed, cot_all, cut, n_rep)
    gate_tied, _ = lax.optimization_barrier((gate_grad, down_chunks[0][0]))
    two_grad_part = call(
        back_kernel,
        shape((group, width), BF),
        (group // step,),
        [hidden_block, hidden_block, whole((2, width, hidden))],
        token_block,
    )(gate_tied, up_grad, w_pair)
    gate_grad, _ = lax.optimization_barrier((gate_grad, two_grad_part))
    two_grad = lax.psum_scatter(two_grad_part, "shard", scatter_dimension=0, tiled=True)
    mid_grad, branch, gain_two_rows = call(
        middle_back_kernel,
        (shape((rows, width), F32), shape((rows, width), BF), shape((rows, width), BF)),
    )(two_grad, x_mid, gain_two, cotangent)

    gate_chunks = pair_grad(ids, two_all, gate_grad, fine, n_rep, n_shard)
    up_grad, _ = lax.optimization_barrier((up_grad, gate_chunks[0]))
    up_chunks = pair_grad(ids, two_all, up_grad, fine, n_rep, n_shard)
    pair_chunks = list(zip(gate_chunks, up_chunks))
    mixed, _ = lax.optimization_barrier((mixed, up_chunks[0]))
    down_part = rows_cols(mixed, down_weight).astype(BF)
    down_rows = lax.psum_scatter(down_part, "shard", scatter_dimension=0, tiled=True)
    layer_out = (x_mid + down_rows.astype(F32)).astype(BF)
    w_down_grad = parts_rep(down_chunks, n_rep)
    w_down_grad = tuple(
        sum(part.astype(F32) for part in parts).astype(BF) for parts in w_down_grad
    )
    down_out = place(gather_rep(w_down_grad, n_rep), r)
    w_pair_grad = parts_rep(pair_chunks, n_rep)
    w_pair_grad = flat_call(
        sum_kernel, ids, (shape((2, fine, hidden), BF),) * n_shard, w_pair_grad[0] + w_pair_grad[1]
    )
    w_pair_grad = exchange_shard(w_pair_grad)
    w_pair_grad = flat_call(
        widen_kernel,
        ids,
        (shape((fine, n_shard * hidden), BF),) * 2,
        w_pair_grad,
        [pltpu.VMEM((n_shard, 2, fine, hidden), BF)],
    )
    w_pair_grad = gather_rep(w_pair_grad, n_rep)
    gate_out = place([piece[:1] for piece in w_pair_grad], r)
    up_out = place([piece[1:] for piece in w_pair_grad], r)

    branch_all = spread(branch, "rep", n_rep).reshape(all_rows, width)
    in_grad = cols_cols(branch_all, w_o).astype(BF)
    branch_all, in_grad = lax.optimization_barrier((branch_all, in_grad))
    in_grad = in_grad.reshape(all_rows, n_rep, pair * fine).transpose(1, 0, 2)
    in_grad = swap(in_grad, "rep").reshape(n_rep, n_rep, rows, pair * fine)
    w_o_grad = rows_rows(out_in, branch_all).astype(BF)
    w_o_grad = lax.psum_scatter(w_o_grad, "shard", scatter_dimension=0, tiled=True)
    o_out = place([(v,) for v in gather_direct(w_o_grad, n_rep)], r)
    query_grad, kv_grad = call(
        partial(attend_back_kernel, fine),
        (shape((n_rep, rows, q_cols), BF), shape((n_rep, span, LANES), F32)),
        (n_rep,),
        [
            head_block,
            probs_block,
            by_block((rows, q_cols)),
            table,
            by_block((HALO, LANES)),
            table,
            table,
        ],
        (by_block((rows, q_cols)), by_block((span, LANES))),
    )(in_grad, probs, queries, kv_own, kv_halo, cosine, sine)
    kv_back = lax.ppermute(
        kv_grad[:, :HALO], "shard", [(i + 1, i) for i in range(n_shard - 1)]
    )
    grad_cols = qkv_cols + LANES
    one_grad_part, w_qkv_grad = call(
        in_back_kernel,
        (shape((n_rep, rows, width), BF), shape((width, grad_cols), BF)),
        (n_rep,),
        [
            by_block((rows, q_cols)),
            by_block((span, LANES)),
            by_block((HALO, LANES)),
            table,
            table,
            x_block,
            x_block,
            whole((rows, width)),
            whole((width, qkv_cols)),
        ],
        (x_block, pl.BlockSpec((width, grad_cols), lambda g: (0, 0))),
        [pltpu.VMEM((width, grad_cols), F32)],
    )(
        query_grad, kv_grad, kv_back, cosine, sine, normed_one, x_all, gain_two_rows, w_qkv
    )
    w_qkv_grad = lax.psum_scatter(w_qkv_grad, "shard", scatter_dimension=0, tiled=True)
    input_grad = call(last_kernel, shape((rows, width), BF))(
        swap(one_grad_part, "rep"), tokens, gain_one, mid_grad
    )
    q_out, k_out, v_out, gain_sums = flat_call(
        partial(qkv_kernel, share),
        ids,
        (
            shape((own, width), F32),
            shape((own, KVH * HD), F32),
            shape((own, KVH * HD), F32),
            shape((own, LANES), F32),
        ),
        gather_direct(w_qkv_grad, n_rep),
        [pltpu.VMEM((n_rep, own, HD), F32)] * 2,
    )
    return (
        layer_out,
        input_grad,
        gain_sums[:, 0],
        gain_sums[:, HD],
        q_out,
        k_out,
        v_out,
        o_out,
        gate_out,
        up_out,
        down_out,
    )


def solution(mesh):
    split = P("shard", None)
    by_token = P(("rep", "shard"), None)
    return jax.shard_map(
        partial(body, mesh.shape["rep"], mesh.shape["shard"]),
        mesh=mesh,
        in_specs=(by_token, P("rep", None), P("rep", None), P("shard"), P("shard"))
        + (split,) * 7
        + (by_token,),
        out_specs=(by_token, by_token, P("shard"), P("shard")) + (split,) * 7,
        check_vma=False,
    )
```

```python
from functools import partial

import jax
import jax.numpy as jnp
from jax import lax
from jax.experimental import pallas as pl
from jax.experimental.pallas import tpu as pltpu
from jax.sharding import PartitionSpec as P


H = 32
KVH = 4
HD = 64
HALO = 64
LANES = 128

EPSILON = 1e-05
ROPE_BASE = 10000.0
NEG_FILL = -1e30

BF = jnp.bfloat16
F32 = jnp.float32


def dot(left, right, contract):
    return lax.dot_general(left, right, (contract, ((), ())), preferred_element_type=F32)


def rows_cols(left, right):
    return dot(left, right, ((1,), (0,)))


def rows_rows(left, right):
    return dot(left, right, ((0,), (0,)))


def cols_cols(left, right):
    return dot(left, right, ((1,), (1,)))


def spread(value, axis, count):
    wide = jnp.broadcast_to(value[None], (count,) + value.shape)
    return lax.all_to_all(wide, axis, split_axis=0, concat_axis=0, tiled=True)


def swap(value, axis):
    return lax.all_to_all(value, axis, split_axis=0, concat_axis=0, tiled=True)


def pairs(count, step):
    return [(i, i ^ step) for i in range(count)]


def send(value, axis, count, step):
    return lax.ppermute(value, axis, pairs(count, step))


def parts_rep(chunks, count):
    go = lambda value, step: send(value, "rep", count, step)
    if count != 4:
        return [
            [chunks[0][h]] + [go(chunks[k][h], k) for k in range(1, count)]
            for h in range(2)
        ]
    add = lambda left, right: (left.astype(F32) + right.astype(F32)).astype(BF)
    first_one = go(chunks[1][0], 1)
    first_two = go(chunks[3][0], 1)
    second_one = go(chunks[2][1], 2)
    second_two = go(chunks[3][1], 2)
    last_one = go(add(chunks[2][0], first_two), 2)
    last_two = go(add(chunks[1][1], second_two), 1)
    return [[chunks[0][0], first_one, last_one], [chunks[0][1], second_one, last_two]]


def gather_direct(value, count):
    return [value] + [send(value, "rep", count, k) for k in range(1, count)]


def gather_rep(halves, count):
    go = lambda value, step: send(value, "rep", count, step)
    if count != 4:
        return [halves] + [tuple(go(v, k) for v in halves) for k in range(1, count)]
    one = tuple(go(v, 1) for v in halves)
    two = tuple(go(v, 2) for v in halves)
    return [halves, one, two, (go(one[0], 2), go(two[1], 1))]


def place_kernel(count, me_ref, *refs):
    parts, out_ref = refs[:-1], refs[-1]
    at = pl.program_id(0)
    size = len(parts) // count
    for k in range(count):

        @pl.when(at == jnp.bitwise_xor(me_ref[0], k))
        def _(k=k):
            row = 0
            for part in parts[k * size : (k + 1) * size]:
                out_ref[0, row : row + part.shape[0]] = part[...].astype(F32)
                row += part.shape[0]


def place(pieces, me):
    count = len(pieces)
    flat = [part for piece in pieces for part in piece]
    rows = sum(part.shape[0] for part in pieces[0])
    width = flat[0].shape[1]
    grid = pltpu.PrefetchScalarGridSpec(
        num_scalar_prefetch=1,
        grid=(count,),
        in_specs=[
            pl.BlockSpec(part.shape, lambda g, me: (0, 0), pipeline_mode=pl.Buffered(1))
            for part in flat
        ],
        out_specs=pl.BlockSpec((1, rows, width), lambda g, me: (g, 0, 0)),
    )
    return pl.pallas_call(
        partial(place_kernel, count),
        out_shape=shape((count, rows, width), F32),
        grid_spec=grid,
        compiler_params=pltpu.CompilerParams(vmem_limit_bytes=56 * 1024 * 1024),
    )(me.astype(jnp.int32).reshape(1), *flat).reshape(count * rows, width)


def split_kernel(id_ref, gate_ref, up_ref, *refs):
    outs, both = refs[:-1], refs[-1]
    hidden = both.shape[3]
    for h, ref in enumerate((gate_ref, up_ref)):
        value = ref[...]
        for at in range(len(outs)):
            both[at, h] = value[:, at * hidden : (at + 1) * hidden]
    for k, out in enumerate(outs):
        out[...] = both[jnp.bitwise_xor(id_ref[1], k)]


def split_pair(ids, gate, up, fine, count):
    hidden = gate.shape[1] // count
    rows = pl.BlockSpec((fine, gate.shape[1]), lambda g, ids: (ids[0], 0))
    piece = (2, fine, hidden)
    return pl.pallas_call(
        split_kernel,
        out_shape=(shape(piece, BF),) * count,
        grid_spec=pltpu.PrefetchScalarGridSpec(
            num_scalar_prefetch=1,
            grid=(1,),
            in_specs=[rows, rows],
            out_specs=(pl.BlockSpec(piece, lambda g, ids: (0, 0, 0)),) * count,
            scratch_shapes=[pltpu.VMEM((count,) + piece, BF)],
        ),
        name="split_pair",
    )(ids, gate, up)


def flat_call(kernel, ids, out_shape, values, scratch=()):
    specs = [pl.BlockSpec(memory_space=pltpu.SMEM)]
    specs += [pl.BlockSpec(memory_space=pltpu.VMEM)] * len(values)
    return pl.pallas_call(
        kernel,
        out_shape=out_shape,
        in_specs=specs,
        scratch_shapes=list(scratch),
        compiler_params=pltpu.CompilerParams(vmem_limit_bytes=56 * 1024 * 1024),
    )(ids, *values)


def order_kernel(id_ref, *refs):
    pieces, (gate_ref, up_ref) = refs[:-2], refs[-2:]
    for k, piece in enumerate(pieces):
        at = jnp.bitwise_xor(id_ref[1], k)
        gate_ref[at] = piece[0]
        up_ref[at] = piece[1]


def join_kernel(id_ref, *refs):
    out_ref = refs[-1]
    for k in range(len(refs) // 2):
        at = jnp.bitwise_xor(id_ref[0], k)
        for h in range(2):
            value = refs[2 * k + h]
            for row in range(value.shape[0]):
                out_ref[h, row, at] = value[row]


def sum_kernel(id_ref, *refs):
    count = refs[0].shape[0]
    outs = refs[len(refs) - count :]
    parts = refs[: len(refs) - count]
    half = len(parts) // 2
    for k, out in enumerate(outs):
        at = jnp.bitwise_xor(id_ref[1], k)
        for h in range(2):
            total = parts[h * half][at].astype(F32)
            for part in parts[h * half + 1 : (h + 1) * half]:
                total += part[at].astype(F32)
            out[h] = total.astype(BF)


def widen_kernel(id_ref, *refs):
    pieces, (gate_ref, up_ref, both) = refs[:-3], refs[-3:]
    hidden = both.shape[3]
    for k, piece in enumerate(pieces):
        both[jnp.bitwise_xor(id_ref[1], k)] = piece[...]
    for h, ref in enumerate((gate_ref, up_ref)):
        for at in range(len(pieces)):
            ref[:, at * hidden : (at + 1) * hidden] = both[at, h]


def qkv_kernel(share, id_ref, *refs):
    pieces = refs[:-6]
    q_ref, k_ref, v_ref, gain_ref, k_all, v_all = refs[-6:]
    count = k_all.shape[0]
    q_cols = q_ref.shape[1] // count
    total = 0.0
    for k, piece in enumerate(pieces):
        at = jnp.bitwise_xor(id_ref[0], k)
        value = piece[...].astype(F32)
        q_ref[:, pl.ds(pl.multiple_of(at * q_cols, LANES), q_cols)] = value[:, :q_cols]
        k_all[at] = value[:, q_cols : q_cols + HD]
        v_all[at] = value[:, q_cols + HD : q_cols + 2 * HD]
        total += value[:, q_cols + 2 * HD :]
    gain_ref[...] = total
    for ref, both in ((k_ref, k_all), (v_ref, v_all)):
        for head in range(count // share):
            total = both[head * share]
            for other in range(head * share + 1, (head + 1) * share):
                total += both[other]
            ref[:, head * HD : (head + 1) * HD] = total


def pair_grad_kernel(fine, id_ref, x_ref, grad_ref, *refs):
    outs, total_ref = refs[:-1], refs[-1]
    total_ref[...] = rows_rows(x_ref[...], grad_ref[...])
    own = fine * len(outs)
    for k, out in enumerate(outs):
        row = jnp.bitwise_xor(id_ref[0], k) * fine
        for block in range(out.shape[0]):
            at = pl.multiple_of(block * own + row, fine)
            out[block] = total_ref[pl.ds(at, fine)].astype(BF)


def pair_grad(ids, x, grad, fine, count, blocks):
    width, hidden = x.shape[1], grad.shape[1]
    tile = 2 * fine * count
    out = (2, fine, hidden)
    return pl.pallas_call(
        partial(pair_grad_kernel, fine),
        out_shape=(shape((blocks, fine, hidden), BF),) * count,
        grid_spec=pltpu.PrefetchScalarGridSpec(
            num_scalar_prefetch=1,
            grid=(width // tile,),
            in_specs=[
                pl.BlockSpec((x.shape[0], tile), lambda g, ids: (0, g)),
                pl.BlockSpec(grad.shape, lambda g, ids: (0, 0), pipeline_mode=pl.Buffered(1)),
            ],
            out_specs=(pl.BlockSpec(out, lambda g, ids: (g, 0, 0)),) * count,
            scratch_shapes=[pltpu.VMEM((tile, hidden), F32)],
        ),
        compiler_params=pltpu.CompilerParams(vmem_limit_bytes=56 * 1024 * 1024),
    )(ids, x, grad)


def norm_scale(value):
    return lax.rsqrt(jnp.mean(value * value, axis=1, keepdims=True) + EPSILON)


def turn(tile, cosine, sine):
    lane = lax.broadcasted_iota(jnp.int32, tile.shape, 1)
    swapped = jnp.where(
        lane % HD < HD // 2,
        -pltpu.roll(tile, LANES - HD // 2, 1),
        pltpu.roll(tile, HD // 2, 1),
    )
    return tile * cosine + swapped * sine


def turn_first(tile, cosine, sine):
    lane = lax.broadcasted_iota(jnp.int32, tile.shape, 1)
    return jnp.where(lane < HD, turn(tile, cosine, sine), tile)


def in_kernel(x_ref, gain_ref, w_ref, cos_ref, sin_ref, normed_ref, q_ref, kv_ref):
    x = x_ref[0].astype(F32)
    normed = (x * norm_scale(x) * gain_ref[...]).astype(BF)
    normed_ref[0] = normed
    qkv = rows_cols(normed, w_ref[...])
    cosine, sine = cos_ref[0], sin_ref[0]
    q_cols = q_ref.shape[2]
    for at in range(0, q_cols, LANES):
        q_ref[0, :, at : at + LANES] = turn(qkv[:, at : at + LANES], cosine, sine).astype(BF)
    kv_ref[0] = turn_first(qkv[:, q_cols:], cosine, sine).astype(BF)


def stack_heads(value):
    return jnp.concatenate(
        [value[:, at : at + HD] for at in range(0, value.shape[1], HD)], axis=0
    )


def unstack_heads(value, rows):
    return jnp.concatenate(
        [value[at : at + rows] for at in range(0, value.shape[0], rows)], axis=1
    )


def attend_kernel(fine, q_ref, own_ref, halo_ref, pos_ref, probs_ref, out_ref):
    rows, q_cols = q_ref.shape[1:]
    heads = q_cols // HD
    count = out_ref.shape[0]
    kv = jnp.concatenate([halo_ref[0], own_ref[0]], axis=0)
    keys, values = kv[:, :HD], kv[:, HD:]
    span = kv.shape[0]
    scores = cols_cols(stack_heads(q_ref[0]), keys) * (HD**-0.5)
    query = lax.broadcasted_iota(jnp.int32, (rows, span), 0) + HALO
    key = lax.broadcasted_iota(jnp.int32, (rows, span), 1)
    first = query - pos_ref[0][:, :1].astype(jnp.int32)
    allowed = (key >= first) & (key <= query)
    scores = jnp.where(allowed[None], scores.reshape(heads, rows, span), NEG_FILL)
    grown = jnp.exp(scores - jnp.max(scores, axis=-1, keepdims=True))
    probs = grown / jnp.sum(grown, axis=-1, keepdims=True)
    probs_ref[0] = probs
    mixed = rows_cols(probs.reshape(heads * rows, span).astype(BF), values)
    mixed = unstack_heads(mixed, rows).astype(BF)
    for to in range(count):
        out_ref[to, 0] = jnp.concatenate(
            [
                mixed[:, at + to * fine : at + (to + 1) * fine]
                for at in range(0, q_cols, count * fine)
            ],
            axis=1,
        )


def attend_back_kernel(
    fine, grad_ref, probs_ref, q_ref, own_ref, halo_ref, cos_ref, sin_ref, q_out, kv_out
):
    rows, q_cols = q_ref.shape[1:]
    heads = q_cols // HD
    count = grad_ref.shape[0]
    kv = jnp.concatenate([halo_ref[0], own_ref[0]], axis=0)
    keys, values = kv[:, :HD], kv[:, HD:]
    span = kv.shape[0]
    grad = jnp.concatenate(
        [
            grad_ref[source, 0][:, at * fine : (at + 1) * fine]
            for at in range(q_cols // (count * fine))
            for source in range(count)
        ],
        axis=1,
    )
    grad = stack_heads(grad)
    probs = probs_ref[0].reshape(heads * rows, span)
    probs_grad = cols_cols(grad, values)
    inner = jnp.sum(probs * probs_grad, axis=-1, keepdims=True)
    score_grad = (probs * (probs_grad - inner)).astype(BF)
    scale = HD**-0.5
    key_grad = rows_rows(score_grad, stack_heads(q_ref[0])) * scale
    value_grad = rows_rows(probs.astype(BF), grad)
    kv_out[0] = jnp.concatenate([key_grad, value_grad], axis=1)
    query_grad = unstack_heads(rows_cols(score_grad, keys) * scale, rows)
    cosine, sine = cos_ref[0], -sin_ref[0]
    for at in range(0, q_cols, LANES):
        q_out[0, :, at : at + LANES] = turn(
            query_grad[:, at : at + LANES], cosine, sine
        ).astype(BF)


def in_back_kernel(
    dq_ref, dkv_ref, back_ref, cos_ref, sin_ref, normed_ref, x_ref, two_ref, w_ref,
    part_ref, grad_ref, total_ref,
):
    at = pl.program_id(0)
    rows = dq_ref.shape[1]
    own = dkv_ref[0, HALO:]
    tail = own[rows - HALO :] + back_ref[0]
    own = jnp.concatenate([own[: rows - HALO], tail], axis=0)
    own = turn_first(own, cos_ref[0], -sin_ref[0]).astype(BF)
    qkv_grad = jnp.concatenate([dq_ref[0], own], axis=1)
    normed_grad = cols_cols(qkv_grad, w_ref[...])
    part_ref[0] = normed_grad.astype(BF)
    x = x_ref[0].astype(F32)
    one = (normed_grad * x * norm_scale(x)).astype(BF)
    cols = qkv_grad.shape[1]
    lane = lax.broadcasted_iota(jnp.int32, (rows, LANES), 1)

    @pl.when(at == 0)
    def _():
        total_ref[:, :cols] = rows_rows(normed_ref[0], qkv_grad)
        total_ref[:, cols:] = rows_rows(one, (lane < HD).astype(BF)) + rows_rows(
            two_ref[...], (lane >= HD).astype(BF)
        )

    @pl.when(at > 0)
    def _():
        total_ref[:, :cols] += rows_rows(normed_ref[0], qkv_grad)
        total_ref[:, cols:] += rows_rows(one, (lane < HD).astype(BF))

    @pl.when(at == pl.num_programs(0) - 1)
    def _():
        grad_ref[...] = total_ref[...].astype(BF)


def middle_kernel(part_ref, x_ref, gain_ref, mid_ref, normed_ref):
    mid = x_ref[...].astype(F32)
    for at in range(part_ref.shape[0]):
        mid += part_ref[at].astype(F32)
    mid_ref[...] = mid
    normed_ref[...] = (mid * norm_scale(mid) * gain_ref[...]).astype(BF)


def middle_back_kernel(grad_ref, mid_ref, gain_ref, cot_ref, out_ref, low_ref, gain_out_ref):
    mid = mid_ref[...]
    scale = norm_scale(mid)
    grad = grad_ref[...].astype(F32)
    gain_out_ref[...] = (grad * mid * scale).astype(BF)
    scaled = grad * gain_ref[...]
    out = (
        cot_ref[...].astype(F32)
        + scale * scaled
        - mid * scale**3 * jnp.mean(scaled * mid, axis=1, keepdims=True)
    )
    out_ref[...] = out
    low_ref[...] = out.astype(BF)


def last_kernel(part_ref, x_ref, gain_ref, mid_ref, out_ref):
    x = x_ref[...].astype(F32)
    scale = norm_scale(x)
    grad = part_ref[0].astype(F32)
    for at in range(1, part_ref.shape[0]):
        grad += part_ref[at].astype(F32)
    scaled = grad * gain_ref[...]
    out = (
        mid_ref[...]
        + scale * scaled
        - x * scale**3 * jnp.mean(scaled * x, axis=1, keepdims=True)
    )
    out_ref[...] = out.astype(BF)


def forward_kernel(x_ref, back_ref, pair_ref, mixed_ref, gate_out, up_out):
    x = x_ref[...]
    gate = rows_cols(x, pair_ref[0])
    up = rows_cols(x, pair_ref[1])
    mixed_grad = back_ref[...]
    sigma = jax.nn.sigmoid(gate)
    silu = gate * sigma
    mixed_ref[...] = (silu * up).astype(BF)
    gate_out[...] = (mixed_grad * up * sigma * (1.0 + gate * (1.0 - sigma))).astype(BF)
    up_out[...] = (mixed_grad * silu).astype(BF)


def back_kernel(gate_ref, up_ref, pair_ref, part_ref):
    part_ref[...] = (
        cols_cols(gate_ref[...], pair_ref[0]) + cols_cols(up_ref[...], pair_ref[1])
    ).astype(BF)


def shape(dims, kind):
    return jax.ShapeDtypeStruct(dims, kind)


def call(kernel, out_shape, grid=None, in_specs=None, out_specs=None, scratch=()):
    options = {}
    if grid is not None:
        options = {"grid": grid, "in_specs": in_specs, "out_specs": out_specs}
    return pl.pallas_call(
        kernel,
        out_shape=out_shape,
        scratch_shapes=list(scratch),
        compiler_params=pltpu.CompilerParams(vmem_limit_bytes=56 * 1024 * 1024),
        **options,
    )


def by_block(dims):
    return pl.BlockSpec((1,) + dims, lambda g: (g,) + (0,) * len(dims))


def whole(dims):
    return pl.BlockSpec(dims, lambda g: (0,) * len(dims), pipeline_mode=pl.Buffered(1))


def body(
    n_rep,
    n_shard,
    tokens,
    seq_lengths,
    deal_order,
    attn_gain,
    mlp_gain,
    q_weight,
    k_weight,
    v_weight,
    o_weight,
    gate_weight,
    up_weight,
    down_weight,
    cotangent,
):
    rows, width = tokens.shape
    r = lax.axis_index("rep")
    s = lax.axis_index("shard")
    own = width // n_shard
    fine = own // n_rep
    hidden = down_weight.shape[0]
    q_cols = width // n_rep
    heads = H // n_rep
    pair = n_shard // n_rep
    share = max(n_rep // KVH, 1)
    kv_at = (r * KVH) // n_rep
    all_rows = n_rep * rows
    span = HALO + rows
    qkv_cols = q_cols + 2 * HD

    starts = jnp.cumsum(seq_lengths[0]) - seq_lengths[0]
    places = s * rows + jnp.arange(rows, dtype=jnp.int32)
    first = jnp.max(
        jnp.where(starts[None, :] <= places[:, None], starts[None, :], 0), axis=1, keepdims=True
    )
    offset = jnp.broadcast_to((places[:, None] - first).astype(BF), (rows, LANES))

    w_qkv_own = jnp.concatenate(
        [
            lax.dynamic_slice_in_dim(q_weight, r * q_cols, q_cols, 1),
            lax.dynamic_slice_in_dim(k_weight, kv_at * HD, HD, 1),
            lax.dynamic_slice_in_dim(v_weight, kv_at * HD, HD, 1),
        ],
        axis=1,
    )
    w_qkv = lax.all_gather(w_qkv_own, "shard", axis=0, tiled=True)
    w_o = lax.all_gather(
        lax.dynamic_slice_in_dim(o_weight, r * fine, fine, 0), "shard", axis=0, tiled=True
    )
    x_all = spread(jnp.concatenate([tokens, offset], axis=1), "rep", n_rep)
    gains = lax.all_gather(jnp.stack([attn_gain, mlp_gain]), "shard", axis=1, tiled=True)
    gain_one = gains[0:1].astype(F32)
    gain_two = gains[1:2].astype(F32)

    def exchange_shard(pieces):
        rest = [send(pieces[k], "shard", n_shard, k) for k in range(1, n_shard)]
        return [pieces[0]] + rest

    block = (n_shard, fine, hidden)
    ids = jnp.stack([r, s]).astype(jnp.int32)
    gate_tied, up_tied, _ = lax.optimization_barrier((gate_weight, up_weight, gains))
    w_pair = split_pair(ids, gate_tied, up_tied, fine, n_shard)
    w_pair = exchange_shard(w_pair)
    w_pair = flat_call(order_kernel, ids, (shape(block, BF),) * 2, w_pair)
    w_pair = gather_rep(w_pair, n_rep)
    w_pair = flat_call(
        join_kernel,
        ids,
        shape((2, n_shard, n_rep, fine, hidden), BF),
        [half for piece in w_pair for half in piece],
    ).reshape(2, width, hidden)
    cot_all = lax.all_gather(cotangent, "shard", axis=0, tiled=True)

    half = HD // 2
    inverse = ROPE_BASE ** (-2.0 * (jnp.arange(LANES) % half).astype(F32) / HD)
    angles = x_all[:, :, width:].astype(F32) * inverse[None, None, :]
    cosine, sine = jnp.cos(angles), jnp.sin(angles)
    x_block = by_block((rows, width))
    table = by_block((rows, LANES))
    normed_one, queries, kv_own = call(
        in_kernel,
        (
            shape((n_rep, rows, width), BF),
            shape((n_rep, rows, q_cols), BF),
            shape((n_rep, rows, LANES), BF),
        ),
        (n_rep,),
        [x_block, whole((1, width)), whole((width, qkv_cols)), table, table],
        (x_block, by_block((rows, q_cols)), table),
    )(x_all, gain_one, w_qkv, cosine, sine)
    kv_halo = lax.ppermute(
        kv_own[:, rows - HALO :], "shard", [(i, i + 1) for i in range(n_shard - 1)]
    )
    head_block = pl.BlockSpec((n_rep, 1, rows, pair * fine), lambda g: (0, g, 0, 0))
    probs_block = by_block((heads, rows, span))
    probs, out_in = call(
        partial(attend_kernel, fine),
        (
            shape((n_rep, heads, rows, span), F32),
            shape((n_rep, n_rep, rows, pair * fine), BF),
        ),
        (n_rep,),
        [
            by_block((rows, q_cols)),
            table,
            by_block((HALO, LANES)),
            pl.BlockSpec((1, rows, LANES), lambda g: (g, 0, width // LANES)),
        ],
        (probs_block, head_block),
    )(queries, kv_own, kv_halo, x_all)
    out_in = swap(out_in, "rep").reshape(n_rep, all_rows, pair * fine)
    out_in = out_in.transpose(1, 0, 2).reshape(all_rows, q_cols)
    mid_part = rows_cols(out_in, w_o).astype(BF).reshape(n_rep, rows, width)
    x_mid, normed_two = call(
        middle_kernel, (shape((rows, width), F32), shape((rows, width), BF))
    )(swap(mid_part, "rep"), tokens, gain_two)

    two_all = lax.all_gather(normed_two, "shard", axis=0, tiled=True)
    mixed_grad = cols_cols(cot_all, down_weight)
    step = 256
    group = two_all.shape[0]
    token_block = pl.BlockSpec((step, width), lambda g: (g, 0))
    hidden_block = pl.BlockSpec((step, hidden), lambda g: (g, 0))
    mixed, gate_grad, up_grad = call(
        forward_kernel,
        (shape((group, hidden), BF),) * 3,
        (group // step,),
        [token_block, hidden_block, whole((2, width, hidden))],
        (hidden_block,) * 3,
    )(two_all, mixed_grad, w_pair)
    gate_chunks = pair_grad(ids, two_all, gate_grad, fine, n_rep, n_shard)
    gate_tied, _ = lax.optimization_barrier((gate_grad, gate_chunks[0]))
    two_grad_part = call(
        back_kernel,
        shape((group, width), BF),
        (group // step,),
        [hidden_block, hidden_block, whole((2, width, hidden))],
        token_block,
    )(gate_tied, up_grad, w_pair)
    up_grad, _ = lax.optimization_barrier((up_grad, two_grad_part))
    two_grad = lax.psum_scatter(two_grad_part, "shard", scatter_dimension=0, tiled=True)
    mid_grad, branch, gain_two_rows = call(
        middle_back_kernel,
        (shape((rows, width), F32), shape((rows, width), BF), shape((rows, width), BF)),
    )(two_grad, x_mid, gain_two, cotangent)

    up_chunks = pair_grad(ids, two_all, up_grad, fine, n_rep, n_shard)
    pair_chunks = list(zip(gate_chunks, up_chunks))
    mixed, _ = lax.optimization_barrier((mixed, up_chunks[0]))
    part_rows = hidden // n_rep
    cut = (part_rows // 2 + 15) // 16 * 16
    down_grad = rows_rows(mixed, cot_all).astype(BF)
    down_chunks = []
    for k in range(n_rep):
        at = (r ^ k) * part_rows
        down_chunks.append(
            (
                lax.dynamic_slice_in_dim(down_grad, at, cut, 0),
                lax.dynamic_slice_in_dim(down_grad, at + cut, part_rows - cut, 0),
            )
        )
    down_part = rows_cols(mixed, down_weight).astype(BF)
    down_rows = lax.psum_scatter(down_part, "shard", scatter_dimension=0, tiled=True)
    layer_out = (x_mid + down_rows.astype(F32)).astype(BF)
    w_down_grad = parts_rep(down_chunks, n_rep)
    w_down_grad = tuple(
        sum(part.astype(F32) for part in parts).astype(BF) for parts in w_down_grad
    )
    down_out = place(gather_rep(w_down_grad, n_rep), r)
    w_pair_grad = parts_rep(pair_chunks, n_rep)
    w_pair_grad = flat_call(
        sum_kernel,
        ids,
        (shape((2, fine, hidden), BF),) * n_shard,
        w_pair_grad[0] + w_pair_grad[1],
    )
    w_pair_grad = exchange_shard(w_pair_grad)
    w_pair_grad = flat_call(
        widen_kernel,
        ids,
        (shape((fine, n_shard * hidden), BF),) * 2,
        w_pair_grad,
        [pltpu.VMEM((n_shard, 2, fine, hidden), BF)],
    )
    w_pair_grad = gather_rep(w_pair_grad, n_rep)
    gate_out = place([piece[:1] for piece in w_pair_grad], r)
    up_out = place([piece[1:] for piece in w_pair_grad], r)

    branch_all = spread(branch, "rep", n_rep).reshape(all_rows, width)
    in_grad = cols_cols(branch_all, w_o).astype(BF)
    branch_all, in_grad = lax.optimization_barrier((branch_all, in_grad))
    in_grad = in_grad.reshape(all_rows, n_rep, pair * fine).transpose(1, 0, 2)
    in_grad = swap(in_grad, "rep").reshape(n_rep, n_rep, rows, pair * fine)
    w_o_grad = rows_rows(out_in, branch_all).astype(BF)
    w_o_grad = lax.psum_scatter(w_o_grad, "shard", scatter_dimension=0, tiled=True)
    o_out = place([(v,) for v in gather_direct(w_o_grad, n_rep)], r)
    query_grad, kv_grad = call(
        partial(attend_back_kernel, fine),
        (shape((n_rep, rows, q_cols), BF), shape((n_rep, span, LANES), F32)),
        (n_rep,),
        [
            head_block,
            probs_block,
            by_block((rows, q_cols)),
            table,
            by_block((HALO, LANES)),
            table,
            table,
        ],
        (by_block((rows, q_cols)), by_block((span, LANES))),
    )(in_grad, probs, queries, kv_own, kv_halo, cosine, sine)
    kv_back = lax.ppermute(
        kv_grad[:, :HALO], "shard", [(i + 1, i) for i in range(n_shard - 1)]
    )
    grad_cols = qkv_cols + LANES
    one_grad_part, w_qkv_grad = call(
        in_back_kernel,
        (shape((n_rep, rows, width), BF), shape((width, grad_cols), BF)),
        (n_rep,),
        [
            by_block((rows, q_cols)),
            by_block((span, LANES)),
            by_block((HALO, LANES)),
            table,
            table,
            x_block,
            x_block,
            whole((rows, width)),
            whole((width, qkv_cols)),
        ],
        (x_block, pl.BlockSpec((width, grad_cols), lambda g: (0, 0))),
        [pltpu.VMEM((width, grad_cols), F32)],
    )(
        query_grad, kv_grad, kv_back, cosine, sine, normed_one, x_all, gain_two_rows, w_qkv
    )
    w_qkv_grad = lax.psum_scatter(w_qkv_grad, "shard", scatter_dimension=0, tiled=True)
    input_grad = call(last_kernel, shape((rows, width), BF))(
        swap(one_grad_part, "rep"), tokens, gain_one, mid_grad
    )
    q_out, k_out, v_out, gain_sums = flat_call(
        partial(qkv_kernel, share),
        ids,
        (
            shape((own, width), F32),
            shape((own, KVH * HD), F32),
            shape((own, KVH * HD), F32),
            shape((own, LANES), F32),
        ),
        gather_direct(w_qkv_grad, n_rep),
        [pltpu.VMEM((n_rep, own, HD), F32)] * 2,
    )
    return (
        layer_out,
        input_grad,
        gain_sums[:, 0],
        gain_sums[:, HD],
        q_out,
        k_out,
        v_out,
        o_out,
        gate_out,
        up_out,
        down_out,
    )


def solution(mesh):
    split = P("shard", None)
    by_token = P(("rep", "shard"), None)
    return jax.shard_map(
        partial(body, mesh.shape["rep"], mesh.shape["shard"]),
        mesh=mesh,
        in_specs=(by_token, P("rep", None), P("rep", None), P("shard"), P("shard"))
        + (split,) * 7
        + (by_token,),
        out_specs=(by_token, by_token, P("shard"), P("shard")) + (split,) * 7,
        check_vma=False,
    )
```

```python
from functools import partial

import jax
import jax.numpy as jnp
from jax import lax
from jax.experimental import pallas as pl
from jax.experimental.pallas import tpu as pltpu
from jax.sharding import PartitionSpec as P


H = 32
KVH = 4
HD = 64
HALO = 64
LANES = 128

EPSILON = 1e-05
ROPE_BASE = 10000.0
NEG_FILL = -1e30

BF = jnp.bfloat16
F32 = jnp.float32


def dot(left, right, contract):
    return lax.dot_general(left, right, (contract, ((), ())), preferred_element_type=F32)


def rows_cols(left, right):
    return dot(left, right, ((1,), (0,)))


def rows_rows(left, right):
    return dot(left, right, ((0,), (0,)))


def cols_cols(left, right):
    return dot(left, right, ((1,), (1,)))


def spread(value, axis, count):
    wide = jnp.broadcast_to(value[None], (count,) + value.shape)
    return lax.all_to_all(wide, axis, split_axis=0, concat_axis=0, tiled=True)


def swap(value, axis):
    return lax.all_to_all(value, axis, split_axis=0, concat_axis=0, tiled=True)


def pairs(count, step):
    return [(i, i ^ step) for i in range(count)]


def send(value, axis, count, step):
    return lax.ppermute(value, axis, pairs(count, step))


def parts_rep(chunks, count, after=None):
    go = lambda value, step: send(value, "rep", count, step)
    if count != 4:
        return [
            [chunks[0][h]] + [go(chunks[k][h], k) for k in range(1, count)]
            for h in range(2)
        ]
    add = lambda left, right: (left.astype(F32) + right.astype(F32)).astype(BF)
    first_one = go(chunks[1][0], 1)
    first_two = go(chunks[3][0], 1)
    second_one = go(chunks[2][1], 2)
    second_two = go(chunks[3][1], 2)
    joint_one, joint_two = add(chunks[2][0], first_two), add(chunks[1][1], second_two)
    if after is not None:
        joint_one, joint_two, _ = lax.optimization_barrier((joint_one, joint_two, after))
    last_one, last_two = go(joint_one, 2), go(joint_two, 1)
    return [[chunks[0][0], first_one, last_one], [chunks[0][1], second_one, last_two]]


def gather_direct(value, count):
    return [value] + [send(value, "rep", count, k) for k in range(1, count)]


def gather_rep(halves, count):
    go = lambda value, step: send(value, "rep", count, step)
    if count != 4:
        return [halves] + [tuple(go(v, k) for v in halves) for k in range(1, count)]
    one = tuple(go(v, 1) for v in halves)
    two = tuple(go(v, 2) for v in halves)
    return [halves, one, two, (go(one[0], 2), go(two[1], 1))]


def place_kernel(count, me_ref, *refs):
    parts, out_ref = refs[:-1], refs[-1]
    at = pl.program_id(0)
    size = len(parts) // count
    for k in range(count):

        @pl.when(at == jnp.bitwise_xor(me_ref[0], k))
        def _(k=k):
            row = 0
            for part in parts[k * size : (k + 1) * size]:
                out_ref[0, row : row + part.shape[0]] = part[...].astype(F32)
                row += part.shape[0]


def place(pieces, me):
    count = len(pieces)
    flat = [part for piece in pieces for part in piece]
    rows = sum(part.shape[0] for part in pieces[0])
    width = flat[0].shape[1]
    grid = pltpu.PrefetchScalarGridSpec(
        num_scalar_prefetch=1,
        grid=(count,),
        in_specs=[
            pl.BlockSpec(part.shape, lambda g, me: (0, 0), pipeline_mode=pl.Buffered(1))
            for part in flat
        ],
        out_specs=pl.BlockSpec((1, rows, width), lambda g, me: (g, 0, 0)),
    )
    return pl.pallas_call(
        partial(place_kernel, count),
        out_shape=shape((count, rows, width), F32),
        grid_spec=grid,
        compiler_params=pltpu.CompilerParams(vmem_limit_bytes=56 * 1024 * 1024),
    )(me.astype(jnp.int32).reshape(1), *flat).reshape(count * rows, width)


def split_kernel(id_ref, gate_ref, up_ref, *refs):
    outs, both = refs[:-1], refs[-1]
    hidden = both.shape[3]
    for h, ref in enumerate((gate_ref, up_ref)):
        value = ref[...]
        for at in range(len(outs)):
            both[at, h] = value[:, at * hidden : (at + 1) * hidden]
    for k, out in enumerate(outs):
        out[...] = both[jnp.bitwise_xor(id_ref[1], k)]


def split_pair(ids, gate, up, fine, count):
    hidden = gate.shape[1] // count
    rows = pl.BlockSpec((fine, gate.shape[1]), lambda g, ids: (ids[0], 0))
    piece = (2, fine, hidden)
    return pl.pallas_call(
        split_kernel,
        out_shape=(shape(piece, BF),) * count,
        grid_spec=pltpu.PrefetchScalarGridSpec(
            num_scalar_prefetch=1,
            grid=(1,),
            in_specs=[rows, rows],
            out_specs=(pl.BlockSpec(piece, lambda g, ids: (0, 0, 0)),) * count,
            scratch_shapes=[pltpu.VMEM((count,) + piece, BF)],
        ),
        name="split_pair",
    )(ids, gate, up)


def flat_call(kernel, ids, out_shape, values, scratch=()):
    specs = [pl.BlockSpec(memory_space=pltpu.SMEM)]
    specs += [pl.BlockSpec(memory_space=pltpu.VMEM)] * len(values)
    return pl.pallas_call(
        kernel,
        out_shape=out_shape,
        in_specs=specs,
        scratch_shapes=list(scratch),
        compiler_params=pltpu.CompilerParams(vmem_limit_bytes=56 * 1024 * 1024),
    )(ids, *values)


def order_kernel(id_ref, *refs):
    pieces, (gate_ref, up_ref) = refs[:-2], refs[-2:]
    for k, piece in enumerate(pieces):
        at = jnp.bitwise_xor(id_ref[1], k)
        gate_ref[at] = piece[0]
        up_ref[at] = piece[1]


def join_kernel(id_ref, *refs):
    out_ref = refs[-1]
    for k in range(len(refs) // 2):
        at = jnp.bitwise_xor(id_ref[0], k)
        for h in range(2):
            value = refs[2 * k + h]
            for row in range(value.shape[0]):
                out_ref[h, row, at] = value[row]


def sum_kernel(id_ref, *refs):
    count = refs[0].shape[0]
    outs = refs[len(refs) - count :]
    parts = refs[: len(refs) - count]
    half = len(parts) // 2
    for k, out in enumerate(outs):
        at = jnp.bitwise_xor(id_ref[1], k)
        for h in range(2):
            total = parts[h * half][at].astype(F32)
            for part in parts[h * half + 1 : (h + 1) * half]:
                total += part[at].astype(F32)
            out[h] = total.astype(BF)


def widen_kernel(id_ref, *refs):
    pieces, (gate_ref, up_ref, both) = refs[:-3], refs[-3:]
    hidden = both.shape[3]
    for k, piece in enumerate(pieces):
        both[jnp.bitwise_xor(id_ref[1], k)] = piece[...]
    for h, ref in enumerate((gate_ref, up_ref)):
        for at in range(len(pieces)):
            ref[:, at * hidden : (at + 1) * hidden] = both[at, h]


def qkv_kernel(share, id_ref, *refs):
    pieces = refs[:-6]
    q_ref, k_ref, v_ref, gain_ref, k_all, v_all = refs[-6:]
    count = k_all.shape[0]
    q_cols = q_ref.shape[1] // count
    total = 0.0
    for k, piece in enumerate(pieces):
        at = jnp.bitwise_xor(id_ref[0], k)
        value = piece[...].astype(F32)
        q_ref[:, pl.ds(pl.multiple_of(at * q_cols, LANES), q_cols)] = value[:, :q_cols]
        k_all[at] = value[:, q_cols : q_cols + HD]
        v_all[at] = value[:, q_cols + HD : q_cols + 2 * HD]
        total += value[:, q_cols + 2 * HD :]
    gain_ref[...] = total
    for ref, both in ((k_ref, k_all), (v_ref, v_all)):
        for head in range(count // share):
            total = both[head * share]
            for other in range(head * share + 1, (head + 1) * share):
                total += both[other]
            ref[:, head * HD : (head + 1) * HD] = total


def pair_grad_kernel(fine, id_ref, x_ref, grad_ref, *refs):
    outs, total_ref = refs[:-1], refs[-1]
    total_ref[...] = rows_rows(x_ref[...], grad_ref[...])
    own = fine * len(outs)
    for k, out in enumerate(outs):
        row = jnp.bitwise_xor(id_ref[0], k) * fine
        for block in range(out.shape[0]):
            at = pl.multiple_of(block * own + row, fine)
            out[block] = total_ref[pl.ds(at, fine)].astype(BF)


def pair_grad(ids, x, grad, fine, count, blocks):
    width, hidden = x.shape[1], grad.shape[1]
    tile = 2 * fine * count
    out = (2, fine, hidden)
    return pl.pallas_call(
        partial(pair_grad_kernel, fine),
        out_shape=(shape((blocks, fine, hidden), BF),) * count,
        grid_spec=pltpu.PrefetchScalarGridSpec(
            num_scalar_prefetch=1,
            grid=(width // tile,),
            in_specs=[
                pl.BlockSpec((x.shape[0], tile), lambda g, ids: (0, g)),
                pl.BlockSpec(grad.shape, lambda g, ids: (0, 0), pipeline_mode=pl.Buffered(1)),
            ],
            out_specs=(pl.BlockSpec(out, lambda g, ids: (g, 0, 0)),) * count,
            scratch_shapes=[pltpu.VMEM((tile, hidden), F32)],
        ),
        compiler_params=pltpu.CompilerParams(vmem_limit_bytes=56 * 1024 * 1024),
    )(ids, x, grad)


def norm_scale(value):
    return lax.rsqrt(jnp.mean(value * value, axis=1, keepdims=True) + EPSILON)


def turn(tile, cosine, sine):
    lane = lax.broadcasted_iota(jnp.int32, tile.shape, 1)
    swapped = jnp.where(
        lane % HD < HD // 2,
        -pltpu.roll(tile, LANES - HD // 2, 1),
        pltpu.roll(tile, HD // 2, 1),
    )
    return tile * cosine + swapped * sine


def turn_first(tile, cosine, sine):
    lane = lax.broadcasted_iota(jnp.int32, tile.shape, 1)
    return jnp.where(lane < HD, turn(tile, cosine, sine), tile)


def in_kernel(x_ref, gain_ref, w_ref, cos_ref, sin_ref, normed_ref, q_ref, kv_ref):
    x = x_ref[0].astype(F32)
    normed = (x * norm_scale(x) * gain_ref[...]).astype(BF)
    normed_ref[0] = normed
    qkv = rows_cols(normed, w_ref[...])
    cosine, sine = cos_ref[0], sin_ref[0]
    q_cols = q_ref.shape[2]
    for at in range(0, q_cols, LANES):
        q_ref[0, :, at : at + LANES] = turn(qkv[:, at : at + LANES], cosine, sine).astype(BF)
    kv_ref[0] = turn_first(qkv[:, q_cols:], cosine, sine).astype(BF)


def stack_heads(value):
    return jnp.concatenate(
        [value[:, at : at + HD] for at in range(0, value.shape[1], HD)], axis=0
    )


def unstack_heads(value, rows):
    return jnp.concatenate(
        [value[at : at + rows] for at in range(0, value.shape[0], rows)], axis=1
    )


def attend_kernel(fine, q_ref, own_ref, halo_ref, pos_ref, probs_ref, out_ref):
    rows, q_cols = q_ref.shape[1:]
    heads = q_cols // HD
    count = out_ref.shape[0]
    kv = jnp.concatenate([halo_ref[0], own_ref[0]], axis=0)
    keys, values = kv[:, :HD], kv[:, HD:]
    span = kv.shape[0]
    scores = cols_cols(stack_heads(q_ref[0]), keys) * (HD**-0.5)
    query = lax.broadcasted_iota(jnp.int32, (rows, span), 0) + HALO
    key = lax.broadcasted_iota(jnp.int32, (rows, span), 1)
    first = query - pos_ref[0][:, :1].astype(jnp.int32)
    allowed = (key >= first) & (key <= query)
    scores = jnp.where(allowed[None], scores.reshape(heads, rows, span), NEG_FILL)
    grown = jnp.exp(scores - jnp.max(scores, axis=-1, keepdims=True))
    probs = grown / jnp.sum(grown, axis=-1, keepdims=True)
    probs_ref[0] = probs
    mixed = rows_cols(probs.reshape(heads * rows, span).astype(BF), values)
    mixed = unstack_heads(mixed, rows).astype(BF)
    for to in range(count):
        out_ref[to, 0] = jnp.concatenate(
            [
                mixed[:, at + to * fine : at + (to + 1) * fine]
                for at in range(0, q_cols, count * fine)
            ],
            axis=1,
        )


def attend_back_kernel(
    fine, grad_ref, probs_ref, q_ref, own_ref, halo_ref, cos_ref, sin_ref, q_out, kv_out
):
    rows, q_cols = q_ref.shape[1:]
    heads = q_cols // HD
    count = grad_ref.shape[0]
    kv = jnp.concatenate([halo_ref[0], own_ref[0]], axis=0)
    keys, values = kv[:, :HD], kv[:, HD:]
    span = kv.shape[0]
    grad = jnp.concatenate(
        [
            grad_ref[source, 0][:, at * fine : (at + 1) * fine]
            for at in range(q_cols // (count * fine))
            for source in range(count)
        ],
        axis=1,
    )
    grad = stack_heads(grad)
    probs = probs_ref[0].reshape(heads * rows, span)
    probs_grad = cols_cols(grad, values)
    inner = jnp.sum(probs * probs_grad, axis=-1, keepdims=True)
    score_grad = (probs * (probs_grad - inner)).astype(BF)
    scale = HD**-0.5
    key_grad = rows_rows(score_grad, stack_heads(q_ref[0])) * scale
    value_grad = rows_rows(probs.astype(BF), grad)
    kv_out[0] = jnp.concatenate([key_grad, value_grad], axis=1)
    query_grad = unstack_heads(rows_cols(score_grad, keys) * scale, rows)
    cosine, sine = cos_ref[0], -sin_ref[0]
    for at in range(0, q_cols, LANES):
        q_out[0, :, at : at + LANES] = turn(
            query_grad[:, at : at + LANES], cosine, sine
        ).astype(BF)


def in_back_kernel(
    dq_ref, dkv_ref, back_ref, cos_ref, sin_ref, normed_ref, x_ref, two_ref, w_ref,
    part_ref, grad_ref, total_ref,
):
    at = pl.program_id(0)
    rows = dq_ref.shape[1]
    own = dkv_ref[0, HALO:]
    tail = own[rows - HALO :] + back_ref[0]
    own = jnp.concatenate([own[: rows - HALO], tail], axis=0)
    own = turn_first(own, cos_ref[0], -sin_ref[0]).astype(BF)
    qkv_grad = jnp.concatenate([dq_ref[0], own], axis=1)
    normed_grad = cols_cols(qkv_grad, w_ref[...])
    part_ref[0] = normed_grad.astype(BF)
    x = x_ref[0].astype(F32)
    one = (normed_grad * x * norm_scale(x)).astype(BF)
    cols = qkv_grad.shape[1]
    lane = lax.broadcasted_iota(jnp.int32, (rows, LANES), 1)

    @pl.when(at == 0)
    def _():
        total_ref[:, :cols] = rows_rows(normed_ref[0], qkv_grad)
        total_ref[:, cols:] = rows_rows(one, (lane < HD).astype(BF)) + rows_rows(
            two_ref[...], (lane >= HD).astype(BF)
        )

    @pl.when(at > 0)
    def _():
        total_ref[:, :cols] += rows_rows(normed_ref[0], qkv_grad)
        total_ref[:, cols:] += rows_rows(one, (lane < HD).astype(BF))

    @pl.when(at == pl.num_programs(0) - 1)
    def _():
        grad_ref[...] = total_ref[...].astype(BF)


def middle_kernel(part_ref, x_ref, gain_ref, mid_ref, normed_ref):
    mid = x_ref[...].astype(F32)
    for at in range(part_ref.shape[0]):
        mid += part_ref[at].astype(F32)
    mid_ref[...] = mid
    normed_ref[...] = (mid * norm_scale(mid) * gain_ref[...]).astype(BF)


def middle_back_kernel(grad_ref, mid_ref, gain_ref, cot_ref, out_ref, low_ref, gain_out_ref):
    mid = mid_ref[...]
    scale = norm_scale(mid)
    grad = grad_ref[...].astype(F32)
    gain_out_ref[...] = (grad * mid * scale).astype(BF)
    scaled = grad * gain_ref[...]
    out = (
        cot_ref[...].astype(F32)
        + scale * scaled
        - mid * scale**3 * jnp.mean(scaled * mid, axis=1, keepdims=True)
    )
    out_ref[...] = out
    low_ref[...] = out.astype(BF)


def last_kernel(part_ref, x_ref, gain_ref, mid_ref, out_ref):
    x = x_ref[...].astype(F32)
    scale = norm_scale(x)
    grad = part_ref[0].astype(F32)
    for at in range(1, part_ref.shape[0]):
        grad += part_ref[at].astype(F32)
    scaled = grad * gain_ref[...]
    out = (
        mid_ref[...]
        + scale * scaled
        - x * scale**3 * jnp.mean(scaled * x, axis=1, keepdims=True)
    )
    out_ref[...] = out.astype(BF)


def forward_kernel(x_ref, back_ref, pair_ref, mixed_ref, gate_out, up_out):
    x = x_ref[...]
    gate = rows_cols(x, pair_ref[0])
    up = rows_cols(x, pair_ref[1])
    mixed_grad = back_ref[...]
    sigma = jax.nn.sigmoid(gate)
    silu = gate * sigma
    mixed_ref[...] = (silu * up).astype(BF)
    gate_out[...] = (mixed_grad * up * sigma * (1.0 + gate * (1.0 - sigma))).astype(BF)
    up_out[...] = (mixed_grad * silu).astype(BF)


def back_kernel(gate_ref, up_ref, pair_ref, part_ref):
    part_ref[...] = (
        cols_cols(gate_ref[...], pair_ref[0]) + cols_cols(up_ref[...], pair_ref[1])
    ).astype(BF)


def shape(dims, kind):
    return jax.ShapeDtypeStruct(dims, kind)


def call(kernel, out_shape, grid=None, in_specs=None, out_specs=None, scratch=()):
    options = {}
    if grid is not None:
        options = {"grid": grid, "in_specs": in_specs, "out_specs": out_specs}
    return pl.pallas_call(
        kernel,
        out_shape=out_shape,
        scratch_shapes=list(scratch),
        compiler_params=pltpu.CompilerParams(vmem_limit_bytes=56 * 1024 * 1024),
        **options,
    )


def by_block(dims):
    return pl.BlockSpec((1,) + dims, lambda g: (g,) + (0,) * len(dims))


def whole(dims):
    return pl.BlockSpec(dims, lambda g: (0,) * len(dims), pipeline_mode=pl.Buffered(1))


def body(
    n_rep,
    n_shard,
    tokens,
    seq_lengths,
    deal_order,
    attn_gain,
    mlp_gain,
    q_weight,
    k_weight,
    v_weight,
    o_weight,
    gate_weight,
    up_weight,
    down_weight,
    cotangent,
):
    rows, width = tokens.shape
    r = lax.axis_index("rep")
    s = lax.axis_index("shard")
    own = width // n_shard
    fine = own // n_rep
    hidden = down_weight.shape[0]
    q_cols = width // n_rep
    heads = H // n_rep
    pair = n_shard // n_rep
    share = max(n_rep // KVH, 1)
    kv_at = (r * KVH) // n_rep
    all_rows = n_rep * rows
    span = HALO + rows
    qkv_cols = q_cols + 2 * HD

    starts = jnp.cumsum(seq_lengths[0]) - seq_lengths[0]
    places = s * rows + jnp.arange(rows, dtype=jnp.int32)
    first = jnp.max(
        jnp.where(starts[None, :] <= places[:, None], starts[None, :], 0), axis=1, keepdims=True
    )
    offset = jnp.broadcast_to((places[:, None] - first).astype(BF), (rows, LANES))

    w_qkv_own = jnp.concatenate(
        [
            lax.dynamic_slice_in_dim(q_weight, r * q_cols, q_cols, 1),
            lax.dynamic_slice_in_dim(k_weight, kv_at * HD, HD, 1),
            lax.dynamic_slice_in_dim(v_weight, kv_at * HD, HD, 1),
        ],
        axis=1,
    )
    w_qkv = lax.all_gather(w_qkv_own, "shard", axis=0, tiled=True)
    w_o = lax.all_gather(
        lax.dynamic_slice_in_dim(o_weight, r * fine, fine, 0), "shard", axis=0, tiled=True
    )
    x_all = spread(jnp.concatenate([tokens, offset], axis=1), "rep", n_rep)
    gains = lax.all_gather(jnp.stack([attn_gain, mlp_gain]), "shard", axis=1, tiled=True)
    gain_one = gains[0:1].astype(F32)
    gain_two = gains[1:2].astype(F32)

    def exchange_shard(pieces):
        rest = [send(pieces[k], "shard", n_shard, k) for k in range(1, n_shard)]
        return [pieces[0]] + rest

    block = (n_shard, fine, hidden)
    ids = jnp.stack([r, s]).astype(jnp.int32)
    gate_tied, up_tied, _ = lax.optimization_barrier((gate_weight, up_weight, gains))
    w_pair = split_pair(ids, gate_tied, up_tied, fine, n_shard)
    w_pair = exchange_shard(w_pair)
    w_pair = flat_call(order_kernel, ids, (shape(block, BF),) * 2, w_pair)
    w_pair = gather_rep(w_pair, n_rep)
    w_pair = flat_call(
        join_kernel,
        ids,
        shape((2, n_shard, n_rep, fine, hidden), BF),
        [half for piece in w_pair for half in piece],
    ).reshape(2, width, hidden)
    cot_all = lax.all_gather(cotangent, "shard", axis=0, tiled=True)

    half = HD // 2
    inverse = ROPE_BASE ** (-2.0 * (jnp.arange(LANES) % half).astype(F32) / HD)
    angles = x_all[:, :, width:].astype(F32) * inverse[None, None, :]
    cosine, sine = jnp.cos(angles), jnp.sin(angles)
    x_block = by_block((rows, width))
    table = by_block((rows, LANES))
    normed_one, queries, kv_own = call(
        in_kernel,
        (
            shape((n_rep, rows, width), BF),
            shape((n_rep, rows, q_cols), BF),
            shape((n_rep, rows, LANES), BF),
        ),
        (n_rep,),
        [x_block, whole((1, width)), whole((width, qkv_cols)), table, table],
        (x_block, by_block((rows, q_cols)), table),
    )(x_all, gain_one, w_qkv, cosine, sine)
    kv_halo = lax.ppermute(
        kv_own[:, rows - HALO :], "shard", [(i, i + 1) for i in range(n_shard - 1)]
    )
    head_block = pl.BlockSpec((n_rep, 1, rows, pair * fine), lambda g: (0, g, 0, 0))
    probs_block = by_block((heads, rows, span))
    probs, out_in = call(
        partial(attend_kernel, fine),
        (
            shape((n_rep, heads, rows, span), F32),
            shape((n_rep, n_rep, rows, pair * fine), BF),
        ),
        (n_rep,),
        [
            by_block((rows, q_cols)),
            table,
            by_block((HALO, LANES)),
            pl.BlockSpec((1, rows, LANES), lambda g: (g, 0, width // LANES)),
        ],
        (probs_block, head_block),
    )(queries, kv_own, kv_halo, x_all)
    out_in = swap(out_in, "rep").reshape(n_rep, all_rows, pair * fine)
    out_in = out_in.transpose(1, 0, 2).reshape(all_rows, q_cols)
    mid_part = rows_cols(out_in, w_o).astype(BF).reshape(n_rep, rows, width)
    x_mid, normed_two = call(
        middle_kernel, (shape((rows, width), F32), shape((rows, width), BF))
    )(swap(mid_part, "rep"), tokens, gain_two)

    two_all = lax.all_gather(normed_two, "shard", axis=0, tiled=True)
    mixed_grad = cols_cols(cot_all, down_weight)
    step = 256
    group = two_all.shape[0]
    token_block = pl.BlockSpec((step, width), lambda g: (g, 0))
    hidden_block = pl.BlockSpec((step, hidden), lambda g: (g, 0))
    mixed, gate_grad, up_grad = call(
        forward_kernel,
        (shape((group, hidden), BF),) * 3,
        (group // step,),
        [token_block, hidden_block, whole((2, width, hidden))],
        (hidden_block,) * 3,
    )(two_all, mixed_grad, w_pair)
    gate_chunks = pair_grad(ids, two_all, gate_grad, fine, n_rep, n_shard)
    gate_tied, _ = lax.optimization_barrier((gate_grad, gate_chunks[0]))
    two_grad_part = call(
        back_kernel,
        shape((group, width), BF),
        (group // step,),
        [hidden_block, hidden_block, whole((2, width, hidden))],
        token_block,
    )(gate_tied, up_grad, w_pair)
    up_grad, _ = lax.optimization_barrier((up_grad, two_grad_part))
    two_grad = lax.psum_scatter(two_grad_part, "shard", scatter_dimension=0, tiled=True)
    mid_grad, branch, gain_two_rows = call(
        middle_back_kernel,
        (shape((rows, width), F32), shape((rows, width), BF), shape((rows, width), BF)),
    )(two_grad, x_mid, gain_two, cotangent)

    up_chunks = pair_grad(ids, two_all, up_grad, fine, n_rep, n_shard)
    pair_chunks = list(zip(gate_chunks, up_chunks))
    mixed, _ = lax.optimization_barrier((mixed, up_chunks[0]))
    part_rows = hidden // n_rep
    cut = (part_rows // 2 + 15) // 16 * 16
    down_grad = rows_rows(mixed, cot_all).astype(BF)
    down_chunks = []
    for k in range(n_rep):
        at = (r ^ k) * part_rows
        down_chunks.append(
            (
                lax.dynamic_slice_in_dim(down_grad, at, cut, 0),
                lax.dynamic_slice_in_dim(down_grad, at + cut, part_rows - cut, 0),
            )
        )
    down_part = rows_cols(mixed, down_weight).astype(BF)
    down_rows = lax.psum_scatter(down_part, "shard", scatter_dimension=0, tiled=True)
    layer_out = (x_mid + down_rows.astype(F32)).astype(BF)
    w_pair_grad = parts_rep(pair_chunks, n_rep)
    w_pair_grad = flat_call(
        sum_kernel,
        ids,
        (shape((2, fine, hidden), BF),) * n_shard,
        w_pair_grad[0] + w_pair_grad[1],
    )
    w_pair_grad = exchange_shard(w_pair_grad)
    w_pair_grad = flat_call(
        widen_kernel,
        ids,
        (shape((fine, n_shard * hidden), BF),) * 2,
        w_pair_grad,
        [pltpu.VMEM((n_shard, 2, fine, hidden), BF)],
    )
    w_pair_grad = gather_rep(w_pair_grad, n_rep)
    gate_out = place([piece[:1] for piece in w_pair_grad], r)
    up_out = place([piece[1:] for piece in w_pair_grad], r)

    branch_all = spread(branch, "rep", n_rep).reshape(all_rows, width)
    in_grad = cols_cols(branch_all, w_o).astype(BF)
    in_grad = in_grad.reshape(all_rows, n_rep, pair * fine).transpose(1, 0, 2)
    swapped = swap(in_grad, "rep").reshape(n_rep, n_rep, rows, pair * fine)
    w_down_grad = parts_rep(down_chunks, n_rep, in_grad)
    w_down_grad = tuple(
        sum(part.astype(F32) for part in parts).astype(BF) for parts in w_down_grad
    )
    down_out = place(gather_rep(w_down_grad, n_rep), r)
    query_grad, kv_grad = call(
        partial(attend_back_kernel, fine),
        (shape((n_rep, rows, q_cols), BF), shape((n_rep, span, LANES), F32)),
        (n_rep,),
        [
            head_block,
            probs_block,
            by_block((rows, q_cols)),
            table,
            by_block((HALO, LANES)),
            table,
            table,
        ],
        (by_block((rows, q_cols)), by_block((span, LANES))),
    )(swapped, probs, queries, kv_own, kv_halo, cosine, sine)
    kv_back = lax.ppermute(
        kv_grad[:, :HALO], "shard", [(i + 1, i) for i in range(n_shard - 1)]
    )
    grad_cols = qkv_cols + LANES
    one_grad_part, w_qkv_grad = call(
        in_back_kernel,
        (shape((n_rep, rows, width), BF), shape((width, grad_cols), BF)),
        (n_rep,),
        [
            by_block((rows, q_cols)),
            by_block((span, LANES)),
            by_block((HALO, LANES)),
            table,
            table,
            x_block,
            x_block,
            whole((rows, width)),
            whole((width, qkv_cols)),
        ],
        (x_block, pl.BlockSpec((width, grad_cols), lambda g: (0, 0))),
        [pltpu.VMEM((width, grad_cols), F32)],
    )(
        query_grad, kv_grad, kv_back, cosine, sine, normed_one, x_all, gain_two_rows, w_qkv
    )
    branch_all, _ = lax.optimization_barrier((branch_all, w_qkv_grad))
    w_qkv_grad = lax.psum_scatter(w_qkv_grad, "shard", scatter_dimension=0, tiled=True)
    w_o_grad = rows_rows(out_in, branch_all).astype(BF)
    w_o_grad = lax.psum_scatter(w_o_grad, "shard", scatter_dimension=0, tiled=True)
    o_out = place([(v,) for v in gather_direct(w_o_grad, n_rep)], r)
    input_grad = call(last_kernel, shape((rows, width), BF))(
        swap(one_grad_part, "rep"), tokens, gain_one, mid_grad
    )
    q_out, k_out, v_out, gain_sums = flat_call(
        partial(qkv_kernel, share),
        ids,
        (
            shape((own, width), F32),
            shape((own, KVH * HD), F32),
            shape((own, KVH * HD), F32),
            shape((own, LANES), F32),
        ),
        gather_direct(w_qkv_grad, n_rep),
        [pltpu.VMEM((n_rep, own, HD), F32)] * 2,
    )
    return (
        layer_out,
        input_grad,
        gain_sums[:, 0],
        gain_sums[:, HD],
        q_out,
        k_out,
        v_out,
        o_out,
        gate_out,
        up_out,
        down_out,
    )


def solution(mesh):
    split = P("shard", None)
    by_token = P(("rep", "shard"), None)
    return jax.shard_map(
        partial(body, mesh.shape["rep"], mesh.shape["shard"]),
        mesh=mesh,
        in_specs=(by_token, P("rep", None), P("rep", None), P("shard"), P("shard"))
        + (split,) * 7
        + (by_token,),
        out_specs=(by_token, by_token, P("shard"), P("shard")) + (split,) * 7,
        check_vma=False,
    )
```

```python
from functools import partial

import jax
import jax.numpy as jnp
from jax import lax
from jax.experimental import pallas as pl
from jax.experimental.pallas import tpu as pltpu
from jax.sharding import PartitionSpec as P


H = 32
KVH = 4
HD = 64
HALO = 64
LANES = 128

EPSILON = 1e-05
ROPE_BASE = 10000.0
NEG_FILL = -1e30

BF = jnp.bfloat16
F32 = jnp.float32


def dot(left, right, contract):
    return lax.dot_general(left, right, (contract, ((), ())), preferred_element_type=F32)


def rows_cols(left, right):
    return dot(left, right, ((1,), (0,)))


def rows_rows(left, right):
    return dot(left, right, ((0,), (0,)))


def cols_cols(left, right):
    return dot(left, right, ((1,), (1,)))


def spread(value, axis, count):
    wide = jnp.broadcast_to(value[None], (count,) + value.shape)
    return lax.all_to_all(wide, axis, split_axis=0, concat_axis=0, tiled=True)


def swap(value, axis):
    return lax.all_to_all(value, axis, split_axis=0, concat_axis=0, tiled=True)


def pairs(count, step):
    return [(i, i ^ step) for i in range(count)]


def send(value, axis, count, step):
    return lax.ppermute(value, axis, pairs(count, step))


def parts_rep(chunks, count):
    go = lambda value, step: send(value, "rep", count, step)
    if count != 4:
        return [
            [chunks[0][h]] + [go(chunks[k][h], k) for k in range(1, count)]
            for h in range(2)
        ]
    add = lambda left, right: (left.astype(F32) + right.astype(F32)).astype(BF)
    first_one = go(chunks[1][0], 1)
    first_two = go(chunks[3][0], 1)
    second_one = go(chunks[2][1], 2)
    second_two = go(chunks[3][1], 2)
    last_one = go(add(chunks[2][0], first_two), 2)
    last_two = go(add(chunks[1][1], second_two), 1)
    return [[chunks[0][0], first_one, last_one], [chunks[0][1], second_one, last_two]]


def gather_two(value, count):
    go = lambda value, step: send(value, "rep", count, step)
    if count != 4:
        return [(value,)] + [(go(value, k),) for k in range(1, count)]
    half = value.shape[0] // 2
    one, two = go(value, 1), go(value, 2)
    return [(value,), (one,), (two,), (go(one[:half], 2), go(two[half:], 1))]


def gather_rep(halves, count):
    go = lambda value, step: send(value, "rep", count, step)
    if count != 4:
        return [halves] + [tuple(go(v, k) for v in halves) for k in range(1, count)]
    one = tuple(go(v, 1) for v in halves)
    two = tuple(go(v, 2) for v in halves)
    return [halves, one, two, (go(one[0], 2), go(two[1], 1))]


def place_kernel(sizes, me_ref, *refs):
    parts, out_ref = list(refs[:-1]), refs[-1]
    at = pl.program_id(0)
    for k, size in enumerate(sizes):
        mine, parts = parts[:size], parts[size:]

        @pl.when(at == jnp.bitwise_xor(me_ref[0], k))
        def _(mine=mine):
            row = 0
            for part in mine:
                out_ref[0, row : row + part.shape[0]] = part[...].astype(F32)
                row += part.shape[0]


def place(pieces, me):
    count = len(pieces)
    flat = [part for piece in pieces for part in piece]
    rows = sum(part.shape[0] for part in pieces[0])
    width = flat[0].shape[1]
    grid = pltpu.PrefetchScalarGridSpec(
        num_scalar_prefetch=1,
        grid=(count,),
        in_specs=[
            pl.BlockSpec(part.shape, lambda g, me: (0, 0), pipeline_mode=pl.Buffered(1))
            for part in flat
        ],
        out_specs=pl.BlockSpec((1, rows, width), lambda g, me: (g, 0, 0)),
    )
    return pl.pallas_call(
        partial(place_kernel, [len(piece) for piece in pieces]),
        out_shape=shape((count, rows, width), F32),
        grid_spec=grid,
        compiler_params=pltpu.CompilerParams(vmem_limit_bytes=56 * 1024 * 1024),
    )(me.astype(jnp.int32).reshape(1), *flat).reshape(count * rows, width)


def split_kernel(id_ref, gate_ref, up_ref, *refs):
    outs, both = refs[:-1], refs[-1]
    hidden = both.shape[3]
    for h, ref in enumerate((gate_ref, up_ref)):
        value = ref[...]
        for at in range(len(outs)):
            both[at, h] = value[:, at * hidden : (at + 1) * hidden]
    for k, out in enumerate(outs):
        out[...] = both[jnp.bitwise_xor(id_ref[1], k)]


def split_pair(ids, gate, up, fine, count):
    hidden = gate.shape[1] // count
    rows = pl.BlockSpec((fine, gate.shape[1]), lambda g, ids: (ids[0], 0))
    piece = (2, fine, hidden)
    return pl.pallas_call(
        split_kernel,
        out_shape=(shape(piece, BF),) * count,
        grid_spec=pltpu.PrefetchScalarGridSpec(
            num_scalar_prefetch=1,
            grid=(1,),
            in_specs=[rows, rows],
            out_specs=(pl.BlockSpec(piece, lambda g, ids: (0, 0, 0)),) * count,
            scratch_shapes=[pltpu.VMEM((count,) + piece, BF)],
        ),
        name="split_pair",
    )(ids, gate, up)


def flat_call(kernel, ids, out_shape, values, scratch=()):
    specs = [pl.BlockSpec(memory_space=pltpu.SMEM)]
    specs += [pl.BlockSpec(memory_space=pltpu.VMEM)] * len(values)
    return pl.pallas_call(
        kernel,
        out_shape=out_shape,
        in_specs=specs,
        scratch_shapes=list(scratch),
        compiler_params=pltpu.CompilerParams(vmem_limit_bytes=56 * 1024 * 1024),
    )(ids, *values)


def order_kernel(id_ref, *refs):
    pieces, (gate_ref, up_ref) = refs[:-2], refs[-2:]
    for k, piece in enumerate(pieces):
        at = jnp.bitwise_xor(id_ref[1], k)
        gate_ref[at] = piece[0]
        up_ref[at] = piece[1]


def join_kernel(id_ref, *refs):
    out_ref = refs[-1]
    for k in range(len(refs) // 2):
        at = jnp.bitwise_xor(id_ref[0], k)
        for h in range(2):
            value = refs[2 * k + h]
            for row in range(value.shape[0]):
                out_ref[h, row, at] = value[row]


def sum_kernel(id_ref, *refs):
    count = refs[0].shape[0]
    outs = refs[len(refs) - count :]
    parts = refs[: len(refs) - count]
    half = len(parts) // 2
    for k, out in enumerate(outs):
        at = jnp.bitwise_xor(id_ref[1], k)
        for h in range(2):
            total = parts[h * half][at].astype(F32)
            for part in parts[h * half + 1 : (h + 1) * half]:
                total += part[at].astype(F32)
            out[h] = total.astype(BF)


def widen_kernel(id_ref, *refs):
    pieces, (gate_ref, up_ref, both) = refs[:-3], refs[-3:]
    hidden = both.shape[3]
    for k, piece in enumerate(pieces):
        both[jnp.bitwise_xor(id_ref[1], k)] = piece[...]
    for h, ref in enumerate((gate_ref, up_ref)):
        for at in range(len(pieces)):
            ref[:, at * hidden : (at + 1) * hidden] = both[at, h]


def qkv_kernel(share, sizes, id_ref, *refs):
    pieces = refs[:-6]
    q_ref, k_ref, v_ref, gain_ref, k_all, v_all = refs[-6:]
    count = k_all.shape[0]
    q_cols = q_ref.shape[1] // count
    gain_ref[...] = jnp.zeros_like(gain_ref)
    pieces = list(pieces)
    for k, size in enumerate(sizes):
        at = jnp.bitwise_xor(id_ref[0], k)
        row = 0
        for piece in pieces[:size]:
            value = piece[...].astype(F32)
            rows = slice(row, row + value.shape[0])
            q_ref[rows, pl.ds(pl.multiple_of(at * q_cols, LANES), q_cols)] = value[:, :q_cols]
            k_all[at, rows] = value[:, q_cols : q_cols + HD]
            v_all[at, rows] = value[:, q_cols + HD : q_cols + 2 * HD]
            gain_ref[rows] += value[:, q_cols + 2 * HD :]
            row = rows.stop
        pieces = pieces[size:]
    for ref, both in ((k_ref, k_all), (v_ref, v_all)):
        for head in range(count // share):
            total = both[head * share]
            for other in range(head * share + 1, (head + 1) * share):
                total += both[other]
            ref[:, head * HD : (head + 1) * HD] = total


def pair_grad_kernel(fine, id_ref, x_ref, grad_ref, *refs):
    outs, total_ref = refs[:-1], refs[-1]
    total_ref[...] = rows_rows(x_ref[...], grad_ref[...])
    own = fine * len(outs)
    for k, out in enumerate(outs):
        row = jnp.bitwise_xor(id_ref[0], k) * fine
        for block in range(out.shape[0]):
            at = pl.multiple_of(block * own + row, fine)
            out[block] = total_ref[pl.ds(at, fine)].astype(BF)


def pair_grad(ids, x, grad, fine, count, blocks):
    width, hidden = x.shape[1], grad.shape[1]
    tile = 2 * fine * count
    out = (2, fine, hidden)
    return pl.pallas_call(
        partial(pair_grad_kernel, fine),
        out_shape=(shape((blocks, fine, hidden), BF),) * count,
        grid_spec=pltpu.PrefetchScalarGridSpec(
            num_scalar_prefetch=1,
            grid=(width // tile,),
            in_specs=[
                pl.BlockSpec((x.shape[0], tile), lambda g, ids: (0, g)),
                pl.BlockSpec(grad.shape, lambda g, ids: (0, 0), pipeline_mode=pl.Buffered(1)),
            ],
            out_specs=(pl.BlockSpec(out, lambda g, ids: (g, 0, 0)),) * count,
            scratch_shapes=[pltpu.VMEM((tile, hidden), F32)],
        ),
        compiler_params=pltpu.CompilerParams(vmem_limit_bytes=56 * 1024 * 1024),
    )(ids, x, grad)


def stack_kernel(sizes, id_ref, *refs):
    parts, out_ref = list(refs[:-1]), refs[-1]
    for k, size in enumerate(sizes):
        at = jnp.bitwise_xor(id_ref[0], k)
        row = 0
        for part in parts[:size]:
            out_ref[at, row : row + part.shape[0]] = part[...]
            row += part.shape[0]
        parts = parts[size:]


def norm_scale(value):
    return lax.rsqrt(jnp.mean(value * value, axis=1, keepdims=True) + EPSILON)


def turn(tile, cosine, sine):
    lane = lax.broadcasted_iota(jnp.int32, tile.shape, 1)
    swapped = jnp.where(
        lane % HD < HD // 2,
        -pltpu.roll(tile, LANES - HD // 2, 1),
        pltpu.roll(tile, HD // 2, 1),
    )
    return tile * cosine + swapped * sine


def turn_first(tile, cosine, sine):
    lane = lax.broadcasted_iota(jnp.int32, tile.shape, 1)
    return jnp.where(lane < HD, turn(tile, cosine, sine), tile)


def in_kernel(x_ref, gain_ref, w_ref, cos_ref, sin_ref, normed_ref, q_ref, kv_ref):
    x = x_ref[0].astype(F32)
    normed = (x * norm_scale(x) * gain_ref[...]).astype(BF)
    normed_ref[0] = normed
    qkv = rows_cols(normed, w_ref[...])
    cosine, sine = cos_ref[0], sin_ref[0]
    q_cols = q_ref.shape[2]
    for at in range(0, q_cols, LANES):
        q_ref[0, :, at : at + LANES] = turn(qkv[:, at : at + LANES], cosine, sine).astype(BF)
    kv_ref[0] = turn_first(qkv[:, q_cols:], cosine, sine).astype(BF)


def stack_heads(value):
    return jnp.concatenate(
        [value[:, at : at + HD] for at in range(0, value.shape[1], HD)], axis=0
    )


def unstack_heads(value, rows):
    return jnp.concatenate(
        [value[at : at + rows] for at in range(0, value.shape[0], rows)], axis=1
    )


def attend_kernel(fine, q_ref, own_ref, halo_ref, pos_ref, probs_ref, out_ref):
    rows, q_cols = q_ref.shape[1:]
    heads = q_cols // HD
    count = out_ref.shape[0]
    kv = jnp.concatenate([halo_ref[0], own_ref[0]], axis=0)
    keys, values = kv[:, :HD], kv[:, HD:]
    span = kv.shape[0]
    scores = cols_cols(stack_heads(q_ref[0]), keys) * (HD**-0.5)
    query = lax.broadcasted_iota(jnp.int32, (rows, span), 0) + HALO
    key = lax.broadcasted_iota(jnp.int32, (rows, span), 1)
    first = query - pos_ref[0][:, :1].astype(jnp.int32)
    allowed = (key >= first) & (key <= query)
    scores = jnp.where(allowed[None], scores.reshape(heads, rows, span), NEG_FILL)
    grown = jnp.exp(scores - jnp.max(scores, axis=-1, keepdims=True))
    probs = grown / jnp.sum(grown, axis=-1, keepdims=True)
    probs_ref[0] = probs
    mixed = rows_cols(probs.reshape(heads * rows, span).astype(BF), values)
    mixed = unstack_heads(mixed, rows).astype(BF)
    for to in range(count):
        out_ref[to, 0] = jnp.concatenate(
            [
                mixed[:, at + to * fine : at + (to + 1) * fine]
                for at in range(0, q_cols, count * fine)
            ],
            axis=1,
        )


def attend_back_kernel(
    fine, grad_ref, probs_ref, q_ref, own_ref, halo_ref, cos_ref, sin_ref, q_out, kv_out
):
    rows, q_cols = q_ref.shape[1:]
    heads = q_cols // HD
    count = grad_ref.shape[0]
    kv = jnp.concatenate([halo_ref[0], own_ref[0]], axis=0)
    keys, values = kv[:, :HD], kv[:, HD:]
    span = kv.shape[0]
    grad = jnp.concatenate(
        [
            grad_ref[source, 0][:, at * fine : (at + 1) * fine]
            for at in range(q_cols // (count * fine))
            for source in range(count)
        ],
        axis=1,
    )
    grad = stack_heads(grad)
    probs = probs_ref[0].reshape(heads * rows, span)
    probs_grad = cols_cols(grad, values)
    inner = jnp.sum(probs * probs_grad, axis=-1, keepdims=True)
    score_grad = (probs * (probs_grad - inner)).astype(BF)
    scale = HD**-0.5
    key_grad = rows_rows(score_grad, stack_heads(q_ref[0])) * scale
    value_grad = rows_rows(probs.astype(BF), grad)
    kv_out[0] = jnp.concatenate([key_grad, value_grad], axis=1)
    query_grad = unstack_heads(rows_cols(score_grad, keys) * scale, rows)
    cosine, sine = cos_ref[0], -sin_ref[0]
    for at in range(0, q_cols, LANES):
        q_out[0, :, at : at + LANES] = turn(
            query_grad[:, at : at + LANES], cosine, sine
        ).astype(BF)


def in_back_kernel(
    id_ref, dq_ref, dkv_ref, back_ref, cos_ref, sin_ref, normed_ref, x_ref, two_ref, w_ref,
    part_ref, grad_ref, total_ref,
):
    at = pl.program_id(0)
    rows = dq_ref.shape[1]
    own = dkv_ref[0, HALO:]
    tail = own[rows - HALO :] + back_ref[0]
    own = jnp.concatenate([own[: rows - HALO], tail], axis=0)
    own = turn_first(own, cos_ref[0], -sin_ref[0]).astype(BF)
    qkv_grad = jnp.concatenate([dq_ref[0], own], axis=1)
    normed_grad = cols_cols(qkv_grad, w_ref[...])
    part_ref[0] = normed_grad.astype(BF)
    x = x_ref[0].astype(F32)
    one = (normed_grad * x * norm_scale(x)).astype(BF)
    cols = qkv_grad.shape[1]
    lane = lax.broadcasted_iota(jnp.int32, (rows, LANES), 1)

    @pl.when(at == 0)
    def _():
        total_ref[:, :cols] = rows_rows(normed_ref[0], qkv_grad)
        total_ref[:, cols:] = rows_rows(one, (lane < HD).astype(BF)) + rows_rows(
            two_ref[...], (lane >= HD).astype(BF)
        )

    @pl.when(at > 0)
    def _():
        total_ref[:, :cols] += rows_rows(normed_ref[0], qkv_grad)
        total_ref[:, cols:] += rows_rows(one, (lane < HD).astype(BF))

    @pl.when(at == pl.num_programs(0) - 1)
    def _():
        grad_ref[...] = total_ref[...].astype(BF)


def middle_kernel(part_ref, x_ref, gain_ref, mid_ref, normed_ref):
    mid = x_ref[...].astype(F32)
    for at in range(part_ref.shape[0]):
        mid += part_ref[at].astype(F32)
    mid_ref[...] = mid
    normed_ref[...] = (mid * norm_scale(mid) * gain_ref[...]).astype(BF)


def middle_back_kernel(grad_ref, mid_ref, gain_ref, cot_ref, out_ref, low_ref, gain_out_ref):
    mid = mid_ref[...]
    scale = norm_scale(mid)
    grad = grad_ref[...].astype(F32)
    gain_out_ref[...] = (grad * mid * scale).astype(BF)
    scaled = grad * gain_ref[...]
    out = (
        cot_ref[...].astype(F32)
        + scale * scaled
        - mid * scale**3 * jnp.mean(scaled * mid, axis=1, keepdims=True)
    )
    out_ref[...] = out
    low_ref[...] = out.astype(BF)


def last_kernel(id_ref, *refs):
    parts, (x_ref, gain_ref, mid_ref, out_ref) = refs[:-4], refs[-4:]
    x = x_ref[...].astype(F32)
    scale = norm_scale(x)
    half = len(parts) // 2
    halves = []
    for h in range(2):
        total = parts[h * half][...].astype(F32)
        for part in parts[h * half + 1 : (h + 1) * half]:
            total += part[...].astype(F32)
        halves.append(total)
    grad = jnp.concatenate(halves, axis=0)
    scaled = grad * gain_ref[...]
    out = (
        mid_ref[...]
        + scale * scaled
        - x * scale**3 * jnp.mean(scaled * x, axis=1, keepdims=True)
    )
    out_ref[...] = out.astype(BF)


def forward_kernel(x_ref, back_ref, pair_ref, mixed_ref, gate_out, up_out):
    x = x_ref[...]
    gate = rows_cols(x, pair_ref[0])
    up = rows_cols(x, pair_ref[1])
    mixed_grad = back_ref[...]
    sigma = jax.nn.sigmoid(gate)
    silu = gate * sigma
    mixed_ref[...] = (silu * up).astype(BF)
    gate_out[...] = (mixed_grad * up * sigma * (1.0 + gate * (1.0 - sigma))).astype(BF)
    up_out[...] = (mixed_grad * silu).astype(BF)


def back_kernel(gate_ref, up_ref, pair_ref, part_ref):
    part_ref[...] = (
        cols_cols(gate_ref[...], pair_ref[0]) + cols_cols(up_ref[...], pair_ref[1])
    ).astype(BF)


def shape(dims, kind):
    return jax.ShapeDtypeStruct(dims, kind)


def call(kernel, out_shape, grid=None, in_specs=None, out_specs=None, scratch=()):
    options = {}
    if grid is not None:
        options = {"grid": grid, "in_specs": in_specs, "out_specs": out_specs}
    return pl.pallas_call(
        kernel,
        out_shape=out_shape,
        scratch_shapes=list(scratch),
        compiler_params=pltpu.CompilerParams(vmem_limit_bytes=56 * 1024 * 1024),
        **options,
    )


def by_block(dims):
    return pl.BlockSpec((1,) + dims, lambda g: (g,) + (0,) * len(dims))


def whole(dims):
    return pl.BlockSpec(dims, lambda g: (0,) * len(dims), pipeline_mode=pl.Buffered(1))


def body(
    n_rep,
    n_shard,
    tokens,
    seq_lengths,
    deal_order,
    attn_gain,
    mlp_gain,
    q_weight,
    k_weight,
    v_weight,
    o_weight,
    gate_weight,
    up_weight,
    down_weight,
    cotangent,
):
    rows, width = tokens.shape
    r = lax.axis_index("rep")
    s = lax.axis_index("shard")
    own = width // n_shard
    fine = own // n_rep
    hidden = down_weight.shape[0]
    q_cols = width // n_rep
    heads = H // n_rep
    pair = n_shard // n_rep
    share = max(n_rep // KVH, 1)
    kv_at = (r * KVH) // n_rep
    all_rows = n_rep * rows
    span = HALO + rows
    qkv_cols = q_cols + 2 * HD

    starts = jnp.cumsum(seq_lengths[0]) - seq_lengths[0]
    places = s * rows + jnp.arange(rows, dtype=jnp.int32)
    first = jnp.max(
        jnp.where(starts[None, :] <= places[:, None], starts[None, :], 0), axis=1, keepdims=True
    )
    offset = jnp.broadcast_to((places[:, None] - first).astype(BF), (rows, LANES))

    w_qkv_own = jnp.concatenate(
        [
            lax.dynamic_slice_in_dim(q_weight, r * q_cols, q_cols, 1),
            lax.dynamic_slice_in_dim(k_weight, kv_at * HD, HD, 1),
            lax.dynamic_slice_in_dim(v_weight, kv_at * HD, HD, 1),
        ],
        axis=1,
    )
    w_qkv = lax.all_gather(w_qkv_own, "shard", axis=0, tiled=True)
    w_o = lax.all_gather(
        lax.dynamic_slice_in_dim(o_weight, r * fine, fine, 0), "shard", axis=0, tiled=True
    )
    x_all = spread(jnp.concatenate([tokens, offset], axis=1), "rep", n_rep)
    gains = lax.all_gather(jnp.stack([attn_gain, mlp_gain]), "shard", axis=1, tiled=True)
    gain_one = gains[0:1].astype(F32)
    gain_two = gains[1:2].astype(F32)

    def exchange_shard(pieces):
        rest = [send(pieces[k], "shard", n_shard, k) for k in range(1, n_shard)]
        return [pieces[0]] + rest

    block = (n_shard, fine, hidden)
    ids = jnp.stack([r, s]).astype(jnp.int32)
    gate_tied, up_tied, _ = lax.optimization_barrier((gate_weight, up_weight, gains))
    w_pair = split_pair(ids, gate_tied, up_tied, fine, n_shard)
    w_pair = exchange_shard(w_pair)
    w_pair = flat_call(order_kernel, ids, (shape(block, BF),) * 2, w_pair)
    w_pair = gather_rep(w_pair, n_rep)
    w_pair = flat_call(
        join_kernel,
        ids,
        shape((2, n_shard, n_rep, fine, hidden), BF),
        [half for piece in w_pair for half in piece],
    ).reshape(2, width, hidden)
    cot_all = lax.all_gather(cotangent, "shard", axis=0, tiled=True)

    half = HD // 2
    inverse = ROPE_BASE ** (-2.0 * (jnp.arange(LANES) % half).astype(F32) / HD)
    angles = x_all[:, :, width:].astype(F32) * inverse[None, None, :]
    cosine, sine = jnp.cos(angles), jnp.sin(angles)
    x_block = by_block((rows, width))
    table = by_block((rows, LANES))
    normed_one, queries, kv_own = call(
        in_kernel,
        (
            shape((n_rep, rows, width), BF),
            shape((n_rep, rows, q_cols), BF),
            shape((n_rep, rows, LANES), BF),
        ),
        (n_rep,),
        [x_block, whole((1, width)), whole((width, qkv_cols)), table, table],
        (x_block, by_block((rows, q_cols)), table),
    )(x_all, gain_one, w_qkv, cosine, sine)
    kv_halo = lax.ppermute(
        kv_own[:, rows - HALO :], "shard", [(i, i + 1) for i in range(n_shard - 1)]
    )
    head_block = pl.BlockSpec((n_rep, 1, rows, pair * fine), lambda g: (0, g, 0, 0))
    probs_block = by_block((heads, rows, span))
    probs, out_in = call(
        partial(attend_kernel, fine),
        (
            shape((n_rep, heads, rows, span), F32),
            shape((n_rep, n_rep, rows, pair * fine), BF),
        ),
        (n_rep,),
        [
            by_block((rows, q_cols)),
            table,
            by_block((HALO, LANES)),
            pl.BlockSpec((1, rows, LANES), lambda g: (g, 0, width // LANES)),
        ],
        (probs_block, head_block),
    )(queries, kv_own, kv_halo, x_all)
    out_in = swap(out_in, "rep").reshape(n_rep, all_rows, pair * fine)
    out_in = out_in.transpose(1, 0, 2).reshape(all_rows, q_cols)
    mid_part = rows_cols(out_in, w_o).astype(BF).reshape(n_rep, rows, width)
    x_mid, normed_two = call(
        middle_kernel, (shape((rows, width), F32), shape((rows, width), BF))
    )(swap(mid_part, "rep"), tokens, gain_two)

    two_all = lax.all_gather(normed_two, "shard", axis=0, tiled=True)
    mixed_grad = cols_cols(cot_all, down_weight)
    step = 256
    group = two_all.shape[0]
    token_block = pl.BlockSpec((step, width), lambda g: (g, 0))
    hidden_block = pl.BlockSpec((step, hidden), lambda g: (g, 0))
    mixed, gate_grad, up_grad = call(
        forward_kernel,
        (shape((group, hidden), BF),) * 3,
        (group // step,),
        [token_block, hidden_block, whole((2, width, hidden))],
        (hidden_block,) * 3,
    )(two_all, mixed_grad, w_pair)
    gate_chunks = pair_grad(ids, two_all, gate_grad, fine, n_rep, n_shard)
    gate_tied, _ = lax.optimization_barrier((gate_grad, gate_chunks[0]))
    two_grad_part = call(
        back_kernel,
        shape((group, width), BF),
        (group // step,),
        [hidden_block, hidden_block, whole((2, width, hidden))],
        token_block,
    )(gate_tied, up_grad, w_pair)
    up_grad, _ = lax.optimization_barrier((up_grad, two_grad_part))
    two_grad = lax.psum_scatter(two_grad_part, "shard", scatter_dimension=0, tiled=True)
    mid_grad, branch, gain_two_rows = call(
        middle_back_kernel,
        (shape((rows, width), F32), shape((rows, width), BF), shape((rows, width), BF)),
    )(two_grad, x_mid, gain_two, cotangent)

    up_chunks = pair_grad(ids, two_all, up_grad, fine, n_rep, n_shard)
    pair_chunks = list(zip(gate_chunks, up_chunks))
    mixed, _ = lax.optimization_barrier((mixed, up_chunks[0]))
    part_rows = hidden // n_rep
    cut = (part_rows // 2 + 15) // 16 * 16
    down_grad = rows_rows(mixed, cot_all).astype(BF)
    down_chunks = []
    for k in range(n_rep):
        at = (r ^ k) * part_rows
        down_chunks.append(
            (
                lax.dynamic_slice_in_dim(down_grad, at, cut, 0),
                lax.dynamic_slice_in_dim(down_grad, at + cut, part_rows - cut, 0),
            )
        )
    down_part = rows_cols(mixed, down_weight).astype(BF)
    down_rows = lax.psum_scatter(down_part, "shard", scatter_dimension=0, tiled=True)
    layer_out = (x_mid + down_rows.astype(F32)).astype(BF)
    w_down_grad = parts_rep(down_chunks, n_rep)
    w_down_grad = tuple(
        sum(part.astype(F32) for part in parts).astype(BF) for parts in w_down_grad
    )
    down_out = place(gather_rep(w_down_grad, n_rep), r)
    w_pair_grad = parts_rep(pair_chunks, n_rep)
    w_pair_grad = flat_call(
        sum_kernel,
        ids,
        (shape((2, fine, hidden), BF),) * n_shard,
        w_pair_grad[0] + w_pair_grad[1],
    )
    w_pair_grad = exchange_shard(w_pair_grad)
    w_pair_grad = flat_call(
        widen_kernel,
        ids,
        (shape((fine, n_shard * hidden), BF),) * 2,
        w_pair_grad,
        [pltpu.VMEM((n_shard, 2, fine, hidden), BF)],
    )
    w_pair_grad = gather_rep(w_pair_grad, n_rep)
    gate_out = place([piece[:1] for piece in w_pair_grad], r)
    up_out = place([piece[1:] for piece in w_pair_grad], r)

    branch = gather_two(branch, n_rep)
    branch_all = flat_call(
        partial(stack_kernel, [len(piece) for piece in branch]),
        ids,
        shape((n_rep, rows, width), BF),
        [part for piece in branch for part in piece],
    ).reshape(all_rows, width)
    in_grad = cols_cols(branch_all, w_o).astype(BF)
    branch_all, in_grad = lax.optimization_barrier((branch_all, in_grad))
    in_grad = in_grad.reshape(all_rows, n_rep, pair * fine).transpose(1, 0, 2)
    in_grad = swap(in_grad, "rep").reshape(n_rep, n_rep, rows, pair * fine)
    w_o_grad = rows_rows(out_in, branch_all).astype(BF)
    w_o_grad = lax.psum_scatter(w_o_grad, "shard", scatter_dimension=0, tiled=True)
    o_out = place(gather_two(w_o_grad, n_rep), r)
    query_grad, kv_grad = call(
        partial(attend_back_kernel, fine),
        (shape((n_rep, rows, q_cols), BF), shape((n_rep, span, LANES), F32)),
        (n_rep,),
        [
            head_block,
            probs_block,
            by_block((rows, q_cols)),
            table,
            by_block((HALO, LANES)),
            table,
            table,
        ],
        (by_block((rows, q_cols)), by_block((span, LANES))),
    )(in_grad, probs, queries, kv_own, kv_halo, cosine, sine)
    kv_back = lax.ppermute(
        kv_grad[:, :HALO], "shard", [(i + 1, i) for i in range(n_shard - 1)]
    )
    grad_cols = qkv_cols + LANES
    steady = lambda *dims: pl.BlockSpec(
        dims, lambda g, ids: (0,) * len(dims), pipeline_mode=pl.Buffered(1)
    )
    block_of = lambda *dims: pl.BlockSpec(
        (1,) + dims, lambda g, ids: (g,) + (0,) * len(dims)
    )
    one_grad_part, w_qkv_grad = pl.pallas_call(
        in_back_kernel,
        out_shape=(shape((n_rep, rows, width), BF), shape((width, grad_cols), BF)),
        grid_spec=pltpu.PrefetchScalarGridSpec(
            num_scalar_prefetch=1,
            grid=(n_rep,),
            in_specs=[
                block_of(rows, q_cols),
                block_of(span, LANES),
                block_of(HALO, LANES),
                block_of(rows, LANES),
                block_of(rows, LANES),
                block_of(rows, width),
                block_of(rows, width),
                steady(rows, width),
                steady(width, qkv_cols),
            ],
            out_specs=(
                pl.BlockSpec(
                    (1, rows, width), lambda g, ids: (jnp.bitwise_xor(g, ids[0]), 0, 0)
                ),
                pl.BlockSpec((width, grad_cols), lambda g, ids: (0, 0)),
            ),
            scratch_shapes=[pltpu.VMEM((width, grad_cols), F32)],
        ),
        name="attn_in_back",
        compiler_params=pltpu.CompilerParams(vmem_limit_bytes=56 * 1024 * 1024),
    )(
        ids, query_grad, kv_grad, kv_back, cosine, sine, normed_one, x_all, gain_two_rows,
        w_qkv,
    )
    w_qkv_grad = lax.psum_scatter(w_qkv_grad, "shard", scatter_dimension=0, tiled=True)
    one_grad = [one_grad_part[k] for k in range(n_rep)]
    one_grad = [(part[: rows // 2], part[rows // 2 :]) for part in one_grad]
    one_grad = parts_rep(one_grad, n_rep)
    input_grad = flat_call(
        last_kernel,
        ids,
        shape((rows, width), BF),
        one_grad[0] + one_grad[1] + [tokens, gain_one, mid_grad],
    )
    w_qkv_grad = [(w_qkv_grad,)] + [
        (send(w_qkv_grad, "rep", n_rep, k),) for k in range(1, n_rep)
    ]
    q_out, k_out, v_out, gain_sums = flat_call(
        partial(qkv_kernel, share, [len(piece) for piece in w_qkv_grad]),
        ids,
        (
            shape((own, width), F32),
            shape((own, KVH * HD), F32),
            shape((own, KVH * HD), F32),
            shape((own, LANES), F32),
        ),
        [part for piece in w_qkv_grad for part in piece],
        [pltpu.VMEM((n_rep, own, HD), F32)] * 2,
    )
    return (
        layer_out,
        input_grad,
        gain_sums[:, 0],
        gain_sums[:, HD],
        q_out,
        k_out,
        v_out,
        o_out,
        gate_out,
        up_out,
        down_out,
    )


def solution(mesh):
    split = P("shard", None)
    by_token = P(("rep", "shard"), None)
    return jax.shard_map(
        partial(body, mesh.shape["rep"], mesh.shape["shard"]),
        mesh=mesh,
        in_specs=(by_token, P("rep", None), P("rep", None), P("shard"), P("shard"))
        + (split,) * 7
        + (by_token,),
        out_specs=(by_token, by_token, P("shard"), P("shard")) + (split,) * 7,
        check_vma=False,
    )
```

```python
from functools import partial

import jax
import jax.numpy as jnp
from jax import lax
from jax.experimental import pallas as pl
from jax.experimental.pallas import tpu as pltpu
from jax.sharding import PartitionSpec as P


H = 32
KVH = 4
HD = 64
HALO = 64
LANES = 128

EPSILON = 1e-05
ROPE_BASE = 10000.0
NEG_FILL = -1e30

BF = jnp.bfloat16
F32 = jnp.float32


def dot(left, right, contract):
    return lax.dot_general(left, right, (contract, ((), ())), preferred_element_type=F32)


def rows_cols(left, right):
    return dot(left, right, ((1,), (0,)))


def rows_rows(left, right):
    return dot(left, right, ((0,), (0,)))


def cols_cols(left, right):
    return dot(left, right, ((1,), (1,)))


def spread(value, axis, count):
    wide = jnp.broadcast_to(value[None], (count,) + value.shape)
    return lax.all_to_all(wide, axis, split_axis=0, concat_axis=0, tiled=True)


def swap(value, axis):
    return lax.all_to_all(value, axis, split_axis=0, concat_axis=0, tiled=True)


def pairs(count, step):
    return [(i, i ^ step) for i in range(count)]


def send(value, axis, count, step):
    return lax.ppermute(value, axis, pairs(count, step))


def parts_rep(chunks, count):
    go = lambda value, step: send(value, "rep", count, step)
    if count != 4:
        return [
            [chunks[0][h]] + [go(chunks[k][h], k) for k in range(1, count)]
            for h in range(2)
        ]
    add = lambda left, right: (left.astype(F32) + right.astype(F32)).astype(BF)
    first_one = go(chunks[1][0], 1)
    first_two = go(chunks[3][0], 1)
    second_one = go(chunks[2][1], 2)
    second_two = go(chunks[3][1], 2)
    last_one = go(add(chunks[2][0], first_two), 2)
    last_two = go(add(chunks[1][1], second_two), 1)
    return [[chunks[0][0], first_one, last_one], [chunks[0][1], second_one, last_two]]


def gather_two(value, count):
    go = lambda value, step: send(value, "rep", count, step)
    if count != 4:
        return [(value,)] + [(go(value, k),) for k in range(1, count)]
    half = value.shape[0] // 2
    one, two = go(value, 1), go(value, 2)
    return [(value,), (one,), (two,), (go(one[:half], 2), go(two[half:], 1))]


def gather_direct(value, count):
    return [(value,)] + [(send(value, "rep", count, k),) for k in range(1, count)]


def gather_rep(halves, count):
    go = lambda value, step: send(value, "rep", count, step)
    if count != 4:
        return [halves] + [tuple(go(v, k) for v in halves) for k in range(1, count)]
    one = tuple(go(v, 1) for v in halves)
    two = tuple(go(v, 2) for v in halves)
    return [halves, one, two, (go(one[0], 2), go(two[1], 1))]


def place_kernel(sizes, me_ref, *refs):
    parts, out_ref = list(refs[:-1]), refs[-1]
    at = pl.program_id(0)
    for k, size in enumerate(sizes):
        mine, parts = parts[:size], parts[size:]

        @pl.when(at == jnp.bitwise_xor(me_ref[0], k))
        def _(mine=mine):
            row = 0
            for part in mine:
                out_ref[0, row : row + part.shape[0]] = part[...].astype(F32)
                row += part.shape[0]


def place(pieces, me):
    count = len(pieces)
    flat = [part for piece in pieces for part in piece]
    rows = sum(part.shape[0] for part in pieces[0])
    width = flat[0].shape[1]
    grid = pltpu.PrefetchScalarGridSpec(
        num_scalar_prefetch=1,
        grid=(count,),
        in_specs=[
            pl.BlockSpec(part.shape, lambda g, me: (0, 0), pipeline_mode=pl.Buffered(1))
            for part in flat
        ],
        out_specs=pl.BlockSpec((1, rows, width), lambda g, me: (g, 0, 0)),
    )
    return pl.pallas_call(
        partial(place_kernel, [len(piece) for piece in pieces]),
        out_shape=shape((count, rows, width), F32),
        grid_spec=grid,
        compiler_params=pltpu.CompilerParams(vmem_limit_bytes=56 * 1024 * 1024),
    )(me.astype(jnp.int32).reshape(1), *flat).reshape(count * rows, width)


def split_kernel(id_ref, gate_ref, up_ref, *refs):
    outs, both = refs[:-1], refs[-1]
    hidden = both.shape[3]
    for h, ref in enumerate((gate_ref, up_ref)):
        value = ref[...]
        for at in range(len(outs)):
            both[at, h] = value[:, at * hidden : (at + 1) * hidden]
    for k, out in enumerate(outs):
        out[...] = both[jnp.bitwise_xor(id_ref[1], k)]


def split_pair(ids, gate, up, fine, count):
    hidden = gate.shape[1] // count
    rows = pl.BlockSpec((fine, gate.shape[1]), lambda g, ids: (ids[0], 0))
    piece = (2, fine, hidden)
    return pl.pallas_call(
        split_kernel,
        out_shape=(shape(piece, BF),) * count,
        grid_spec=pltpu.PrefetchScalarGridSpec(
            num_scalar_prefetch=1,
            grid=(1,),
            in_specs=[rows, rows],
            out_specs=(pl.BlockSpec(piece, lambda g, ids: (0, 0, 0)),) * count,
            scratch_shapes=[pltpu.VMEM((count,) + piece, BF)],
        ),
        name="split_pair",
    )(ids, gate, up)


def flat_call(kernel, ids, out_shape, values, scratch=()):
    specs = [pl.BlockSpec(memory_space=pltpu.SMEM)]
    specs += [pl.BlockSpec(memory_space=pltpu.VMEM)] * len(values)
    return pl.pallas_call(
        kernel,
        out_shape=out_shape,
        in_specs=specs,
        scratch_shapes=list(scratch),
        compiler_params=pltpu.CompilerParams(vmem_limit_bytes=56 * 1024 * 1024),
    )(ids, *values)


def order_kernel(id_ref, *refs):
    pieces, (gate_ref, up_ref) = refs[:-2], refs[-2:]
    for k, piece in enumerate(pieces):
        at = jnp.bitwise_xor(id_ref[1], k)
        gate_ref[at] = piece[0]
        up_ref[at] = piece[1]


def join_kernel(id_ref, *refs):
    out_ref = refs[-1]
    for k in range(len(refs) // 2):
        at = jnp.bitwise_xor(id_ref[0], k)
        for h in range(2):
            value = refs[2 * k + h]
            for row in range(value.shape[0]):
                out_ref[h, row, at] = value[row]


def sum_kernel(id_ref, *refs):
    count = refs[0].shape[0]
    outs = refs[len(refs) - count :]
    parts = refs[: len(refs) - count]
    half = len(parts) // 2
    for k, out in enumerate(outs):
        at = jnp.bitwise_xor(id_ref[1], k)
        for h in range(2):
            total = parts[h * half][at].astype(F32)
            for part in parts[h * half + 1 : (h + 1) * half]:
                total += part[at].astype(F32)
            out[h] = total.astype(BF)


def widen_kernel(id_ref, *refs):
    pieces, (gate_ref, up_ref, both) = refs[:-3], refs[-3:]
    hidden = both.shape[3]
    for k, piece in enumerate(pieces):
        both[jnp.bitwise_xor(id_ref[1], k)] = piece[...]
    for h, ref in enumerate((gate_ref, up_ref)):
        for at in range(len(pieces)):
            ref[:, at * hidden : (at + 1) * hidden] = both[at, h]


def qkv_kernel(share, sizes, id_ref, *refs):
    pieces = refs[:-6]
    q_ref, k_ref, v_ref, gain_ref, k_all, v_all = refs[-6:]
    count = k_all.shape[0]
    q_cols = q_ref.shape[1] // count
    gain_ref[...] = jnp.zeros_like(gain_ref)
    pieces = list(pieces)
    for k, size in enumerate(sizes):
        at = jnp.bitwise_xor(id_ref[0], k)
        row = 0
        for piece in pieces[:size]:
            value = piece[...].astype(F32)
            rows = slice(row, row + value.shape[0])
            q_ref[rows, pl.ds(pl.multiple_of(at * q_cols, LANES), q_cols)] = value[:, :q_cols]
            k_all[at, rows] = value[:, q_cols : q_cols + HD]
            v_all[at, rows] = value[:, q_cols + HD : q_cols + 2 * HD]
            gain_ref[rows] += value[:, q_cols + 2 * HD :]
            row = rows.stop
        pieces = pieces[size:]
    for ref, both in ((k_ref, k_all), (v_ref, v_all)):
        for head in range(count // share):
            total = both[head * share]
            for other in range(head * share + 1, (head + 1) * share):
                total += both[other]
            ref[:, head * HD : (head + 1) * HD] = total


def pair_grad_kernel(fine, id_ref, x_ref, grad_ref, *refs):
    outs, total_ref = refs[:-1], refs[-1]
    total_ref[...] = rows_rows(x_ref[...], grad_ref[...])
    own = fine * len(outs)
    for k, out in enumerate(outs):
        row = jnp.bitwise_xor(id_ref[0], k) * fine
        for block in range(out.shape[0]):
            at = pl.multiple_of(block * own + row, fine)
            out[block] = total_ref[pl.ds(at, fine)].astype(BF)


def pair_grad(ids, x, grad, fine, count, blocks):
    width, hidden = x.shape[1], grad.shape[1]
    tile = 2 * fine * count
    out = (2, fine, hidden)
    return pl.pallas_call(
        partial(pair_grad_kernel, fine),
        out_shape=(shape((blocks, fine, hidden), BF),) * count,
        grid_spec=pltpu.PrefetchScalarGridSpec(
            num_scalar_prefetch=1,
            grid=(width // tile,),
            in_specs=[
                pl.BlockSpec((x.shape[0], tile), lambda g, ids: (0, g)),
                pl.BlockSpec(grad.shape, lambda g, ids: (0, 0), pipeline_mode=pl.Buffered(1)),
            ],
            out_specs=(pl.BlockSpec(out, lambda g, ids: (g, 0, 0)),) * count,
            scratch_shapes=[pltpu.VMEM((tile, hidden), F32)],
        ),
        compiler_params=pltpu.CompilerParams(vmem_limit_bytes=56 * 1024 * 1024),
    )(ids, x, grad)


def stack_kernel(sizes, id_ref, *refs):
    parts, out_ref = list(refs[:-1]), refs[-1]
    for k, size in enumerate(sizes):
        at = jnp.bitwise_xor(id_ref[0], k)
        row = 0
        for part in parts[:size]:
            out_ref[at, row : row + part.shape[0]] = part[...]
            row += part.shape[0]
        parts = parts[size:]


def norm_scale(value):
    return lax.rsqrt(jnp.mean(value * value, axis=1, keepdims=True) + EPSILON)


def turn(tile, cosine, sine):
    lane = lax.broadcasted_iota(jnp.int32, tile.shape, 1)
    swapped = jnp.where(
        lane % HD < HD // 2,
        -pltpu.roll(tile, LANES - HD // 2, 1),
        pltpu.roll(tile, HD // 2, 1),
    )
    return tile * cosine + swapped * sine


def turn_first(tile, cosine, sine):
    lane = lax.broadcasted_iota(jnp.int32, tile.shape, 1)
    return jnp.where(lane < HD, turn(tile, cosine, sine), tile)


def in_kernel(x_ref, gain_ref, w_ref, cos_ref, sin_ref, normed_ref, q_ref, kv_ref):
    x = x_ref[0].astype(F32)
    normed = (x * norm_scale(x) * gain_ref[...]).astype(BF)
    normed_ref[0] = normed
    qkv = rows_cols(normed, w_ref[...])
    cosine, sine = cos_ref[0], sin_ref[0]
    q_cols = q_ref.shape[2]
    for at in range(0, q_cols, LANES):
        q_ref[0, :, at : at + LANES] = turn(qkv[:, at : at + LANES], cosine, sine).astype(BF)
    kv_ref[0] = turn_first(qkv[:, q_cols:], cosine, sine).astype(BF)


def stack_heads(value):
    return jnp.concatenate(
        [value[:, at : at + HD] for at in range(0, value.shape[1], HD)], axis=0
    )


def unstack_heads(value, rows):
    return jnp.concatenate(
        [value[at : at + rows] for at in range(0, value.shape[0], rows)], axis=1
    )


def attend_kernel(fine, q_ref, own_ref, halo_ref, pos_ref, probs_ref, out_ref):
    rows, q_cols = q_ref.shape[1:]
    heads = q_cols // HD
    count = out_ref.shape[0]
    kv = jnp.concatenate([halo_ref[0], own_ref[0]], axis=0)
    keys, values = kv[:, :HD], kv[:, HD:]
    span = kv.shape[0]
    scores = cols_cols(stack_heads(q_ref[0]), keys) * (HD**-0.5)
    query = lax.broadcasted_iota(jnp.int32, (rows, span), 0) + HALO
    key = lax.broadcasted_iota(jnp.int32, (rows, span), 1)
    first = query - pos_ref[0][:, :1].astype(jnp.int32)
    allowed = (key >= first) & (key <= query)
    scores = jnp.where(allowed[None], scores.reshape(heads, rows, span), NEG_FILL)
    grown = jnp.exp(scores - jnp.max(scores, axis=-1, keepdims=True))
    probs = grown / jnp.sum(grown, axis=-1, keepdims=True)
    probs_ref[0] = probs
    mixed = rows_cols(probs.reshape(heads * rows, span).astype(BF), values)
    mixed = unstack_heads(mixed, rows).astype(BF)
    for to in range(count):
        out_ref[to, 0] = jnp.concatenate(
            [
                mixed[:, at + to * fine : at + (to + 1) * fine]
                for at in range(0, q_cols, count * fine)
            ],
            axis=1,
        )


def attend_back_kernel(
    fine, grad_ref, probs_ref, q_ref, own_ref, halo_ref, cos_ref, sin_ref, q_out, kv_out
):
    rows, q_cols = q_ref.shape[1:]
    heads = q_cols // HD
    count = grad_ref.shape[0]
    kv = jnp.concatenate([halo_ref[0], own_ref[0]], axis=0)
    keys, values = kv[:, :HD], kv[:, HD:]
    span = kv.shape[0]
    grad = jnp.concatenate(
        [
            grad_ref[source, 0][:, at * fine : (at + 1) * fine]
            for at in range(q_cols // (count * fine))
            for source in range(count)
        ],
        axis=1,
    )
    grad = stack_heads(grad)
    probs = probs_ref[0].reshape(heads * rows, span)
    probs_grad = cols_cols(grad, values)
    inner = jnp.sum(probs * probs_grad, axis=-1, keepdims=True)
    score_grad = (probs * (probs_grad - inner)).astype(BF)
    scale = HD**-0.5
    key_grad = rows_rows(score_grad, stack_heads(q_ref[0])) * scale
    value_grad = rows_rows(probs.astype(BF), grad)
    kv_out[0] = jnp.concatenate([key_grad, value_grad], axis=1)
    query_grad = unstack_heads(rows_cols(score_grad, keys) * scale, rows)
    cosine, sine = cos_ref[0], -sin_ref[0]
    for at in range(0, q_cols, LANES):
        q_out[0, :, at : at + LANES] = turn(
            query_grad[:, at : at + LANES], cosine, sine
        ).astype(BF)


def in_back_kernel(
    id_ref, dq_ref, dkv_ref, back_ref, cos_ref, sin_ref, normed_ref, x_ref, two_ref, w_ref,
    part_ref, grad_ref, total_ref,
):
    at = pl.program_id(0)
    rows = dq_ref.shape[1]
    own = dkv_ref[0, HALO:]
    tail = own[rows - HALO :] + back_ref[0]
    own = jnp.concatenate([own[: rows - HALO], tail], axis=0)
    own = turn_first(own, cos_ref[0], -sin_ref[0]).astype(BF)
    qkv_grad = jnp.concatenate([dq_ref[0], own], axis=1)
    normed_grad = cols_cols(qkv_grad, w_ref[...])
    part_ref[0] = normed_grad.astype(BF)
    x = x_ref[0].astype(F32)
    one = (normed_grad * x * norm_scale(x)).astype(BF)
    cols = qkv_grad.shape[1]
    lane = lax.broadcasted_iota(jnp.int32, (rows, LANES), 1)

    @pl.when(at == 0)
    def _():
        total_ref[:, :cols] = rows_rows(normed_ref[0], qkv_grad)
        total_ref[:, cols:] = rows_rows(one, (lane < HD).astype(BF)) + rows_rows(
            two_ref[...], (lane >= HD).astype(BF)
        )

    @pl.when(at > 0)
    def _():
        total_ref[:, :cols] += rows_rows(normed_ref[0], qkv_grad)
        total_ref[:, cols:] += rows_rows(one, (lane < HD).astype(BF))

    @pl.when(at == pl.num_programs(0) - 1)
    def _():
        grad_ref[...] = total_ref[...].astype(BF)


def middle_kernel(part_ref, x_ref, gain_ref, mid_ref, normed_ref):
    mid = x_ref[...].astype(F32)
    for at in range(part_ref.shape[0]):
        mid += part_ref[at].astype(F32)
    mid_ref[...] = mid
    normed_ref[...] = (mid * norm_scale(mid) * gain_ref[...]).astype(BF)


def middle_back_kernel(grad_ref, mid_ref, gain_ref, cot_ref, out_ref, low_ref, gain_out_ref):
    mid = mid_ref[...]
    scale = norm_scale(mid)
    grad = grad_ref[...].astype(F32)
    gain_out_ref[...] = (grad * mid * scale).astype(BF)
    scaled = grad * gain_ref[...]
    out = (
        cot_ref[...].astype(F32)
        + scale * scaled
        - mid * scale**3 * jnp.mean(scaled * mid, axis=1, keepdims=True)
    )
    out_ref[...] = out
    low_ref[...] = out.astype(BF)


def last_kernel(id_ref, *refs):
    parts, (x_ref, gain_ref, mid_ref, out_ref) = refs[:-4], refs[-4:]
    x = x_ref[...].astype(F32)
    scale = norm_scale(x)
    half = len(parts) // 2
    halves = []
    for h in range(2):
        total = parts[h * half][...].astype(F32)
        for part in parts[h * half + 1 : (h + 1) * half]:
            total += part[...].astype(F32)
        halves.append(total)
    grad = jnp.concatenate(halves, axis=0)
    scaled = grad * gain_ref[...]
    out = (
        mid_ref[...]
        + scale * scaled
        - x * scale**3 * jnp.mean(scaled * x, axis=1, keepdims=True)
    )
    out_ref[...] = out.astype(BF)


def forward_kernel(x_ref, back_ref, pair_ref, mixed_ref, gate_out, up_out):
    x = x_ref[...]
    gate = rows_cols(x, pair_ref[0])
    up = rows_cols(x, pair_ref[1])
    mixed_grad = back_ref[...]
    sigma = jax.nn.sigmoid(gate)
    silu = gate * sigma
    mixed_ref[...] = (silu * up).astype(BF)
    gate_out[...] = (mixed_grad * up * sigma * (1.0 + gate * (1.0 - sigma))).astype(BF)
    up_out[...] = (mixed_grad * silu).astype(BF)


def back_kernel(gate_ref, up_ref, pair_ref, part_ref):
    part_ref[...] = (
        cols_cols(gate_ref[...], pair_ref[0]) + cols_cols(up_ref[...], pair_ref[1])
    ).astype(BF)


def shape(dims, kind):
    return jax.ShapeDtypeStruct(dims, kind)


def call(kernel, out_shape, grid=None, in_specs=None, out_specs=None, scratch=()):
    options = {}
    if grid is not None:
        options = {"grid": grid, "in_specs": in_specs, "out_specs": out_specs}
    return pl.pallas_call(
        kernel,
        out_shape=out_shape,
        scratch_shapes=list(scratch),
        compiler_params=pltpu.CompilerParams(vmem_limit_bytes=56 * 1024 * 1024),
        **options,
    )


def by_block(dims):
    return pl.BlockSpec((1,) + dims, lambda g: (g,) + (0,) * len(dims))


def whole(dims):
    return pl.BlockSpec(dims, lambda g: (0,) * len(dims), pipeline_mode=pl.Buffered(1))


def body(
    n_rep,
    n_shard,
    tokens,
    seq_lengths,
    deal_order,
    attn_gain,
    mlp_gain,
    q_weight,
    k_weight,
    v_weight,
    o_weight,
    gate_weight,
    up_weight,
    down_weight,
    cotangent,
):
    rows, width = tokens.shape
    r = lax.axis_index("rep")
    s = lax.axis_index("shard")
    own = width // n_shard
    fine = own // n_rep
    hidden = down_weight.shape[0]
    q_cols = width // n_rep
    heads = H // n_rep
    pair = n_shard // n_rep
    share = max(n_rep // KVH, 1)
    kv_at = (r * KVH) // n_rep
    all_rows = n_rep * rows
    span = HALO + rows
    qkv_cols = q_cols + 2 * HD

    starts = jnp.cumsum(seq_lengths[0]) - seq_lengths[0]
    places = s * rows + jnp.arange(rows, dtype=jnp.int32)
    first = jnp.max(
        jnp.where(starts[None, :] <= places[:, None], starts[None, :], 0), axis=1, keepdims=True
    )
    offset = jnp.broadcast_to((places[:, None] - first).astype(BF), (rows, LANES))

    w_qkv_own = jnp.concatenate(
        [
            lax.dynamic_slice_in_dim(q_weight, r * q_cols, q_cols, 1),
            lax.dynamic_slice_in_dim(k_weight, kv_at * HD, HD, 1),
            lax.dynamic_slice_in_dim(v_weight, kv_at * HD, HD, 1),
        ],
        axis=1,
    )
    w_qkv = lax.all_gather(w_qkv_own, "shard", axis=0, tiled=True)
    w_o = lax.all_gather(
        lax.dynamic_slice_in_dim(o_weight, r * fine, fine, 0), "shard", axis=0, tiled=True
    )
    x_all = spread(jnp.concatenate([tokens, offset], axis=1), "rep", n_rep)
    gains = lax.all_gather(jnp.stack([attn_gain, mlp_gain]), "shard", axis=1, tiled=True)
    gain_one = gains[0:1].astype(F32)
    gain_two = gains[1:2].astype(F32)

    def exchange_shard(pieces):
        rest = [send(pieces[k], "shard", n_shard, k) for k in range(1, n_shard)]
        return [pieces[0]] + rest

    block = (n_shard, fine, hidden)
    ids = jnp.stack([r, s]).astype(jnp.int32)
    gate_tied, up_tied, _ = lax.optimization_barrier((gate_weight, up_weight, gains))
    w_pair = split_pair(ids, gate_tied, up_tied, fine, n_shard)
    w_pair = exchange_shard(w_pair)
    w_pair = flat_call(order_kernel, ids, (shape(block, BF),) * 2, w_pair)
    w_pair = gather_rep(w_pair, n_rep)
    w_pair = flat_call(
        join_kernel,
        ids,
        shape((2, n_shard, n_rep, fine, hidden), BF),
        [half for piece in w_pair for half in piece],
    ).reshape(2, width, hidden)
    cot_all = lax.all_gather(cotangent, "shard", axis=0, tiled=True)

    half = HD // 2
    inverse = ROPE_BASE ** (-2.0 * (jnp.arange(LANES) % half).astype(F32) / HD)
    angles = x_all[:, :, width:].astype(F32) * inverse[None, None, :]
    cosine, sine = jnp.cos(angles), jnp.sin(angles)
    x_block = by_block((rows, width))
    table = by_block((rows, LANES))
    normed_one, queries, kv_own = call(
        in_kernel,
        (
            shape((n_rep, rows, width), BF),
            shape((n_rep, rows, q_cols), BF),
            shape((n_rep, rows, LANES), BF),
        ),
        (n_rep,),
        [x_block, whole((1, width)), whole((width, qkv_cols)), table, table],
        (x_block, by_block((rows, q_cols)), table),
    )(x_all, gain_one, w_qkv, cosine, sine)
    kv_halo = lax.ppermute(
        kv_own[:, rows - HALO :], "shard", [(i, i + 1) for i in range(n_shard - 1)]
    )
    head_block = pl.BlockSpec((n_rep, 1, rows, pair * fine), lambda g: (0, g, 0, 0))
    probs_block = by_block((heads, rows, span))
    probs, out_in = call(
        partial(attend_kernel, fine),
        (
            shape((n_rep, heads, rows, span), F32),
            shape((n_rep, n_rep, rows, pair * fine), BF),
        ),
        (n_rep,),
        [
            by_block((rows, q_cols)),
            table,
            by_block((HALO, LANES)),
            pl.BlockSpec((1, rows, LANES), lambda g: (g, 0, width // LANES)),
        ],
        (probs_block, head_block),
    )(queries, kv_own, kv_halo, x_all)
    out_in = swap(out_in, "rep").reshape(n_rep, all_rows, pair * fine)
    out_in = out_in.transpose(1, 0, 2).reshape(all_rows, q_cols)
    mid_part = rows_cols(out_in, w_o).astype(BF).reshape(n_rep, rows, width)
    x_mid, normed_two = call(
        middle_kernel, (shape((rows, width), F32), shape((rows, width), BF))
    )(swap(mid_part, "rep"), tokens, gain_two)

    two_all = lax.all_gather(normed_two, "shard", axis=0, tiled=True)
    mixed_grad = cols_cols(cot_all, down_weight)
    step = 256
    group = two_all.shape[0]
    token_block = pl.BlockSpec((step, width), lambda g: (g, 0))
    hidden_block = pl.BlockSpec((step, hidden), lambda g: (g, 0))
    mixed, gate_grad, up_grad = call(
        forward_kernel,
        (shape((group, hidden), BF),) * 3,
        (group // step,),
        [token_block, hidden_block, whole((2, width, hidden))],
        (hidden_block,) * 3,
    )(two_all, mixed_grad, w_pair)
    gate_chunks = pair_grad(ids, two_all, gate_grad, fine, n_rep, n_shard)
    gate_tied, _ = lax.optimization_barrier((gate_grad, gate_chunks[0]))
    two_grad_part = call(
        back_kernel,
        shape((group, width), BF),
        (group // step,),
        [hidden_block, hidden_block, whole((2, width, hidden))],
        token_block,
    )(gate_tied, up_grad, w_pair)
    up_grad, _ = lax.optimization_barrier((up_grad, two_grad_part))
    two_grad = lax.psum_scatter(two_grad_part, "shard", scatter_dimension=0, tiled=True)
    mid_grad, branch, gain_two_rows = call(
        middle_back_kernel,
        (shape((rows, width), F32), shape((rows, width), BF), shape((rows, width), BF)),
    )(two_grad, x_mid, gain_two, cotangent)

    up_chunks = pair_grad(ids, two_all, up_grad, fine, n_rep, n_shard)
    pair_chunks = list(zip(gate_chunks, up_chunks))
    mixed, _ = lax.optimization_barrier((mixed, up_chunks[0]))
    part_rows = hidden // n_rep
    cut = (part_rows // 2 + 15) // 16 * 16
    down_grad = rows_rows(mixed, cot_all).astype(BF)
    down_chunks = []
    for k in range(n_rep):
        at = (r ^ k) * part_rows
        down_chunks.append(
            (
                lax.dynamic_slice_in_dim(down_grad, at, cut, 0),
                lax.dynamic_slice_in_dim(down_grad, at + cut, part_rows - cut, 0),
            )
        )
    down_part = rows_cols(mixed, down_weight).astype(BF)
    down_rows = lax.psum_scatter(down_part, "shard", scatter_dimension=0, tiled=True)
    layer_out = (x_mid + down_rows.astype(F32)).astype(BF)
    w_down_grad = parts_rep(down_chunks, n_rep)
    w_down_grad = tuple(
        sum(part.astype(F32) for part in parts).astype(BF) for parts in w_down_grad
    )
    down_out = place(gather_rep(w_down_grad, n_rep), r)
    w_pair_grad = parts_rep(pair_chunks, n_rep)
    w_pair_grad = flat_call(
        sum_kernel,
        ids,
        (shape((2, fine, hidden), BF),) * n_shard,
        w_pair_grad[0] + w_pair_grad[1],
    )
    w_pair_grad = exchange_shard(w_pair_grad)
    w_pair_grad = flat_call(
        widen_kernel,
        ids,
        (shape((fine, n_shard * hidden), BF),) * 2,
        w_pair_grad,
        [pltpu.VMEM((n_shard, 2, fine, hidden), BF)],
    )
    w_pair_grad = gather_rep(w_pair_grad, n_rep)
    gate_out = place([piece[:1] for piece in w_pair_grad], r)
    up_out = place([piece[1:] for piece in w_pair_grad], r)

    branch = gather_two(branch, n_rep)
    branch_all = flat_call(
        partial(stack_kernel, [len(piece) for piece in branch]),
        ids,
        shape((n_rep, rows, width), BF),
        [part for piece in branch for part in piece],
    ).reshape(all_rows, width)
    in_grad = cols_cols(branch_all, w_o).astype(BF)
    in_grad = in_grad.reshape(all_rows, n_rep, pair * fine).transpose(1, 0, 2)
    in_grad = swap(in_grad, "rep").reshape(n_rep, n_rep, rows, pair * fine)
    query_grad, kv_grad = call(
        partial(attend_back_kernel, fine),
        (shape((n_rep, rows, q_cols), BF), shape((n_rep, span, LANES), F32)),
        (n_rep,),
        [
            head_block,
            probs_block,
            by_block((rows, q_cols)),
            table,
            by_block((HALO, LANES)),
            table,
            table,
        ],
        (by_block((rows, q_cols)), by_block((span, LANES))),
    )(in_grad, probs, queries, kv_own, kv_halo, cosine, sine)
    kv_back = lax.ppermute(
        kv_grad[:, :HALO], "shard", [(i + 1, i) for i in range(n_shard - 1)]
    )
    grad_cols = qkv_cols + LANES
    steady = lambda *dims: pl.BlockSpec(
        dims, lambda g, ids: (0,) * len(dims), pipeline_mode=pl.Buffered(1)
    )
    block_of = lambda *dims: pl.BlockSpec(
        (1,) + dims, lambda g, ids: (g,) + (0,) * len(dims)
    )
    one_grad_part, w_qkv_grad = pl.pallas_call(
        in_back_kernel,
        out_shape=(shape((n_rep, rows, width), BF), shape((width, grad_cols), BF)),
        grid_spec=pltpu.PrefetchScalarGridSpec(
            num_scalar_prefetch=1,
            grid=(n_rep,),
            in_specs=[
                block_of(rows, q_cols),
                block_of(span, LANES),
                block_of(HALO, LANES),
                block_of(rows, LANES),
                block_of(rows, LANES),
                block_of(rows, width),
                block_of(rows, width),
                steady(rows, width),
                steady(width, qkv_cols),
            ],
            out_specs=(
                pl.BlockSpec(
                    (1, rows, width), lambda g, ids: (jnp.bitwise_xor(g, ids[0]), 0, 0)
                ),
                pl.BlockSpec((width, grad_cols), lambda g, ids: (0, 0)),
            ),
            scratch_shapes=[pltpu.VMEM((width, grad_cols), F32)],
        ),
        name="attn_in_back",
        compiler_params=pltpu.CompilerParams(vmem_limit_bytes=56 * 1024 * 1024),
    )(
        ids, query_grad, kv_grad, kv_back, cosine, sine, normed_one, x_all, gain_two_rows,
        w_qkv,
    )
    branch_all, _ = lax.optimization_barrier((branch_all, w_qkv_grad))
    w_qkv_grad = lax.psum_scatter(w_qkv_grad, "shard", scatter_dimension=0, tiled=True)
    w_o_grad = rows_rows(out_in, branch_all).astype(BF)
    w_o_grad = lax.psum_scatter(w_o_grad, "shard", scatter_dimension=0, tiled=True)
    o_out = place(gather_direct(w_o_grad, n_rep), r)
    one_grad = [one_grad_part[k] for k in range(n_rep)]
    one_grad = [(part[: rows // 2], part[rows // 2 :]) for part in one_grad]
    one_grad = parts_rep(one_grad, n_rep)
    input_grad = flat_call(
        last_kernel,
        ids,
        shape((rows, width), BF),
        one_grad[0] + one_grad[1] + [tokens, gain_one, mid_grad],
    )
    w_qkv_grad = gather_direct(w_qkv_grad, n_rep)
    q_out, k_out, v_out, gain_sums = flat_call(
        partial(qkv_kernel, share, [len(piece) for piece in w_qkv_grad]),
        ids,
        (
            shape((own, width), F32),
            shape((own, KVH * HD), F32),
            shape((own, KVH * HD), F32),
            shape((own, LANES), F32),
        ),
        [part for piece in w_qkv_grad for part in piece],
        [pltpu.VMEM((n_rep, own, HD), F32)] * 2,
    )
    return (
        layer_out,
        input_grad,
        gain_sums[:, 0],
        gain_sums[:, HD],
        q_out,
        k_out,
        v_out,
        o_out,
        gate_out,
        up_out,
        down_out,
    )


def solution(mesh):
    split = P("shard", None)
    by_token = P(("rep", "shard"), None)
    return jax.shard_map(
        partial(body, mesh.shape["rep"], mesh.shape["shard"]),
        mesh=mesh,
        in_specs=(by_token, P("rep", None), P("rep", None), P("shard"), P("shard"))
        + (split,) * 7
        + (by_token,),
        out_specs=(by_token, by_token, P("shard"), P("shard")) + (split,) * 7,
        check_vma=False,
    )
```

```python
from functools import partial

import jax
import jax.numpy as jnp
from jax import lax
from jax.experimental import pallas as pl
from jax.experimental.pallas import tpu as pltpu
from jax.sharding import PartitionSpec as P


H = 32
KVH = 4
HD = 64
HALO = 64
LANES = 128

EPSILON = 1e-05
ROPE_BASE = 10000.0
NEG_FILL = -1e30

BF = jnp.bfloat16
F32 = jnp.float32


def dot(left, right, contract):
    return lax.dot_general(left, right, (contract, ((), ())), preferred_element_type=F32)


def rows_cols(left, right):
    return dot(left, right, ((1,), (0,)))


def rows_rows(left, right):
    return dot(left, right, ((0,), (0,)))


def cols_cols(left, right):
    return dot(left, right, ((1,), (1,)))


def spread(value, axis, count):
    wide = jnp.broadcast_to(value[None], (count,) + value.shape)
    return lax.all_to_all(wide, axis, split_axis=0, concat_axis=0, tiled=True)


def swap(value, axis):
    return lax.all_to_all(value, axis, split_axis=0, concat_axis=0, tiled=True)


def pairs(count, step):
    return [(i, i ^ step) for i in range(count)]


def send(value, axis, count, step):
    return lax.ppermute(value, axis, pairs(count, step))


def parts_rep(chunks, count):
    go = lambda value, step: send(value, "rep", count, step)
    if count != 4:
        return [
            [chunks[0][h]] + [go(chunks[k][h], k) for k in range(1, count)]
            for h in range(2)
        ]
    add = lambda left, right: (left.astype(F32) + right.astype(F32)).astype(BF)
    first_one = go(chunks[1][0], 1)
    first_two = go(chunks[3][0], 1)
    second_one = go(chunks[2][1], 2)
    second_two = go(chunks[3][1], 2)
    last_one = go(add(chunks[2][0], first_two), 2)
    last_two = go(add(chunks[1][1], second_two), 1)
    return [[chunks[0][0], first_one, last_one], [chunks[0][1], second_one, last_two]]


def gather_two(value, count, half=None):
    go = lambda value, step: send(value, "rep", count, step)
    if count != 4:
        return [(value,)] + [(go(value, k),) for k in range(1, count)]
    half = half or value.shape[0] // 2
    one, two = go(value, 1), go(value, 2)
    return [(value,), (one,), (two,), (go(one[:half], 2), go(two[half:], 1))]


def gather_direct(value, count):
    return [(value,)] + [(send(value, "rep", count, k),) for k in range(1, count)]


def gather_rep(halves, count):
    go = lambda value, step: send(value, "rep", count, step)
    if count != 4:
        return [halves] + [tuple(go(v, k) for v in halves) for k in range(1, count)]
    one = tuple(go(v, 1) for v in halves)
    two = tuple(go(v, 2) for v in halves)
    return [halves, one, two, (go(one[0], 2), go(two[1], 1))]


def place_kernel(sizes, me_ref, *refs):
    parts, out_ref = list(refs[:-1]), refs[-1]
    at = pl.program_id(0)
    for k, size in enumerate(sizes):
        mine, parts = parts[:size], parts[size:]

        @pl.when(at == jnp.bitwise_xor(me_ref[0], k))
        def _(mine=mine):
            row = 0
            for part in mine:
                out_ref[0, row : row + part.shape[0]] = part[...].astype(F32)
                row += part.shape[0]


def place(pieces, me):
    count = len(pieces)
    flat = [part for piece in pieces for part in piece]
    rows = sum(part.shape[0] for part in pieces[0])
    width = flat[0].shape[1]
    grid = pltpu.PrefetchScalarGridSpec(
        num_scalar_prefetch=1,
        grid=(count,),
        in_specs=[
            pl.BlockSpec(part.shape, lambda g, me: (0, 0), pipeline_mode=pl.Buffered(1))
            for part in flat
        ],
        out_specs=pl.BlockSpec((1, rows, width), lambda g, me: (g, 0, 0)),
    )
    return pl.pallas_call(
        partial(place_kernel, [len(piece) for piece in pieces]),
        out_shape=shape((count, rows, width), F32),
        grid_spec=grid,
        compiler_params=pltpu.CompilerParams(vmem_limit_bytes=56 * 1024 * 1024),
    )(me.astype(jnp.int32).reshape(1), *flat).reshape(count * rows, width)


def split_kernel(id_ref, gate_ref, up_ref, *refs):
    outs, both = refs[:-1], refs[-1]
    hidden = both.shape[3]
    for h, ref in enumerate((gate_ref, up_ref)):
        value = ref[...]
        for at in range(len(outs)):
            both[at, h] = value[:, at * hidden : (at + 1) * hidden]
    for k, out in enumerate(outs):
        out[...] = both[jnp.bitwise_xor(id_ref[1], k)]


def split_pair(ids, gate, up, fine, count):
    hidden = gate.shape[1] // count
    rows = pl.BlockSpec((fine, gate.shape[1]), lambda g, ids: (ids[0], 0))
    piece = (2, fine, hidden)
    return pl.pallas_call(
        split_kernel,
        out_shape=(shape(piece, BF),) * count,
        grid_spec=pltpu.PrefetchScalarGridSpec(
            num_scalar_prefetch=1,
            grid=(1,),
            in_specs=[rows, rows],
            out_specs=(pl.BlockSpec(piece, lambda g, ids: (0, 0, 0)),) * count,
            scratch_shapes=[pltpu.VMEM((count,) + piece, BF)],
        ),
        name="split_pair",
    )(ids, gate, up)


def flat_call(kernel, ids, out_shape, values, scratch=()):
    specs = [pl.BlockSpec(memory_space=pltpu.SMEM)]
    specs += [pl.BlockSpec(memory_space=pltpu.VMEM)] * len(values)
    return pl.pallas_call(
        kernel,
        out_shape=out_shape,
        in_specs=specs,
        scratch_shapes=list(scratch),
        compiler_params=pltpu.CompilerParams(vmem_limit_bytes=56 * 1024 * 1024),
    )(ids, *values)


def order_kernel(id_ref, *refs):
    pieces, (gate_ref, up_ref) = refs[:-2], refs[-2:]
    for k, piece in enumerate(pieces):
        at = jnp.bitwise_xor(id_ref[1], k)
        gate_ref[at] = piece[0]
        up_ref[at] = piece[1]


def join_kernel(id_ref, *refs):
    out_ref = refs[-1]
    for k in range(len(refs) // 2):
        at = jnp.bitwise_xor(id_ref[0], k)
        for h in range(2):
            value = refs[2 * k + h]
            for row in range(value.shape[0]):
                out_ref[h, row, at] = value[row]


def sum_kernel(id_ref, *refs):
    count = refs[0].shape[0]
    outs = refs[len(refs) - count :]
    parts = refs[: len(refs) - count]
    half = len(parts) // 2
    for k, out in enumerate(outs):
        at = jnp.bitwise_xor(id_ref[1], k)
        for h in range(2):
            total = parts[h * half][at].astype(F32)
            for part in parts[h * half + 1 : (h + 1) * half]:
                total += part[at].astype(F32)
            out[h] = total.astype(BF)


def widen_kernel(id_ref, *refs):
    pieces, (gate_ref, up_ref, both) = refs[:-3], refs[-3:]
    hidden = both.shape[3]
    for k, piece in enumerate(pieces):
        both[jnp.bitwise_xor(id_ref[1], k)] = piece[...]
    for h, ref in enumerate((gate_ref, up_ref)):
        for at in range(len(pieces)):
            ref[:, at * hidden : (at + 1) * hidden] = both[at, h]


def attn_kernel(share, fine, id_ref, *refs):
    pieces = refs[:-7]
    q_ref, k_ref, v_ref, o_ref, gain_ref, k_all, v_all = refs[-7:]
    count = k_all.shape[0]
    q_cols = q_ref.shape[1] // count
    o_at = q_cols + 2 * HD + LANES
    total = 0.0
    for k, piece in enumerate(pieces):
        at = jnp.bitwise_xor(id_ref[0], k)
        value = piece[...].astype(F32)
        q_ref[:, pl.ds(pl.multiple_of(at * q_cols, LANES), q_cols)] = value[:, :q_cols]
        k_all[at] = value[:, q_cols : q_cols + HD]
        v_all[at] = value[:, q_cols + HD : q_cols + 2 * HD]
        total += value[:, q_cols + 2 * HD : o_at]
        rows = pl.ds(pl.multiple_of(at * fine, fine), fine)
        for block in range(count):
            o_ref[rows, block * q_cols : (block + 1) * q_cols] = value[
                block * fine : (block + 1) * fine, o_at:
            ]
    gain_ref[...] = total
    for ref, both in ((k_ref, k_all), (v_ref, v_all)):
        for head in range(count // share):
            total = both[head * share]
            for other in range(head * share + 1, (head + 1) * share):
                total += both[other]
            ref[:, head * HD : (head + 1) * HD] = total


def pair_grad_kernel(fine, id_ref, x_ref, grad_ref, *refs):
    outs, total_ref = refs[:-1], refs[-1]
    total_ref[...] = rows_rows(x_ref[...], grad_ref[...])
    own = fine * len(outs)
    for k, out in enumerate(outs):
        row = jnp.bitwise_xor(id_ref[0], k) * fine
        for block in range(out.shape[0]):
            at = pl.multiple_of(block * own + row, fine)
            out[block] = total_ref[pl.ds(at, fine)].astype(BF)


def pair_grad(ids, x, grad, fine, count, blocks):
    width, hidden = x.shape[1], grad.shape[1]
    tile = 2 * fine * count
    out = (2, fine, hidden)
    return pl.pallas_call(
        partial(pair_grad_kernel, fine),
        out_shape=(shape((blocks, fine, hidden), BF),) * count,
        grid_spec=pltpu.PrefetchScalarGridSpec(
            num_scalar_prefetch=1,
            grid=(width // tile,),
            in_specs=[
                pl.BlockSpec((x.shape[0], tile), lambda g, ids: (0, g)),
                pl.BlockSpec(grad.shape, lambda g, ids: (0, 0), pipeline_mode=pl.Buffered(1)),
            ],
            out_specs=(pl.BlockSpec(out, lambda g, ids: (g, 0, 0)),) * count,
            scratch_shapes=[pltpu.VMEM((tile, hidden), F32)],
        ),
        compiler_params=pltpu.CompilerParams(vmem_limit_bytes=56 * 1024 * 1024),
    )(ids, x, grad)


def stack_kernel(sizes, id_ref, *refs):
    parts, out_ref = list(refs[:-1]), refs[-1]
    for k, size in enumerate(sizes):
        at = jnp.bitwise_xor(id_ref[0], k)
        row = 0
        for part in parts[:size]:
            out_ref[at, row : row + part.shape[0]] = part[...]
            row += part.shape[0]
        parts = parts[size:]


def norm_scale(value):
    return lax.rsqrt(jnp.mean(value * value, axis=1, keepdims=True) + EPSILON)


def turn(tile, cosine, sine):
    lane = lax.broadcasted_iota(jnp.int32, tile.shape, 1)
    swapped = jnp.where(
        lane % HD < HD // 2,
        -pltpu.roll(tile, LANES - HD // 2, 1),
        pltpu.roll(tile, HD // 2, 1),
    )
    return tile * cosine + swapped * sine


def turn_first(tile, cosine, sine):
    lane = lax.broadcasted_iota(jnp.int32, tile.shape, 1)
    return jnp.where(lane < HD, turn(tile, cosine, sine), tile)


def in_kernel(x_ref, gain_ref, w_ref, cos_ref, sin_ref, normed_ref, q_ref, kv_ref):
    x = x_ref[0].astype(F32)
    normed = (x * norm_scale(x) * gain_ref[...]).astype(BF)
    normed_ref[0] = normed
    qkv = rows_cols(normed, w_ref[...])
    cosine, sine = cos_ref[0], sin_ref[0]
    q_cols = q_ref.shape[2]
    for at in range(0, q_cols, LANES):
        q_ref[0, :, at : at + LANES] = turn(qkv[:, at : at + LANES], cosine, sine).astype(BF)
    kv_ref[0] = turn_first(qkv[:, q_cols:], cosine, sine).astype(BF)


def stack_heads(value):
    return jnp.concatenate(
        [value[:, at : at + HD] for at in range(0, value.shape[1], HD)], axis=0
    )


def unstack_heads(value, rows):
    return jnp.concatenate(
        [value[at : at + rows] for at in range(0, value.shape[0], rows)], axis=1
    )


def attend_kernel(fine, q_ref, own_ref, halo_ref, pos_ref, probs_ref, out_ref):
    rows, q_cols = q_ref.shape[1:]
    heads = q_cols // HD
    count = out_ref.shape[0]
    kv = jnp.concatenate([halo_ref[0], own_ref[0]], axis=0)
    keys, values = kv[:, :HD], kv[:, HD:]
    span = kv.shape[0]
    scores = cols_cols(stack_heads(q_ref[0]), keys) * (HD**-0.5)
    query = lax.broadcasted_iota(jnp.int32, (rows, span), 0) + HALO
    key = lax.broadcasted_iota(jnp.int32, (rows, span), 1)
    first = query - pos_ref[0][:, :1].astype(jnp.int32)
    allowed = (key >= first) & (key <= query)
    scores = jnp.where(allowed[None], scores.reshape(heads, rows, span), NEG_FILL)
    grown = jnp.exp(scores - jnp.max(scores, axis=-1, keepdims=True))
    probs = grown / jnp.sum(grown, axis=-1, keepdims=True)
    probs_ref[0] = probs
    mixed = rows_cols(probs.reshape(heads * rows, span).astype(BF), values)
    mixed = unstack_heads(mixed, rows).astype(BF)
    for to in range(count):
        out_ref[to, 0] = jnp.concatenate(
            [
                mixed[:, at + to * fine : at + (to + 1) * fine]
                for at in range(0, q_cols, count * fine)
            ],
            axis=1,
        )


def attend_back_kernel(
    fine, grad_ref, probs_ref, q_ref, own_ref, halo_ref, cos_ref, sin_ref, q_out, kv_out
):
    rows, q_cols = q_ref.shape[1:]
    heads = q_cols // HD
    count = grad_ref.shape[0]
    kv = jnp.concatenate([halo_ref[0], own_ref[0]], axis=0)
    keys, values = kv[:, :HD], kv[:, HD:]
    span = kv.shape[0]
    grad = jnp.concatenate(
        [
            grad_ref[source, 0][:, at * fine : (at + 1) * fine]
            for at in range(q_cols // (count * fine))
            for source in range(count)
        ],
        axis=1,
    )
    grad = stack_heads(grad)
    probs = probs_ref[0].reshape(heads * rows, span)
    probs_grad = cols_cols(grad, values)
    inner = jnp.sum(probs * probs_grad, axis=-1, keepdims=True)
    score_grad = (probs * (probs_grad - inner)).astype(BF)
    scale = HD**-0.5
    key_grad = rows_rows(score_grad, stack_heads(q_ref[0])) * scale
    value_grad = rows_rows(probs.astype(BF), grad)
    kv_out[0] = jnp.concatenate([key_grad, value_grad], axis=1)
    query_grad = unstack_heads(rows_cols(score_grad, keys) * scale, rows)
    cosine, sine = cos_ref[0], -sin_ref[0]
    for at in range(0, q_cols, LANES):
        q_out[0, :, at : at + LANES] = turn(
            query_grad[:, at : at + LANES], cosine, sine
        ).astype(BF)


def in_back_kernel(
    id_ref, dq_ref, dkv_ref, back_ref, cos_ref, sin_ref, normed_ref, x_ref, two_ref, o_ref,
    w_ref, part_ref, grad_ref, qkv_all, one_all,
):
    at = pl.program_id(0)
    rows = dq_ref.shape[1]
    own = dkv_ref[0, HALO:]
    tail = own[rows - HALO :] + back_ref[0]
    own = jnp.concatenate([own[: rows - HALO], tail], axis=0)
    own = turn_first(own, cos_ref[0], -sin_ref[0]).astype(BF)
    qkv_grad = jnp.concatenate([dq_ref[0], own], axis=1)
    normed_grad = cols_cols(qkv_grad, w_ref[...])
    part_ref[0] = normed_grad.astype(BF)
    x = x_ref[0].astype(F32)
    mine = pl.ds(pl.multiple_of(at * rows, rows), rows)
    qkv_all[mine] = qkv_grad
    one_all[mine] = (normed_grad * x * norm_scale(x)).astype(BF)

    @pl.when(at == pl.num_programs(0) - 1)
    def _():
        cols = qkv_all.shape[1]
        lane = lambda count: lax.broadcasted_iota(jnp.int32, (count, LANES), 1)
        gains = rows_rows(one_all[...], (lane(one_all.shape[0]) < HD).astype(BF))
        gains += rows_rows(two_ref[...], (lane(rows) >= HD).astype(BF))
        grad_ref[:, :cols] = rows_rows(normed_ref[...], qkv_all[...]).astype(BF)
        grad_ref[:, cols : cols + LANES] = gains.astype(BF)
        grad_ref[:, cols + LANES :] = o_ref[...]


def middle_kernel(part_ref, x_ref, gain_ref, mid_ref, normed_ref):
    mid = x_ref[...].astype(F32)
    for at in range(part_ref.shape[0]):
        mid += part_ref[at].astype(F32)
    mid_ref[...] = mid
    normed_ref[...] = (mid * norm_scale(mid) * gain_ref[...]).astype(BF)


def middle_back_kernel(grad_ref, mid_ref, gain_ref, cot_ref, out_ref, low_ref, gain_out_ref):
    mid = mid_ref[...]
    scale = norm_scale(mid)
    grad = grad_ref[...].astype(F32)
    gain_out_ref[...] = (grad * mid * scale).astype(BF)
    scaled = grad * gain_ref[...]
    out = (
        cot_ref[...].astype(F32)
        + scale * scaled
        - mid * scale**3 * jnp.mean(scaled * mid, axis=1, keepdims=True)
    )
    out_ref[...] = out
    low_ref[...] = out.astype(BF)


def last_kernel(id_ref, *refs):
    parts, (x_ref, gain_ref, mid_ref, out_ref) = refs[:-4], refs[-4:]
    x = x_ref[...].astype(F32)
    scale = norm_scale(x)
    half = len(parts) // 2
    halves = []
    for h in range(2):
        total = parts[h * half][...].astype(F32)
        for part in parts[h * half + 1 : (h + 1) * half]:
            total += part[...].astype(F32)
        halves.append(total)
    grad = jnp.concatenate(halves, axis=0)
    scaled = grad * gain_ref[...]
    out = (
        mid_ref[...]
        + scale * scaled
        - x * scale**3 * jnp.mean(scaled * x, axis=1, keepdims=True)
    )
    out_ref[...] = out.astype(BF)


def forward_kernel(x_ref, back_ref, pair_ref, mixed_ref, gate_out, up_out):
    x = x_ref[...]
    gate = rows_cols(x, pair_ref[0])
    up = rows_cols(x, pair_ref[1])
    mixed_grad = back_ref[...]
    sigma = jax.nn.sigmoid(gate)
    silu = gate * sigma
    mixed_ref[...] = (silu * up).astype(BF)
    gate_out[...] = (mixed_grad * up * sigma * (1.0 + gate * (1.0 - sigma))).astype(BF)
    up_out[...] = (mixed_grad * silu).astype(BF)


def back_kernel(gate_ref, up_ref, pair_ref, part_ref):
    part_ref[...] = (
        cols_cols(gate_ref[...], pair_ref[0]) + cols_cols(up_ref[...], pair_ref[1])
    ).astype(BF)


def shape(dims, kind):
    return jax.ShapeDtypeStruct(dims, kind)


def call(kernel, out_shape, grid=None, in_specs=None, out_specs=None, scratch=()):
    options = {}
    if grid is not None:
        options = {"grid": grid, "in_specs": in_specs, "out_specs": out_specs}
    return pl.pallas_call(
        kernel,
        out_shape=out_shape,
        scratch_shapes=list(scratch),
        compiler_params=pltpu.CompilerParams(vmem_limit_bytes=56 * 1024 * 1024),
        **options,
    )


def by_block(dims):
    return pl.BlockSpec((1,) + dims, lambda g: (g,) + (0,) * len(dims))


def whole(dims):
    return pl.BlockSpec(dims, lambda g: (0,) * len(dims), pipeline_mode=pl.Buffered(1))


def body(
    n_rep,
    n_shard,
    tokens,
    seq_lengths,
    deal_order,
    attn_gain,
    mlp_gain,
    q_weight,
    k_weight,
    v_weight,
    o_weight,
    gate_weight,
    up_weight,
    down_weight,
    cotangent,
):
    rows, width = tokens.shape
    r = lax.axis_index("rep")
    s = lax.axis_index("shard")
    own = width // n_shard
    fine = own // n_rep
    hidden = down_weight.shape[0]
    q_cols = width // n_rep
    heads = H // n_rep
    pair = n_shard // n_rep
    share = max(n_rep // KVH, 1)
    kv_at = (r * KVH) // n_rep
    all_rows = n_rep * rows
    span = HALO + rows
    qkv_cols = q_cols + 2 * HD

    starts = jnp.cumsum(seq_lengths[0]) - seq_lengths[0]
    places = s * rows + jnp.arange(rows, dtype=jnp.int32)
    first = jnp.max(
        jnp.where(starts[None, :] <= places[:, None], starts[None, :], 0), axis=1, keepdims=True
    )
    offset = jnp.broadcast_to((places[:, None] - first).astype(BF), (rows, LANES))

    w_qkv_own = jnp.concatenate(
        [
            lax.dynamic_slice_in_dim(q_weight, r * q_cols, q_cols, 1),
            lax.dynamic_slice_in_dim(k_weight, kv_at * HD, HD, 1),
            lax.dynamic_slice_in_dim(v_weight, kv_at * HD, HD, 1),
        ],
        axis=1,
    )
    w_qkv = lax.all_gather(w_qkv_own, "shard", axis=0, tiled=True)
    w_o = lax.all_gather(
        lax.dynamic_slice_in_dim(o_weight, r * fine, fine, 0), "shard", axis=0, tiled=True
    )
    x_all = spread(jnp.concatenate([tokens, offset], axis=1), "rep", n_rep)
    gains = lax.all_gather(jnp.stack([attn_gain, mlp_gain]), "shard", axis=1, tiled=True)
    gain_one = gains[0:1].astype(F32)
    gain_two = gains[1:2].astype(F32)

    def exchange_shard(pieces):
        rest = [send(pieces[k], "shard", n_shard, k) for k in range(1, n_shard)]
        return [pieces[0]] + rest

    block = (n_shard, fine, hidden)
    ids = jnp.stack([r, s]).astype(jnp.int32)
    gate_tied, up_tied, _ = lax.optimization_barrier((gate_weight, up_weight, gains))
    w_pair = split_pair(ids, gate_tied, up_tied, fine, n_shard)
    w_pair = exchange_shard(w_pair)
    w_pair = flat_call(order_kernel, ids, (shape(block, BF),) * 2, w_pair)
    w_pair = gather_rep(w_pair, n_rep)
    w_pair = flat_call(
        join_kernel,
        ids,
        shape((2, n_shard, n_rep, fine, hidden), BF),
        [half for piece in w_pair for half in piece],
    ).reshape(2, width, hidden)
    cot_all = lax.all_gather(cotangent, "shard", axis=0, tiled=True)

    half = HD // 2
    inverse = ROPE_BASE ** (-2.0 * (jnp.arange(LANES) % half).astype(F32) / HD)
    angles = x_all[:, :, width:].astype(F32) * inverse[None, None, :]
    cosine, sine = jnp.cos(angles), jnp.sin(angles)
    x_block = by_block((rows, width))
    table = by_block((rows, LANES))
    normed_one, queries, kv_own = call(
        in_kernel,
        (
            shape((n_rep, rows, width), BF),
            shape((n_rep, rows, q_cols), BF),
            shape((n_rep, rows, LANES), BF),
        ),
        (n_rep,),
        [x_block, whole((1, width)), whole((width, qkv_cols)), table, table],
        (x_block, by_block((rows, q_cols)), table),
    )(x_all, gain_one, w_qkv, cosine, sine)
    kv_halo = lax.ppermute(
        kv_own[:, rows - HALO :], "shard", [(i, i + 1) for i in range(n_shard - 1)]
    )
    head_block = pl.BlockSpec((n_rep, 1, rows, pair * fine), lambda g: (0, g, 0, 0))
    probs_block = by_block((heads, rows, span))
    probs, out_in = call(
        partial(attend_kernel, fine),
        (
            shape((n_rep, heads, rows, span), F32),
            shape((n_rep, n_rep, rows, pair * fine), BF),
        ),
        (n_rep,),
        [
            by_block((rows, q_cols)),
            table,
            by_block((HALO, LANES)),
            pl.BlockSpec((1, rows, LANES), lambda g: (g, 0, width // LANES)),
        ],
        (probs_block, head_block),
    )(queries, kv_own, kv_halo, x_all)
    out_in = swap(out_in, "rep").reshape(n_rep, all_rows, pair * fine)
    out_in = out_in.transpose(1, 0, 2).reshape(all_rows, q_cols)
    mid_part = rows_cols(out_in, w_o).astype(BF).reshape(n_rep, rows, width)
    x_mid, normed_two = call(
        middle_kernel, (shape((rows, width), F32), shape((rows, width), BF))
    )(swap(mid_part, "rep"), tokens, gain_two)

    two_all = lax.all_gather(normed_two, "shard", axis=0, tiled=True)
    mixed_grad = cols_cols(cot_all, down_weight)
    step = 256
    group = two_all.shape[0]
    token_block = pl.BlockSpec((step, width), lambda g: (g, 0))
    hidden_block = pl.BlockSpec((step, hidden), lambda g: (g, 0))
    mixed, gate_grad, up_grad = call(
        forward_kernel,
        (shape((group, hidden), BF),) * 3,
        (group // step,),
        [token_block, hidden_block, whole((2, width, hidden))],
        (hidden_block,) * 3,
    )(two_all, mixed_grad, w_pair)
    gate_chunks = pair_grad(ids, two_all, gate_grad, fine, n_rep, n_shard)
    gate_tied, _ = lax.optimization_barrier((gate_grad, gate_chunks[0]))
    two_grad_part = call(
        back_kernel,
        shape((group, width), BF),
        (group // step,),
        [hidden_block, hidden_block, whole((2, width, hidden))],
        token_block,
    )(gate_tied, up_grad, w_pair)
    up_grad, _ = lax.optimization_barrier((up_grad, two_grad_part))
    two_grad = lax.psum_scatter(two_grad_part, "shard", scatter_dimension=0, tiled=True)
    mid_grad, branch, gain_two_rows = call(
        middle_back_kernel,
        (shape((rows, width), F32), shape((rows, width), BF), shape((rows, width), BF)),
    )(two_grad, x_mid, gain_two, cotangent)

    up_chunks = pair_grad(ids, two_all, up_grad, fine, n_rep, n_shard)
    pair_chunks = list(zip(gate_chunks, up_chunks))
    mixed, _ = lax.optimization_barrier((mixed, up_chunks[0]))
    part_rows = hidden // n_rep
    cut = (part_rows // 2 + 15) // 16 * 16
    down_grad = rows_rows(mixed, cot_all).astype(BF)
    down_chunks = []
    for k in range(n_rep):
        at = (r ^ k) * part_rows
        down_chunks.append(
            (
                lax.dynamic_slice_in_dim(down_grad, at, cut, 0),
                lax.dynamic_slice_in_dim(down_grad, at + cut, part_rows - cut, 0),
            )
        )
    down_part = rows_cols(mixed, down_weight).astype(BF)
    down_rows = lax.psum_scatter(down_part, "shard", scatter_dimension=0, tiled=True)
    layer_out = (x_mid + down_rows.astype(F32)).astype(BF)
    w_down_grad = parts_rep(down_chunks, n_rep)
    w_down_grad = jnp.concatenate(
        [sum(part.astype(F32) for part in parts).astype(BF) for parts in w_down_grad], axis=0
    )
    down_out = place(gather_two(w_down_grad, n_rep, cut), r)
    w_pair_grad = parts_rep(pair_chunks, n_rep)
    w_pair_grad = flat_call(
        sum_kernel,
        ids,
        (shape((2, fine, hidden), BF),) * n_shard,
        w_pair_grad[0] + w_pair_grad[1],
    )
    w_pair_grad = exchange_shard(w_pair_grad)
    w_pair_grad = flat_call(
        widen_kernel,
        ids,
        (shape((fine, n_shard * hidden), BF),) * 2,
        w_pair_grad,
        [pltpu.VMEM((n_shard, 2, fine, hidden), BF)],
    )
    w_pair_grad = gather_rep(w_pair_grad, n_rep)
    gate_out = place([piece[:1] for piece in w_pair_grad], r)
    up_out = place([piece[1:] for piece in w_pair_grad], r)

    branch = gather_two(branch, n_rep)
    branch_all = flat_call(
        partial(stack_kernel, [len(piece) for piece in branch]),
        ids,
        shape((n_rep, rows, width), BF),
        [part for piece in branch for part in piece],
    ).reshape(all_rows, width)
    in_grad = cols_cols(branch_all, w_o).astype(BF)
    branch_all, in_grad = lax.optimization_barrier((branch_all, in_grad))
    w_o_grad = rows_rows(out_in, branch_all).astype(BF)
    w_o_grad = w_o_grad.reshape(n_shard, fine, n_rep, q_cols).transpose(0, 2, 1, 3)
    w_o_grad = w_o_grad.reshape(width, q_cols)
    in_grad = in_grad.reshape(all_rows, n_rep, pair * fine).transpose(1, 0, 2)
    in_grad = swap(in_grad, "rep").reshape(n_rep, n_rep, rows, pair * fine)
    query_grad, kv_grad = call(
        partial(attend_back_kernel, fine),
        (shape((n_rep, rows, q_cols), BF), shape((n_rep, span, LANES), F32)),
        (n_rep,),
        [
            head_block,
            probs_block,
            by_block((rows, q_cols)),
            table,
            by_block((HALO, LANES)),
            table,
            table,
        ],
        (by_block((rows, q_cols)), by_block((span, LANES))),
    )(in_grad, probs, queries, kv_own, kv_halo, cosine, sine)
    kv_back = lax.ppermute(
        kv_grad[:, :HALO], "shard", [(i + 1, i) for i in range(n_shard - 1)]
    )
    grad_cols = qkv_cols + LANES + q_cols
    steady = lambda *dims: pl.BlockSpec(
        dims, lambda g, ids: (0,) * len(dims), pipeline_mode=pl.Buffered(1)
    )
    block_of = lambda *dims: pl.BlockSpec(
        (1,) + dims, lambda g, ids: (g,) + (0,) * len(dims)
    )
    one_grad_part, w_qkv_grad = pl.pallas_call(
        in_back_kernel,
        out_shape=(shape((n_rep, rows, width), BF), shape((width, grad_cols), BF)),
        grid_spec=pltpu.PrefetchScalarGridSpec(
            num_scalar_prefetch=1,
            grid=(n_rep,),
            in_specs=[
                block_of(rows, q_cols),
                block_of(span, LANES),
                block_of(HALO, LANES),
                block_of(rows, LANES),
                block_of(rows, LANES),
                steady(all_rows, width),
                block_of(rows, width),
                steady(rows, width),
                steady(width, q_cols),
                steady(width, qkv_cols),
            ],
            out_specs=(
                pl.BlockSpec(
                    (1, rows, width), lambda g, ids: (jnp.bitwise_xor(g, ids[0]), 0, 0)
                ),
                pl.BlockSpec((width, grad_cols), lambda g, ids: (0, 0)),
            ),
            scratch_shapes=[
                pltpu.VMEM((all_rows, qkv_cols), BF),
                pltpu.VMEM((all_rows, width), BF),
            ],
        ),
        name="attn_in_back",
        compiler_params=pltpu.CompilerParams(vmem_limit_bytes=56 * 1024 * 1024),
    )(
        ids, query_grad, kv_grad, kv_back, cosine, sine,
        normed_one.reshape(all_rows, width), x_all, gain_two_rows, w_o_grad, w_qkv,
    )
    w_qkv_grad = lax.psum_scatter(w_qkv_grad, "shard", scatter_dimension=0, tiled=True)
    one_grad = [one_grad_part[k] for k in range(n_rep)]
    one_grad = [(part[: rows // 2], part[rows // 2 :]) for part in one_grad]
    one_grad = parts_rep(one_grad, n_rep)
    input_grad = flat_call(
        last_kernel,
        ids,
        shape((rows, width), BF),
        one_grad[0] + one_grad[1] + [tokens, gain_one, mid_grad],
    )
    q_out, k_out, v_out, o_out, gain_sums = flat_call(
        partial(attn_kernel, share, fine),
        ids,
        (
            shape((own, width), F32),
            shape((own, KVH * HD), F32),
            shape((own, KVH * HD), F32),
            shape((own, width), F32),
            shape((own, LANES), F32),
        ),
        [piece[0] for piece in gather_direct(w_qkv_grad, n_rep)],
        [pltpu.VMEM((n_rep, own, HD), F32)] * 2,
    )
    return (
        layer_out,
        input_grad,
        gain_sums[:, 0],
        gain_sums[:, HD],
        q_out,
        k_out,
        v_out,
        o_out,
        gate_out,
        up_out,
        down_out,
    )


def solution(mesh):
    split = P("shard", None)
    by_token = P(("rep", "shard"), None)
    return jax.shard_map(
        partial(body, mesh.shape["rep"], mesh.shape["shard"]),
        mesh=mesh,
        in_specs=(by_token, P("rep", None), P("rep", None), P("shard"), P("shard"))
        + (split,) * 7
        + (by_token,),
        out_specs=(by_token, by_token, P("shard"), P("shard")) + (split,) * 7,
        check_vma=False,
    )
```
